32 devices in a mesh: dp: 8 (over y, x, core), mp: 4 (over z).
Axes of the slice: x: 2, y: 2, z: 4, core: 2. Of those that a mesh axis runs over, the one named last changes fastest.
Arguments:
- tokens: bfloat16 [16, 1024, 768], P('dp'), may hold values from -6 to 6
- lengths: int32 [16], P('dp'), may hold values from 256 to 1024, as said below
- qkv_weight: bfloat16 [3, 768, 768], P(None, None, 'mp'), may hold values from -0.5 to 0.5
- out_weight: bfloat16 [768, 768], P('mp'), may hold values from -0.3125 to 0.3125
- conv_taps: float32 [12, 33], P('mp'), may hold values from -0.36 to 0.36
- norm1_gain: float32 [768], replicated, may hold values from 0.1 to 1.9
- norm1_bias: float32 [768], replicated, may hold values from -0.5 to 0.5
- norm2_gain: float32 [768], replicated, may hold values from 0.1 to 1.9
- norm2_bias: float32 [768], replicated, may hold values from -0.5 to 0.5
- up_weight: bfloat16 [768, 3072], P(None, 'mp'), may hold values from -0.21875 to 0.21875
- down_weight: bfloat16 [3072, 768], P('mp'), may hold values from -0.109375 to 0.109375
- cotangent: bfloat16 [16, 1024, 768], P('dp'), may hold values from -6 to 6
Outputs:
- output: bfloat16 [16, 1024, 768], P('dp')
- input_grad: bfloat16 [16, 1024, 768], P('dp')
- qkv_grad: float32 [3, 768, 768], P(None, None, 'mp')
- out_grad: float32 [768, 768], P('mp')
- taps_grad: float32 [12, 33], P('mp')
- norm1_gain_grad: float32 [768], replicated
- norm1_bias_grad: float32 [768], replicated
- norm2_gain_grad: float32 [768], replicated
- norm2_bias_grad: float32 [768], replicated
- up_grad: float32 [768, 3072], P(None, 'mp')
- down_grad: float32 [3072, 768], P('mp')
The draws below stay inside these ranges and needn't reach their ends.
Inputs may be any that keep to these rules, and one draw needn't show every extreme that they name: Each entry of lengths is the document's true length, and at least one document in every draw has length exactly 1024.
All inputs are finite; a program needn't handle non-finite values.
Results may differ from the reference program's by a relative error of at most 0.024.
The reference program's roundings to bfloat16 on the way count: a program that leaves them out, or rounds other values in their place, can miss the bound.
Values may be sent and summed in bfloat16 or wider, within the bound.
A program may use at most 256 MiB of HBM per device.

```python
import jax
import jax.numpy as jnp
from jax import lax

D = 768
HEADS = 12
HEAD_DIM = 64
FF = 3072
LANDMARKS = 64
KSIZE = 33
NS_ITERS = 6
SEQ = 1024
DOCS = 16
N_MP = 4


def draw_lengths(key, part):
    first_key, second_key = jax.random.split(jax.random.fold_in(key, 17))
    drawn = jax.random.randint(first_key, (DOCS,), SEQ // 4, SEQ + 1)
    longest = jax.random.randint(second_key, (), 0, DOCS)
    return jnp.where(jnp.arange(DOCS) == longest, SEQ, drawn).astype(jnp.int32)


def steps_of(own_key, extent, cuts, low, largest):
    factor_of = 1.0
    for dim, parts in cuts:
        heights = jax.random.uniform(jax.random.fold_in(jax.random.fold_in(own_key, 6), dim), (parts,), jnp.float32, low / len(cuts), largest / len(cuts))
        factor_of = factor_of * jnp.repeat(jnp.exp(heights), extent[dim] // parts).reshape((-1,) + (1,) * (len(extent) - 1 - dim))
    return factor_of


def scatter_about(own_key, dims, spread, bound, cuts=(), kind=jnp.bfloat16):
    array = spread * jax.random.normal(own_key, dims, jnp.float32)
    if cuts:
        array = array * steps_of(own_key, dims, cuts, -0.22, 0.18)
    return jnp.clip(array, -bound, bound).astype(kind)


def setup_inputs(seed: int = 0) -> dict:
    streams_of = jax.random.split(jax.random.key(seed), 13)
    return {
        "tokens": scatter_about(streams_of[0], (DOCS, SEQ, D), 1.0, 6.0, ((0, 8),)),
        "lengths": draw_lengths(jax.random.fold_in(streams_of[12], 71), 0),
        "qkv_weight": scatter_about(streams_of[2], (3, D, D), (D // 6) ** -0.5, 0.5, ((2, 4),)),
        "out_weight": scatter_about(streams_of[3], (D, D), (D // 2) ** -0.5, 0.3125, ((0, 4),)),
        "conv_taps": scatter_about(streams_of[4], (HEADS, KSIZE), 0.06, 0.36, ((0, 4),), jnp.float32),
        "norm1_gain": jnp.clip(1.0 + 0.18 * jax.random.normal(streams_of[5], (D,), jnp.float32), 0.1, 1.9),
        "norm1_bias": jnp.clip(jax.random.uniform(streams_of[6], (D,), jnp.float32, -0.5, 0.5), -0.5, 0.5),
        "norm2_gain": jnp.clip(1.0 + 0.18 * jax.random.normal(streams_of[7], (D,), jnp.float32), 0.1, 1.9),
        "norm2_bias": jnp.clip(jax.random.uniform(streams_of[8], (D,), jnp.float32, -0.5, 0.5), -0.5, 0.5),
        "up_weight": scatter_about(streams_of[9], (D, FF), D ** -0.5, 0.21875, ((1, 4),)),
        "down_weight": scatter_about(streams_of[10], (FF, D), FF ** -0.5, 0.109375, ((0, 4),)),
        "cotangent": scatter_about(streams_of[11], (DOCS, SEQ, D), 1.0, 6.0, ((0, 8),)),
    }


EPSILON = 1e-05
FULL_PRECISION = lax.Precision.HIGHEST

@jax.custom_vjp
def reduced_precision(v):
    return lax.optimization_barrier(v.astype(jnp.bfloat16)).astype(jnp.float32)

@jax.custom_vjp
def reduced_backward(v):
    return v

def low_keep(v):
    return (reduced_precision(v), None)

def low_pass(kept, grad):
    return (grad,)

def back_keep(v):
    return (v, None)

def back_low(kept, grad):
    return (reduced_precision(grad),)
reduced_precision.defvjp(low_keep, low_pass)
reduced_backward.defvjp(back_keep, back_low)

def rounded_both(values):
    return reduced_precision(reduced_backward(values))

def layer_norm(values, gain_vec, shift_vec):
    average = lax.optimization_barrier(jnp.mean(values, axis=-1, keepdims=True))
    centered = values - average
    variance = lax.optimization_barrier(jnp.mean(centered * centered, axis=-1, keepdims=True))
    return centered * lax.rsqrt(variance + EPSILON) * gain_vec + shift_vec

def newton_schulz(kernel):
    identity_m = jnp.eye(kernel.shape[-1], dtype=kernel.dtype)
    total_sq = lax.optimization_barrier(jnp.sum(kernel * kernel, axis=(1, 2), keepdims=True))
    kernel_inverse = jnp.swapaxes(kernel, 1, 2) / total_sq
    for sweep_no in range(NS_ITERS):
        product = jnp.einsum('hij,hjk->hik', kernel, kernel_inverse, precision=FULL_PRECISION)
        inner_term = 7.0 * identity_m - product
        inner_term = 15.0 * identity_m - jnp.einsum('hij,hjk->hik', product, inner_term, precision=FULL_PRECISION)
        inner_term = 13.0 * identity_m - jnp.einsum('hij,hjk->hik', product, inner_term, precision=FULL_PRECISION)
        kernel_inverse = 0.25 * jnp.einsum('hij,hjk->hik', kernel_inverse, inner_term, precision=FULL_PRECISION)
    return kernel_inverse

def pinv_from(landmark_queries, landmark_keys):
    scores_scale_factor = HEAD_DIM ** (-0.5)
    second_scores = jnp.einsum('ble,gle->lbg', landmark_queries, landmark_keys, precision=FULL_PRECISION) * scores_scale_factor
    return newton_schulz(jax.nn.softmax(second_scores, axis=-1))

def depthwise(values, tap_weights):
    half_span = (KSIZE - 1) // 2
    seq_len = values.shape[0]
    padded = jnp.pad(values, ((half_span, half_span), (0, 0), (0, 0)))
    running = jnp.zeros_like(values)
    for offset in range(KSIZE):
        running = running + padded[offset:offset + seq_len] * tap_weights[:, offset][None, :, None]
    return running

def one_document(tokens_f, length, weights):
    qkv_w, out_w, tap_weights, gain_one, bias_one, gain_two, bias_two, up_w, down_w = weights
    seq_len = tokens_f.shape[0]
    scores_scale_factor = HEAD_DIM ** (-0.5)
    places = jnp.arange(seq_len, dtype=jnp.int32)
    live_flag = places < length
    live_f = live_flag.astype(tokens_f.dtype)
    segment = places * LANDMARKS // length
    segment_membership = ((segment[None, :] == jnp.arange(LANDMARKS, dtype=jnp.int32)[:, None]) & live_flag[None, :]).astype(tokens_f.dtype)
    mean_operator = segment_membership / lax.optimization_barrier(jnp.sum(segment_membership, axis=1, keepdims=True))
    projected = rounded_both(jnp.einsum('sd,tdc->tsc', tokens_f, qkv_w, precision=FULL_PRECISION))
    query_matrix = projected[0].reshape(seq_len, HEADS, HEAD_DIM)
    key_matrix = projected[1].reshape(seq_len, HEADS, HEAD_DIM)
    value_matrix = projected[2].reshape(seq_len, HEADS, HEAD_DIM)
    landmark_queries = reduced_precision(jnp.einsum('ov,vaf->oaf', mean_operator, query_matrix, precision=FULL_PRECISION))
    landmark_keys = reduced_precision(jnp.einsum('ov,vaf->oaf', mean_operator, key_matrix, precision=FULL_PRECISION))
    first_scores = reduced_backward(jnp.einsum('wxe,pxe->xwp', query_matrix, landmark_keys, precision=FULL_PRECISION) * scores_scale_factor)
    first_kernel = reduced_precision(jax.nn.softmax(first_scores, axis=-1))
    kernel_inverse = pinv_from(landmark_queries, landmark_keys)
    third_scores = reduced_backward(jnp.einsum('xyk,pyk->yxp', landmark_queries, key_matrix, precision=FULL_PRECISION) * scores_scale_factor)
    third_scores = jnp.where(live_flag[None, None, :], third_scores, -1e+30)
    third_kernel = reduced_precision(jax.nn.softmax(third_scores, axis=-1))
    landmark_summary = reduced_backward(jnp.einsum('olp,pon->oln', third_kernel, value_matrix, precision=FULL_PRECISION))
    mixing_matrix = reduced_precision(jnp.einsum('lcb,lbf->lcf', kernel_inverse, landmark_summary, precision=FULL_PRECISION))
    landmark_approximation = jnp.einsum('wpb,wbi->pwi', first_kernel, mixing_matrix, precision=FULL_PRECISION)
    local_term = depthwise(value_matrix * live_f[:, None, None], tap_weights)
    context = rounded_both((landmark_approximation + local_term) * live_f[:, None, None]).reshape(seq_len, D)
    context_groups = context.reshape(seq_len, N_MP, D // N_MP)
    out_groups = out_w.reshape(N_MP, D // N_MP, D)
    attn_out = reduced_backward(lax.optimization_barrier(jnp.sum(reduced_precision(jnp.einsum('sgc,gcd->gsd', context_groups, out_groups, precision=FULL_PRECISION)), axis=0)))
    normed = layer_norm(tokens_f + attn_out, gain_one, bias_one)
    hidden_pre = reduced_backward(jnp.dot(reduced_precision(normed), up_w, precision=FULL_PRECISION))
    activated = reduced_precision(jax.nn.gelu(hidden_pre, approximate=False))
    act_groups = activated.reshape(seq_len, N_MP, FF // N_MP)
    down_groups = down_w.reshape(N_MP, FF // N_MP, D)
    branch = reduced_backward(lax.optimization_barrier(jnp.sum(reduced_precision(jnp.einsum('sgf,gfd->gsd', act_groups, down_groups, precision=FULL_PRECISION)), axis=0)))
    return layer_norm(normed + branch, gain_two, bias_two) * live_f[:, None]

def reference(tokens, lengths, qkv_weight, out_weight, conv_taps, norm1_gain, norm1_bias, norm2_gain, norm2_bias, up_weight, down_weight, cotangent):
    params = (qkv_weight.astype(jnp.float32), out_weight.astype(jnp.float32), conv_taps.astype(jnp.float32), norm1_gain.astype(jnp.float32), norm1_bias.astype(jnp.float32), norm2_gain.astype(jnp.float32), norm2_bias.astype(jnp.float32), up_weight.astype(jnp.float32), down_weight.astype(jnp.float32))

    def forward(weights, inputs):

        def per_document(packed):
            return one_document(packed[0], packed[1], weights)
        return lax.map(jax.checkpoint(per_document), (inputs, lengths))
    outputs, pullback = jax.vjp(forward, params, tokens.astype(jnp.float32))
    weight_grads, token_grads = pullback(cotangent.astype(jnp.float32))
    return (outputs.astype(jnp.bfloat16), token_grads.astype(jnp.bfloat16), weight_grads[0], weight_grads[1], weight_grads[2], weight_grads[3], weight_grads[4], weight_grads[5], weight_grads[6], weight_grads[7], weight_grads[8])
```

```python
import functools
import jax
import jax.numpy as jnp
import numpy as np
from jax import lax
from jax.experimental import pallas as pl
from jax.experimental.pallas import tpu as pltpu
from jax.sharding import PartitionSpec as P

HD = 64
LM = 64
KSIZE = 33
HALF = 16
NS_ITERS = 6
EPS = 1e-5
HI = lax.Precision.HIGHEST
BF = jnp.bfloat16
F32 = jnp.float32
SCALE = HD ** -0.5
WIN = 512
BLK = 256


def nn(a, b, precision=None):
    return lax.dot_general(a, b, (((1,), (0,)), ((), ())), precision=precision, preferred_element_type=F32)


def nt(a, b, precision=None):
    return lax.dot_general(a, b, (((1,), (1,)), ((), ())), precision=precision, preferred_element_type=F32)


def tn(a, b, precision=None):
    return lax.dot_general(a, b, (((0,), (0,)), ((), ())), precision=precision, preferred_element_type=F32)


def block_mask(width):
    r = lax.broadcasted_iota(jnp.int32, (width, width), 0) // HD
    c = lax.broadcasted_iota(jnp.int32, (width, width), 1) // HD
    return r == c


def spread(x, heads, mask):
    return jnp.where(mask, jnp.concatenate([x] * heads, axis=0), 0.0)


def members(length, first, count):
    s = lax.broadcasted_iota(jnp.int32, (LM, count), 1) + first
    j = lax.broadcasted_iota(jnp.int32, (LM, count), 0)
    s64 = s * LM
    return (j * length <= s64) & (s64 < (j + 1) * length) & (s < length)


def live_lanes(length, first, count):
    s = lax.broadcasted_iota(jnp.int32, (1, count), 1) + first
    return s < length


def toeplitz(row):
    full = jnp.broadcast_to(row, (BLK, WIN))
    return pltpu.roll(full, 0, 1, stride=1, stride_axis=0)


def windows(x, seq):
    rows = x.shape[0]
    pad = jnp.zeros((rows, 128), x.dtype)
    padded = jnp.concatenate([pad, x, pad], axis=1)
    return [padded[:, b * BLK : b * BLK + WIN] for b in range(seq // BLK)]


def hi_lo(x):
    hi = x.astype(BF)
    return hi, (x - hi.astype(F32)).astype(BF)


def banded(x, row, heads, seq):
    outs = []
    nblk = seq // BLK
    for h in range(heads):
        wins = jnp.concatenate(windows(x[h * HD : (h + 1) * HD], seq), axis=0)
        hi, lo = hi_lo(toeplitz(row[h : h + 1]))
        y = nt(wins, hi) + nt(wins, lo)
        outs.append(jnp.concatenate([y[b * HD : (b + 1) * HD] for b in range(nblk)], axis=1))
    return jnp.concatenate(outs, axis=0)


def attn_fwd_kernel(docs, heads, seq, dest, len_ref, x_ref, wt_ref, taps_ref, qkv_ref, ctx_ref, lq_ref, lk_ref, sum_ref, mix_ref, k2_ref, z_ref, p_ref, l1_ref, l3_ref):
    width = heads * HD
    mask = block_mask(width)
    eye = jnp.where(
        lax.broadcasted_iota(jnp.int32, (width, width), 0) == lax.broadcasted_iota(jnp.int32, (width, width), 1), 1.0, 0.0
    ).astype(F32)
    for d in range(docs):
        for c in range(seq // BLK):
            xc = x_ref[d, c * BLK : (c + 1) * BLK, :]
            qkv_ref[d, :, c * BLK : (c + 1) * BLK] = nt(wt_ref[...], xc).astype(BF)
    k2s = []
    for d in range(docs):
        length = len_ref[d]
        memb = jnp.where(members(length, 0, seq), 1.0, 0.0).astype(F32)
        counts = jnp.maximum(jnp.sum(memb, axis=1, keepdims=True), 1.0)
        memb_b = memb.astype(BF)
        q = qkv_ref[d, 0:width, :]
        k = qkv_ref[d, width : 2 * width, :]
        v = qkv_ref[d, 2 * width : 3 * width, :]
        lq = spread(nt(memb_b, q) / counts, heads, mask).astype(BF)
        lk = spread(nt(memb_b, k) / counts, heads, mask).astype(BF)
        lq_ref[d] = lq
        lk_ref[d] = lk
        s2 = jnp.where(mask, nt(lq, lk) * SCALE, -1e30)
        e2 = jnp.where(mask, jnp.exp(s2 - jnp.max(s2, axis=1, keepdims=True)), 0.0)
        k2 = e2 / jnp.sum(e2, axis=1, keepdims=True)
        k2_ref[d] = k2
        k2s.append(k2)
        s3 = jnp.where(live_lanes(length, 0, seq), nn(lq, k) * SCALE, -1e30)
        m3 = jnp.max(s3, axis=1, keepdims=True)
        e3 = jnp.exp(s3 - m3)
        t3 = jnp.sum(e3, axis=1, keepdims=True)
        l3_ref[d] = jnp.broadcast_to(m3 + jnp.log(t3), (width, 128))
        k3 = (e3 / t3).astype(BF)
        sum_ref[d] = jnp.where(mask, nt(k3, v), 0.0)
    zs = []
    for d in range(docs):
        rows = jnp.sum(k2s[d] * k2s[d], axis=1, keepdims=True)
        tot = jnp.sum(rows.reshape(heads, HD, 1), axis=1, keepdims=True)
        tot = jnp.broadcast_to(tot, (heads, HD, 1)).reshape(width, 1)
        z = k2s[d].T / tot
        z_ref[d, 0] = z
        zs.append(z)
    for i in range(NS_ITERS):
        ps = [nn(k2s[d], zs[d], HI) for d in range(docs)]
        bs = [15.0 * eye - nn(ps[d], 7.0 * eye - ps[d], HI) for d in range(docs)]
        cs = [13.0 * eye - nn(ps[d], bs[d], HI) for d in range(docs)]
        zs = [0.25 * nn(zs[d], cs[d], HI) for d in range(docs)]
        for d in range(docs):
            p_ref[d, i, 0] = ps[d]
            p_ref[d, i, 1] = bs[d]
            p_ref[d, i, 2] = cs[d]
            z_ref[d, i + 1] = zs[d]
    for d in range(docs):
        length = len_ref[d]
        q = qkv_ref[d, 0:width, :]
        v = qkv_ref[d, 2 * width : 3 * width, :]
        live = live_lanes(length, 0, seq)
        mix = jnp.where(mask, nn(zs[d], sum_ref[d], HI), 0.0)
        mix_ref[d] = mix.astype(BF)
        mix_t = mix.T.astype(BF)
        s1 = (nn(lk_ref[d], q) * SCALE).reshape(heads, LM, seq)
        m1 = jnp.max(s1, axis=1, keepdims=True)
        e1 = jnp.exp(s1 - m1)
        t1 = jnp.sum(e1, axis=1, keepdims=True)
        l1_ref[d] = (m1 + jnp.log(t1)).reshape(heads, seq)
        k1 = (e1 / t1).reshape(width, seq).astype(BF)
        vl = jnp.where(live, v, 0).astype(BF)
        ctx = nn(mix_t, k1) + banded(vl, taps_ref[...], heads, seq)
        ctx = jnp.where(live, ctx, 0.0).astype(BF)
        part = seq // dest
        for i in range(dest):
            ctx_ref[i, d] = ctx[:, i * part : (i + 1) * part]


def attn_fwd(lengths, x, wt, taps, dest):
    docs, seq, dim = x.shape
    width = wt.shape[0] // 3
    heads = width // HD
    vm = pl.BlockSpec(memory_space=pltpu.VMEM)
    out = [
        jax.ShapeDtypeStruct((docs, 3 * width, seq), BF),
        jax.ShapeDtypeStruct((dest, docs, width, seq // dest), BF),
        jax.ShapeDtypeStruct((docs, width, width), BF),
        jax.ShapeDtypeStruct((docs, width, width), BF),
        jax.ShapeDtypeStruct((docs, width, width), F32),
        jax.ShapeDtypeStruct((docs, width, width), BF),
        jax.ShapeDtypeStruct((docs, width, width), F32),
        jax.ShapeDtypeStruct((docs, NS_ITERS + 1, width, width), F32),
        jax.ShapeDtypeStruct((docs, NS_ITERS, 3, width, width), F32),
        jax.ShapeDtypeStruct((docs, heads, seq), F32),
        jax.ShapeDtypeStruct((docs, width, 128), F32),
    ]
    return pl.pallas_call(
        functools.partial(attn_fwd_kernel, docs, heads, seq, dest),
        out_shape=out,
        in_specs=[pl.BlockSpec(memory_space=pltpu.SMEM), vm, vm, vm],
        out_specs=[vm] * len(out),
        compiler_params=pltpu.CompilerParams(vmem_limit_bytes=60 * 2**20),
        cost_estimate=pl.CostEstimate(flops=int(8e9), bytes_accessed=int(3e7), transcendentals=0),
        name="attn_fwd",
    )(lengths, x, wt, taps)


def ln_stats(v):
    mu = jnp.mean(v, axis=-1, keepdims=True)
    cen = v - mu
    var = jnp.mean(cen * cen, axis=-1, keepdims=True)
    r = lax.rsqrt(var + EPS)
    return cen * r, r


def ln_back(g, xhat, r):
    m1 = jnp.mean(g, axis=-1, keepdims=True)
    m2 = jnp.mean(g * xhat, axis=-1, keepdims=True)
    return r * (g - m1 - xhat * m2)


ROOT_HALF = 0.7071067811865476
INV_ROOT_2PI = 0.3989422804014327


def ffn_kernel(groups, docs, rows, len_ref, pos_ref, x_ref, cot_ref, ctx_ref, ow_ref, up_ref, dn_ref, g1_ref, b1_ref, g2_ref, b2_ref,
               out_ref, gmix_ref, gctx_ref, gow_ref, gup_ref, gdn_ref, small_ref, nb_s, fac_s, act_s, br_s, x1_s, gn_s):
    n = docs * rows
    dim = x_ref.shape[-1]
    attn = None
    for g in range(groups):
        for d in range(docs):
            pass
    first = pos_ref[0]
    live = jnp.concatenate(
        [
            (lax.broadcasted_iota(jnp.int32, (rows, 1), 0) + first < len_ref[d]).astype(F32)
            for d in range(docs)
        ],
        axis=0,
    )
    parts = []
    for d in range(docs):
        acc = None
        for g in range(groups):
            t = tn(ctx_ref[g, d], ow_ref[g]).astype(BF).astype(F32)
            acc = t if acc is None else acc + t
        parts.append(acc)
    mixed = x_ref[...].reshape(n, dim).astype(F32) + jnp.concatenate(parts, axis=0)
    xh1, r1 = ln_stats(mixed)
    x1_s[...] = xh1
    normed = xh1 * g1_ref[...] + b1_ref[...]
    nb_s[...] = normed.astype(BF)
    br_s[...] = normed

    def fwd_group(g, _):
        h = nt(nb_s[...], up_ref[g])
        phi_big = 0.5 * (1.0 + lax.erf(h * ROOT_HALF))
        act = (h * phi_big).astype(BF)
        act_s[g] = act
        fac_s[g] = phi_big + h * (jnp.exp(-0.5 * h * h) * INV_ROOT_2PI)
        br_s[...] += nn(act, dn_ref[g]).astype(BF).astype(F32)
        return 0

    lax.fori_loop(0, groups, fwd_group, 0)
    xh2, r2 = ln_stats(br_s[...])
    out_ref[...] = (live * (xh2 * g2_ref[...] + b2_ref[...])).astype(BF).reshape(docs, rows, dim)
    g_out = live * cot_ref[...].reshape(n, dim).astype(F32)
    gg2 = jnp.sum(g_out * xh2, axis=0, keepdims=True)
    gb2 = jnp.sum(g_out, axis=0, keepdims=True)
    g_res = ln_back(g_out * g2_ref[...], xh2, r2)
    gn_s[...] = g_res
    gbr = g_res.astype(BF)

    def bwd_group(g, _):
        act = act_s[g]
        gdn_ref[g] = tn(act, gbr).astype(BF)
        g_pre = (nt(gbr, dn_ref[g]) * fac_s[g]).astype(BF)
        gup_ref[g] = tn(g_pre, nb_s[...]).astype(BF)
        gn_s[...] += nn(g_pre, up_ref[g])
        return 0

    lax.fori_loop(0, groups, bwd_group, 0)
    g_n = gn_s[...]
    xh1 = x1_s[...]
    gg1 = jnp.sum(g_n * xh1, axis=0, keepdims=True)
    gb1 = jnp.sum(g_n, axis=0, keepdims=True)
    small_ref[...] = jnp.concatenate([gg1, gb1, gg2, gb2, jnp.zeros((4, dim), F32)], axis=0)
    g_mix = ln_back(g_n * g1_ref[...], xh1, r1)
    gmix_ref[...] = g_mix.reshape(docs, rows, dim)
    g_att = g_mix.astype(BF)
    for g in range(groups):
        acc = None
        for d in range(docs):
            ga = g_att[d * rows : (d + 1) * rows]
            t = nn(ctx_ref[g, d], ga)
            acc = t if acc is None else acc + t
            gctx_ref[g, d] = nt(ow_ref[g], ga).astype(BF)
        gow_ref[g] = acc.astype(BF)


def ffn(lengths, pos, x, cot, ctx, ow, up, dn, g1, b1, g2, b2):
    docs, rows, dim = x.shape
    groups, _, width, _ = ctx.shape
    ff = up.shape[1]
    n = docs * rows
    vm = pl.BlockSpec(memory_space=pltpu.VMEM)
    sm = pl.BlockSpec(memory_space=pltpu.SMEM)
    out = [
        jax.ShapeDtypeStruct((docs, rows, dim), BF),
        jax.ShapeDtypeStruct((docs, rows, dim), F32),
        jax.ShapeDtypeStruct((groups, docs, width, rows), BF),
        jax.ShapeDtypeStruct((groups, width, dim), BF),
        jax.ShapeDtypeStruct((groups, ff, dim), BF),
        jax.ShapeDtypeStruct((groups, ff, dim), BF),
        jax.ShapeDtypeStruct((8, dim), F32),
    ]
    return pl.pallas_call(
        functools.partial(ffn_kernel, groups, docs, rows),
        out_shape=out,
        in_specs=[sm, sm] + [vm] * 10,
        out_specs=[vm] * len(out),
        scratch_shapes=[
            pltpu.VMEM((n, dim), BF),
            pltpu.VMEM((groups, n, ff), F32),
            pltpu.VMEM((groups, n, ff), BF),
            pltpu.VMEM((n, dim), F32),
            pltpu.VMEM((n, dim), F32),
            pltpu.VMEM((n, dim), F32),
        ],
        compiler_params=pltpu.CompilerParams(vmem_limit_bytes=60 * 2**20),
        cost_estimate=pl.CostEstimate(flops=int(1.8e10), bytes_accessed=int(4e7), transcendentals=0),
        name="ffn",
    )(lengths, pos, x, cot, ctx, ow, up, dn, g1, b1, g2, b2)


def attn_bwd_kernel(docs, heads, seq, parts, len_ref, x_ref, wt_ref, taps_ref, rtaps_ref, qkv_ref, gctx_ref, lq_ref, lk_ref, sum_ref, mix_ref, k2_ref,
                    z_ref, p_ref, l1_ref, l3_ref, gqkv_ref, ipart_ref, gtaps_ref, g_s, ginv_s, glq_s, glk_s):
    width = heads * HD
    nblk = seq // BLK
    mask = block_mask(width)
    anti = jnp.where(
        lax.broadcasted_iota(jnp.int32, (BLK, BLK), 0) + lax.broadcasted_iota(jnp.int32, (BLK, BLK), 1) == BLK - 1, 1.0, 0.0
    ).astype(BF)
    gaccs = [None] * heads
    for d in range(docs):
        length = len_ref[d]
        live = live_lanes(length, 0, seq)
        q = qkv_ref[d, 0:width, :]
        k = qkv_ref[d, width : 2 * width, :]
        v = qkv_ref[d, 2 * width : 3 * width, :]
        gc = jnp.concatenate([gctx_ref[i, d] for i in range(parts)], axis=1)
        gc = jnp.where(live, gc, 0).astype(BF)
        lq, lk = lq_ref[d], lk_ref[d]
        s1 = (nn(lk, q) * SCALE).reshape(heads, LM, seq)
        k1 = jnp.exp(s1 - l1_ref[d].reshape(heads, 1, seq))
        gmixing = jnp.where(mask, nt(k1.reshape(width, seq).astype(BF), gc), 0.0)
        gk1 = nn(mix_ref[d], gc).reshape(heads, LM, seq)
        gs1 = (k1 * (gk1 - jnp.sum(gk1 * k1, axis=1, keepdims=True))).reshape(width, seq).astype(BF)
        ginv_s[d] = nt(gmixing, sum_ref[d], HI)
        gsum = tn(z_ref[d, NS_ITERS], gmixing, HI)
        gsum = jnp.where(mask, gsum, 0.0)
        gsum_b = gsum.astype(BF)
        s3 = jnp.where(live, nn(lq, k) * SCALE, -1e30)
        k3 = jnp.exp(s3 - l3_ref[d][:, 0:1])
        gk3 = nn(gsum_b, v)
        gs3 = (k3 * (gk3 - jnp.sum(gk3 * k3, axis=1, keepdims=True))).astype(BF)
        glq_s[d] = jnp.where(mask, nt(gs3, k), 0.0) * SCALE
        glk_s[d] = jnp.where(mask, nt(gs1, q), 0.0) * SCALE
        lq_t = lq.astype(F32).T.astype(BF)
        lk_t = lk.astype(F32).T.astype(BF)
        g_s[d, 0:width, :] = nn(lk_t, gs1) * SCALE
        g_s[d, width : 2 * width, :] = nn(lq_t, gs3) * SCALE
        gv = nn(gsum.T.astype(BF), k3.astype(BF))
        gvl = banded(gc, rtaps_ref[...], heads, seq)
        g_s[d, 2 * width : 3 * width, :] = gv + jnp.where(live, gvl, 0.0)
        vl = jnp.where(live, v, 0).astype(BF)
        for h in range(heads):
            wins = jnp.concatenate(windows(vl[h * HD : (h + 1) * HD], seq), axis=0)
            gch = gc[h * HD : (h + 1) * HD]
            stack = jnp.concatenate([gch[:, b * BLK : (b + 1) * BLK] for b in range(nblk)], axis=0)
            rev = nt(anti, stack).astype(BF)
            t = nn(rev, wins)
            gaccs[h] = t if gaccs[h] is None else gaccs[h] + t
    for h in range(heads):
        rolled = pltpu.roll(gaccs[h], 0, 1, stride=1, stride_axis=0)
        gtaps_ref[h : h + 1, :] = jnp.sum(rolled, axis=0, keepdims=True)
    gz = [ginv_s[d] for d in range(docs)]
    gk = [jnp.zeros((width, width), F32) for _ in range(docs)]
    eye = jnp.where(
        lax.broadcasted_iota(jnp.int32, (width, width), 0) == lax.broadcasted_iota(jnp.int32, (width, width), 1), 1.0, 0.0
    ).astype(F32)
    for i in reversed(range(NS_ITERS)):
        for d in range(docs):
            z, p, b, c = z_ref[d, i], p_ref[d, i, 0], p_ref[d, i, 1], p_ref[d, i, 2]
            a = 7.0 * eye - p
            g = 0.25 * gz[d]
            gc_ = tn(z, g, HI)
            gzn = nt(g, c, HI)
            gp = -nt(gc_, b, HI)
            gb = -tn(p, gc_, HI)
            gp = gp - nt(gb, a, HI)
            ga = -tn(p, gb, HI)
            gp = gp - ga
            gk[d] = gk[d] + nt(gp, z, HI)
            gz[d] = gzn + tn(k2_ref[d], gp, HI)
    for d in range(docs):
        length = len_ref[d]
        k2 = k2_ref[d]
        rows = jnp.sum(k2 * k2, axis=1, keepdims=True)
        tot = jnp.sum(rows.reshape(heads, HD, 1), axis=1, keepdims=True)
        tot = jnp.broadcast_to(tot, (heads, HD, 1)).reshape(width, 1)
        g = gz[d]
        dot = jnp.sum(g * k2.T, axis=1, keepdims=True)
        dot = jnp.sum(dot.reshape(heads, HD, 1), axis=1, keepdims=True)
        dot = jnp.broadcast_to(dot, (heads, HD, 1)).reshape(width, 1)
        gk2 = gk[d] + (g / tot).T - k2 * (2.0 * dot / (tot * tot))
        gs2 = k2 * (gk2 - jnp.sum(gk2 * k2, axis=1, keepdims=True)) * SCALE
        memb = jnp.where(members(length, 0, seq), 1.0, 0.0).astype(F32)
        counts = jnp.maximum(jnp.sum(memb, axis=1, keepdims=True), 1.0)
        counts = jnp.concatenate([counts] * heads, axis=0)
        memb3 = jnp.concatenate([memb.astype(BF)] * heads, axis=0)
        glq = (glq_s[d] + nn(gs2, lk_ref[d].astype(F32), HI)) / counts
        glk = (glk_s[d] + tn(gs2, lq_ref[d].astype(F32), HI)) / counts
        hi, lo = hi_lo(glq.T)
        gq = g_s[d, 0:width, :] + nn(hi, memb3) + nn(lo, memb3)
        hi, lo = hi_lo(glk.T)
        gkk = g_s[d, width : 2 * width, :] + nn(hi, memb3) + nn(lo, memb3)
        g_all = jnp.concatenate([gq, gkk, g_s[d, 2 * width : 3 * width, :]], axis=0).astype(BF)
        gw = nn(g_all, x_ref[d])
        if d == 0:
            gqkv_ref[...] = gw
        else:
            gqkv_ref[...] += gw
        for c in range(nblk):
            ipart_ref[d, c * BLK : (c + 1) * BLK, :] = tn(g_all[:, c * BLK : (c + 1) * BLK], wt_ref[...]).astype(BF)


def attn_bwd(lengths, x, wt, taps, rtaps, qkv, gctx, lq, lk, sm, mix, k2, z, p, l1, l3):
    docs, seq, dim = x.shape
    width = wt.shape[0] // 3
    heads = width // HD
    parts = gctx.shape[0]
    vm = pl.BlockSpec(memory_space=pltpu.VMEM)
    out = [
        jax.ShapeDtypeStruct((3 * width, dim), F32),
        jax.ShapeDtypeStruct((docs, seq, dim), BF),
        jax.ShapeDtypeStruct((heads, WIN), F32),
    ]
    return pl.pallas_call(
        functools.partial(attn_bwd_kernel, docs, heads, seq, parts),
        out_shape=out,
        in_specs=[pl.BlockSpec(memory_space=pltpu.SMEM)] + [vm] * 15,
        out_specs=[vm] * len(out),
        scratch_shapes=[
            pltpu.VMEM((docs, 3 * width, seq), F32),
            pltpu.VMEM((docs, width, width), F32),
            pltpu.VMEM((docs, width, width), F32),
            pltpu.VMEM((docs, width, width), F32),
        ],
        compiler_params=pltpu.CompilerParams(vmem_limit_bytes=60 * 2**20),
        cost_estimate=pl.CostEstimate(flops=int(1.2e10), bytes_accessed=int(3e7), transcendentals=0),
        name="attn_bwd",
    )(lengths, x, wt, taps, rtaps, qkv, gctx, lq, lk, sm, mix, k2, z, p, l1, l3)


def body_factory(dp, mp):
    def body(tokens, lengths, qkv_weight, out_weight, conv_taps, norm1_gain, norm1_bias, norm2_gain, norm2_bias, up_weight, down_weight, cotangent):
        docs, seq, dim = tokens.shape
        width = qkv_weight.shape[2]
        ff = up_weight.shape[1]
        me = lax.axis_index("mp")
        rows = seq // mp
        wt = jnp.transpose(qkv_weight, (0, 2, 1)).reshape(3 * width, dim)
        taps = jnp.pad(conv_taps, ((0, 0), (112, WIN - 112 - KSIZE)))
        rtaps = jnp.pad(conv_taps[:, ::-1], ((0, 0), (112, WIN - 112 - KSIZE)))
        qkv, ctx, lq, lk, sm, mix, k2, z, p, l1, l3 = attn_fwd(lengths, tokens, wt, taps, mp)
        ctx_rows = lax.all_to_all(ctx, "mp", 0, 0, tiled=True)
        w_all = jnp.concatenate([out_weight, up_weight.T, down_weight], axis=0)
        w_all = lax.all_gather(w_all, "mp", axis=0, tiled=False)
        ow, up, dn = w_all[:, :width], w_all[:, width : width + ff], w_all[:, width + ff :]
        first = me * rows
        x_rows = lax.dynamic_slice_in_dim(tokens, first, rows, 1)
        cot_rows = lax.dynamic_slice_in_dim(cotangent, first, rows, 1)
        pos = jnp.reshape(first, (1,)).astype(jnp.int32)
        out_rows, gmix, gctx, gow, gup, gdn, small = ffn(
            lengths, pos, x_rows, cot_rows, ctx_rows, ow, up, dn,
            norm1_gain[None], norm1_bias[None], norm2_gain[None], norm2_bias[None],
        )
        output = lax.all_gather(out_rows, "mp", axis=1, tiled=True)
        gctx_heads = lax.all_to_all(gctx, "mp", 0, 0, tiled=True)
        gw = jnp.concatenate([gow, gup, gdn], axis=1)
        gw = lax.psum_scatter(gw, "mp", scatter_dimension=0, tiled=False)
        gw = lax.psum(gw, "dp").astype(F32)
        gqkv, ipart, gtaps = attn_bwd(lengths, tokens, wt, taps, rtaps, qkv, gctx_heads, lq, lk, sm, mix, k2, z, p, l1, l3)
        ipart = lax.psum_scatter(ipart, "mp", scatter_dimension=1, tiled=True).astype(F32)
        input_grad = lax.all_gather((gmix + ipart).astype(BF), "mp", axis=1, tiled=True)
        gqkv = lax.psum(gqkv.astype(BF), "dp").astype(F32)
        gqkv = jnp.transpose(gqkv.reshape(3, width, dim), (0, 2, 1))
        small = lax.psum(small, ("dp", "mp"))
        gtaps = lax.psum(gtaps, "dp")
        gtaps = lax.slice_in_dim(gtaps, 367, 367 + KSIZE, axis=1)
        return (
            output, input_grad, gqkv, gw[:width], gtaps, small[0], small[1], small[2], small[3],
            gw[width : width + ff].T, gw[width + ff :],
        )
    return body


def solution(mesh):
    return jax.shard_map(
        body_factory(mesh.shape["dp"], mesh.shape["mp"]),
        mesh=mesh,
        in_specs=(
            P("dp", None, None), P("dp"), P(None, None, "mp"), P("mp", None), P("mp", None),
            P(), P(), P(), P(), P(None, "mp"), P("mp", None), P("dp", None, None),
        ),
        out_specs=(
            P("dp", None, None), P("dp", None, None), P(None, None, "mp"), P("mp", None), P("mp", None),
            P(), P(), P(), P(), P(None, "mp"), P("mp", None),
        ),
        check_vma=False,
    )
```

```python
import functools
import jax
import jax.numpy as jnp
import numpy as np
from jax import lax
from jax.experimental import pallas as pl
from jax.experimental.pallas import tpu as pltpu
from jax.sharding import PartitionSpec as P

HD = 64
LM = 64
KSIZE = 33
HALF = 16
NS_ITERS = 6
EPS = 1e-5
HI = lax.Precision.HIGHEST
BF = jnp.bfloat16
F32 = jnp.float32
SCALE = HD ** -0.5
WIN = 512
BLK = 256


def nn(a, b, precision=None):
    return lax.dot_general(a, b, (((1,), (0,)), ((), ())), precision=precision, preferred_element_type=F32)


def nt(a, b, precision=None):
    return lax.dot_general(a, b, (((1,), (1,)), ((), ())), precision=precision, preferred_element_type=F32)


def tn(a, b, precision=None):
    return lax.dot_general(a, b, (((0,), (0,)), ((), ())), precision=precision, preferred_element_type=F32)


def block_mask(width):
    r = lax.broadcasted_iota(jnp.int32, (width, width), 0) // HD
    c = lax.broadcasted_iota(jnp.int32, (width, width), 1) // HD
    return r == c


def spread(x, heads, mask):
    return jnp.where(mask, jnp.concatenate([x] * heads, axis=0), 0.0)


def members(length, first, count):
    s = lax.broadcasted_iota(jnp.int32, (LM, count), 1) + first
    j = lax.broadcasted_iota(jnp.int32, (LM, count), 0)
    s64 = s * LM
    return (j * length <= s64) & (s64 < (j + 1) * length) & (s < length)


def live_lanes(length, first, count):
    s = lax.broadcasted_iota(jnp.int32, (1, count), 1) + first
    return s < length


def toeplitz(row):
    full = jnp.broadcast_to(row, (BLK, WIN))
    return pltpu.roll(full, 0, 1, stride=1, stride_axis=0)


def windows(x, seq):
    rows = x.shape[0]
    pad = jnp.zeros((rows, 128), x.dtype)
    padded = jnp.concatenate([pad, x, pad], axis=1)
    return [padded[:, b * BLK : b * BLK + WIN] for b in range(seq // BLK)]


def hi_lo(x):
    hi = x.astype(BF)
    return hi, (x - hi.astype(F32)).astype(BF)


def banded(x, row, heads, seq):
    outs = []
    nblk = seq // BLK
    for h in range(heads):
        wins = jnp.concatenate(windows(x[h * HD : (h + 1) * HD], seq), axis=0)
        hi, lo = hi_lo(toeplitz(row[h : h + 1]))
        y = nt(wins, hi) + nt(wins, lo)
        outs.append(jnp.concatenate([y[b * HD : (b + 1) * HD] for b in range(nblk)], axis=1))
    return jnp.concatenate(outs, axis=0)


MESH = pl.DeviceIdType.MESH


def flip(i, bit):
    return i + bit * (1 - 2 * ((i // bit) % 2))


def partner(i, m):
    for bit in (1, 2, 4):
        if m & bit:
            i = flip(i, bit)
    return i


def greet(peers):
    bar = pltpu.get_barrier_semaphore()
    for p in peers:
        pl.semaphore_signal(bar, inc=1, device_id=p, device_id_type=MESH)
    pl.semaphore_wait(bar, len(peers))


def rcopy(src, dst, ss, rs, dev):
    return pltpu.make_async_remote_copy(src_ref=src, dst_ref=dst, send_sem=ss, recv_sem=rs, device_id=dev, device_id_type=MESH)


SLOTS = 8
OW_ROWS, UP_ROWS, DN_ROWS = 24, 96, 96
SLICE = OW_ROWS + UP_ROWS + DN_ROWS
CUT = OW_ROWS + UP_ROWS


class Gather:
    def __init__(self, mp, srcs, wall, zsem, xsem, csem, lsem):
        self.wall, self.zsem, self.xsem, self.csem, self.lsem = wall, zsem, xsem, csem, lsem
        self.srcs = srcs
        self.mp = mp
        self.z = lax.axis_index("mp")
        self.d = lax.axis_index("dp")
        self.r = lax.rem(self.d, SLOTS)

    def rows(self, i):
        size = (OW_ROWS, UP_ROWS, DN_ROWS)[i]
        lo = (0, OW_ROWS, CUT)[i]
        return self.srcs[i].at[pl.ds(pl.multiple_of(self.r * size, 8), size)], lo, size

    def z_copies(self, m):
        out = []
        for i in range(3):
            src, lo, size = self.rows(i)
            out.append(rcopy(src, self.wall.at[self.z, self.r, pl.ds(lo, size)], self.zsem.at[0, m - 1, i], self.zsem.at[1, m - 1, i], {"mp": partner(self.z, m)}))
        return out

    def y(self, m):
        s = self.wall.at[partner(self.z, m), self.r]
        return rcopy(s, s, self.xsem.at[0, m - 1, 0], self.xsem.at[1, m - 1, 0], {"dp": flip(self.d, 4)})

    def x(self, m):
        s = self.wall.at[partner(self.z, m), self.r]
        return rcopy(s, s, self.xsem.at[0, m - 1, 1], self.xsem.at[1, m - 1, 1], {"dp": flip(self.d, 2)})

    def yx(self, m):
        s = self.wall.at[partner(self.z, m), flip(self.r, 4), pl.ds(0, CUT)]
        return rcopy(s, s, self.xsem.at[0, m - 1, 2], self.xsem.at[1, m - 1, 2], {"dp": flip(self.d, 2)})

    def xy(self, m):
        s = self.wall.at[partner(self.z, m), flip(self.r, 2), pl.ds(CUT, DN_ROWS)]
        return rcopy(s, s, self.xsem.at[0, m - 1, 3], self.xsem.at[1, m - 1, 3], {"dp": flip(self.d, 4)})

    def core(self, m, q):
        r = (self.r, flip(self.r, 4), flip(self.r, 2), partner(self.r, 6))[q]
        s = self.wall.at[partner(self.z, m), r]
        return rcopy(s, s, self.csem.at[0, m - 1, q], self.csem.at[1, m - 1, q], {"dp": flip(self.d, 1)})

    def start(self):
        for m in range(1, self.mp):
            for c in self.z_copies(m):
                c.start()
        for i in range(3):
            size = (OW_ROWS, UP_ROWS, DN_ROWS)[i]
            lo = (0, OW_ROWS, CUT)[i]
            for r in range(SLOTS):
                pltpu.make_async_copy(self.srcs[i].at[pl.ds(r * size, size)], self.wall.at[self.z, r, pl.ds(lo, size)], self.lsem.at[i, r]).start()

    def step1(self, m):
        for c in self.z_copies(m):
            c.wait_recv()
        self.y(m).start()
        self.x(m).start()
        self.core(m, 0).start()

    def step2(self, m):
        self.y(m).wait_recv()
        self.yx(m).start()
        self.core(m, 1).start()
        self.x(m).wait_recv()
        self.xy(m).start()
        self.core(m, 2).start()

    def step3(self, m):
        self.yx(m).wait_recv()
        self.xy(m).wait_recv()
        self.core(m, 3).start()

    def finish(self):
        for i in range(3):
            size = (OW_ROWS, UP_ROWS, DN_ROWS)[i]
            lo = (0, OW_ROWS, CUT)[i]
            for r in range(SLOTS):
                pltpu.make_async_copy(self.srcs[i].at[pl.ds(r * size, size)], self.wall.at[self.z, r, pl.ds(lo, size)], self.lsem.at[i, r]).wait()
        for m in range(1, self.mp):
            for c in self.z_copies(m):
                c.wait_send()
            for c in (self.y(m), self.x(m), self.yx(m), self.xy(m)):
                c.wait_send()
            for q in range(4):
                self.core(m, q).wait()


def attn_fwd_kernel(docs, heads, seq, dest, len_ref, x_ref, wt_ref, taps_ref, ow_ref, up_ref, dn_ref, qkv_ref, ctx_ref, lq_ref, lk_ref, sum_ref, mix_ref, k2_ref, z_ref, p_ref, l1_ref, l3_ref, wall_ref,
                    ctx_s, zsem, xsem, csem, lsem, asem):
    width = heads * HD
    me = lax.axis_index("mp")
    dd = lax.axis_index("dp")
    greet([{"mp": partner(me, m)} for m in range(1, dest)] + [{"dp": flip(dd, b)} for b in (1, 2, 4)])
    gather = Gather(dest, (ow_ref, up_ref, dn_ref), wall_ref, zsem, xsem, csem, lsem)
    gather.start()

    def a_copy(m, d):
        return rcopy(ctx_s.at[partner(me, m), d], ctx_ref.at[me, d], asem.at[0, m - 1, d], asem.at[1, m - 1, d], {"mp": partner(me, m)})

    mask = block_mask(width)
    eye = jnp.where(
        lax.broadcasted_iota(jnp.int32, (width, width), 0) == lax.broadcasted_iota(jnp.int32, (width, width), 1), 1.0, 0.0
    ).astype(F32)
    for d in range(docs):
        for c in range(seq // BLK):
            xc = x_ref[d, c * BLK : (c + 1) * BLK, :]
            qkv_ref[d, :, c * BLK : (c + 1) * BLK] = nt(wt_ref[...], xc).astype(BF)
    gather.step1(1)
    k2s = []
    for d in range(docs):
        if d == 1:
            gather.step1(2)
        length = len_ref[d]
        memb = jnp.where(members(length, 0, seq), 1.0, 0.0).astype(F32)
        counts = jnp.maximum(jnp.sum(memb, axis=1, keepdims=True), 1.0)
        memb_b = memb.astype(BF)
        q = qkv_ref[d, 0:width, :]
        k = qkv_ref[d, width : 2 * width, :]
        v = qkv_ref[d, 2 * width : 3 * width, :]
        lq = spread(nt(memb_b, q) / counts, heads, mask).astype(BF)
        lk = spread(nt(memb_b, k) / counts, heads, mask).astype(BF)
        lq_ref[d] = lq
        lk_ref[d] = lk
        s2 = jnp.where(mask, nt(lq, lk) * SCALE, -1e30)
        e2 = jnp.where(mask, jnp.exp(s2 - jnp.max(s2, axis=1, keepdims=True)), 0.0)
        k2 = e2 / jnp.sum(e2, axis=1, keepdims=True)
        k2_ref[d] = k2
        k2s.append(k2)
        s3 = jnp.where(live_lanes(length, 0, seq), nn(lq, k) * SCALE, -1e30)
        m3 = jnp.max(s3, axis=1, keepdims=True)
        e3 = jnp.exp(s3 - m3)
        t3 = jnp.sum(e3, axis=1, keepdims=True)
        l3_ref[d] = jnp.broadcast_to(m3 + jnp.log(t3), (width, 128))
        k3 = (e3 / t3).astype(BF)
        sum_ref[d] = jnp.where(mask, nt(k3, v), 0.0)
    zs = []
    for d in range(docs):
        rows = jnp.sum(k2s[d] * k2s[d], axis=1, keepdims=True)
        tot = jnp.sum(rows.reshape(heads, HD, 1), axis=1, keepdims=True)
        tot = jnp.broadcast_to(tot, (heads, HD, 1)).reshape(width, 1)
        z = k2s[d].T / tot
        z_ref[d, 0] = z
        zs.append(z)
    for i in range(NS_ITERS):
        ps = [nn(k2s[d], zs[d], HI) for d in range(docs)]
        bs = [15.0 * eye - nn(ps[d], 7.0 * eye - ps[d], HI) for d in range(docs)]
        cs = [13.0 * eye - nn(ps[d], bs[d], HI) for d in range(docs)]
        zs = [0.25 * nn(zs[d], cs[d], HI) for d in range(docs)]
        for d in range(docs):
            p_ref[d, i, 0] = ps[d]
            p_ref[d, i, 1] = bs[d]
            p_ref[d, i, 2] = cs[d]
            z_ref[d, i + 1] = zs[d]
        if i == 2:
            gather.step1(3)
        if i == 4:
            gather.step2(1)
    for d in range(docs):
        length = len_ref[d]
        q = qkv_ref[d, 0:width, :]
        v = qkv_ref[d, 2 * width : 3 * width, :]
        live = live_lanes(length, 0, seq)
        mix = jnp.where(mask, nn(zs[d], sum_ref[d], HI), 0.0)
        mix_ref[d] = mix.astype(BF)
        mix_t = mix.T.astype(BF)
        s1 = (nn(lk_ref[d], q) * SCALE).reshape(heads, LM, seq)
        m1 = jnp.max(s1, axis=1, keepdims=True)
        e1 = jnp.exp(s1 - m1)
        t1 = jnp.sum(e1, axis=1, keepdims=True)
        l1_ref[d] = (m1 + jnp.log(t1)).reshape(heads, seq)
        k1 = (e1 / t1).reshape(width, seq).astype(BF)
        vl = jnp.where(live, v, 0).astype(BF)
        ctx = nn(mix_t, k1) + banded(vl, taps_ref[...], heads, seq)
        ctx = jnp.where(live, ctx, 0.0).astype(BF)
        part = seq // dest
        for i in range(dest):
            ctx_s[i, d] = ctx[:, i * part : (i + 1) * part]
        for m in range(1, dest):
            a_copy(m, d).start()
        ctx_ref[me, d] = ctx_s[me, d]
        if d == 0:
            gather.step2(2)
    gather.step3(1)
    gather.step2(3)
    gather.step3(2)
    gather.step3(3)
    gather.finish()
    for d in range(docs):
        for m in range(1, dest):
            a_copy(m, d).wait()


def attn_fwd(lengths, x, wt, taps, ow, up, dn, dest):
    docs, seq, dim = x.shape
    width = wt.shape[0] // 3
    heads = width // HD
    vm = pl.BlockSpec(memory_space=pltpu.VMEM)
    out = [
        jax.ShapeDtypeStruct((docs, 3 * width, seq), BF),
        jax.ShapeDtypeStruct((dest, docs, width, seq // dest), BF),
        jax.ShapeDtypeStruct((docs, width, width), BF),
        jax.ShapeDtypeStruct((docs, width, width), BF),
        jax.ShapeDtypeStruct((docs, width, width), F32),
        jax.ShapeDtypeStruct((docs, width, width), BF),
        jax.ShapeDtypeStruct((docs, width, width), F32),
        jax.ShapeDtypeStruct((docs, NS_ITERS + 1, width, width), F32),
        jax.ShapeDtypeStruct((docs, NS_ITERS, 3, width, width), F32),
        jax.ShapeDtypeStruct((docs, heads, seq), F32),
        jax.ShapeDtypeStruct((docs, width, 128), F32),
        jax.ShapeDtypeStruct((dest, SLOTS, SLICE, dim), BF),
    ]
    any_ = pl.BlockSpec(memory_space=pl.ANY)
    dma = pltpu.SemaphoreType.DMA
    return pl.pallas_call(
        functools.partial(attn_fwd_kernel, docs, heads, seq, dest),
        out_shape=out,
        in_specs=[pl.BlockSpec(memory_space=pltpu.SMEM), vm, vm, vm, any_, any_, any_],
        out_specs=[vm] * (len(out) - 1) + [any_],
        scratch_shapes=[
            pltpu.VMEM((dest, docs, width, seq // dest), BF),
            dma((2, dest - 1, 3)),
            dma((2, dest - 1, 4)),
            dma((2, dest - 1, 4)),
            dma((3, SLOTS)),
            dma((2, dest - 1, docs)),
        ],
        compiler_params=pltpu.CompilerParams(vmem_limit_bytes=60 * 2**20, collective_id=0, has_side_effects=True),
        cost_estimate=pl.CostEstimate(flops=int(8e9), bytes_accessed=int(3e7), transcendentals=0),
        name="attn_fwd",
    )(lengths, x, wt, taps, ow, up, dn)


def ln_stats(v):
    mu = jnp.mean(v, axis=-1, keepdims=True)
    cen = v - mu
    var = jnp.mean(cen * cen, axis=-1, keepdims=True)
    r = lax.rsqrt(var + EPS)
    return cen * r, r


def ln_back(g, xhat, r):
    m1 = jnp.mean(g, axis=-1, keepdims=True)
    m2 = jnp.mean(g * xhat, axis=-1, keepdims=True)
    return r * (g - m1 - xhat * m2)


ROOT_HALF = 0.7071067811865476
INV_ROOT_2PI = 0.3989422804014327


def ffn_kernel(groups, docs, rows, len_ref, pos_ref, x_ref, cot_ref, ctx_ref, wall_ref, g1_ref, b1_ref, g2_ref, b2_ref,
               out_ref, gmix_ref, gctx_ref, gw_ref, small_ref, nb_s, fac_s, act_s, br_s, x1_s, gn_s):
    n = docs * rows
    dim = x_ref.shape[-1]
    ff = SLOTS * UP_ROWS

    def ow(g):
        return wall_ref[g, :, 0:OW_ROWS, :].reshape(SLOTS * OW_ROWS, dim)

    def up(g):
        return wall_ref[g, :, OW_ROWS:CUT, :].reshape(SLOTS * UP_ROWS, dim)

    def dn(g):
        return wall_ref[g, :, CUT:SLICE, :].reshape(SLOTS * DN_ROWS, dim)

    first = pos_ref[0]
    live = jnp.concatenate(
        [
            (lax.broadcasted_iota(jnp.int32, (rows, 1), 0) + first < len_ref[d]).astype(F32)
            for d in range(docs)
        ],
        axis=0,
    )
    parts = []
    for d in range(docs):
        acc = None
        for g in range(groups):
            t = tn(ctx_ref[g, d], ow(g)).astype(BF).astype(F32)
            acc = t if acc is None else acc + t
        parts.append(acc)
    mixed = x_ref[...].reshape(n, dim).astype(F32) + jnp.concatenate(parts, axis=0)
    xh1, r1 = ln_stats(mixed)
    x1_s[...] = xh1
    normed = xh1 * g1_ref[...] + b1_ref[...]
    nb_s[...] = normed.astype(BF)
    br_s[...] = normed

    def fwd_group(g, _):
        h = nn(nb_s[...], up(g))
        phi_big = 0.5 * (1.0 + lax.erf(h * ROOT_HALF))
        act = (h * phi_big).astype(BF)
        act_s[g] = act
        fac_s[g] = phi_big + h * (jnp.exp(-0.5 * h * h) * INV_ROOT_2PI)
        br_s[...] += nn(act, dn(g)).astype(BF).astype(F32)
        return 0

    lax.fori_loop(0, groups, fwd_group, 0)
    xh2, r2 = ln_stats(br_s[...])
    out_ref[...] = (live * (xh2 * g2_ref[...] + b2_ref[...])).astype(BF).reshape(docs, rows, dim)
    g_out = live * cot_ref[...].reshape(n, dim).astype(F32)
    gg2 = jnp.sum(g_out * xh2, axis=0, keepdims=True)
    gb2 = jnp.sum(g_out, axis=0, keepdims=True)
    g_res = ln_back(g_out * g2_ref[...], xh2, r2)
    gn_s[...] = g_res
    gbr = g_res.astype(BF)

    def bwd_group(g, _):
        act = act_s[g]
        gw_ref[g, :, CUT:SLICE, :] = tn(act, gbr).astype(BF).reshape(SLOTS, DN_ROWS, dim)
        g_pre = (nt(gbr, dn(g)) * fac_s[g]).astype(BF)
        gw_ref[g, :, OW_ROWS:CUT, :] = tn(nb_s[...], g_pre).astype(BF).reshape(SLOTS, UP_ROWS, ff)
        gn_s[...] += nt(g_pre, up(g))
        return 0

    lax.fori_loop(0, groups, bwd_group, 0)
    g_n = gn_s[...]
    xh1 = x1_s[...]
    gg1 = jnp.sum(g_n * xh1, axis=0, keepdims=True)
    gb1 = jnp.sum(g_n, axis=0, keepdims=True)
    small_ref[...] = jnp.concatenate([gg1, gb1, gg2, gb2, jnp.zeros((4, dim), F32)], axis=0)
    g_mix = ln_back(g_n * g1_ref[...], xh1, r1)
    gmix_ref[...] = g_mix.reshape(docs, rows, dim)
    g_att = g_mix.astype(BF)
    for g in range(groups):
        acc = None
        for d in range(docs):
            ga = g_att[d * rows : (d + 1) * rows]
            t = nn(ctx_ref[g, d], ga)
            acc = t if acc is None else acc + t
            gctx_ref[g, d] = nt(ow(g), ga).astype(BF)
        gw_ref[g, :, 0:OW_ROWS, :] = acc.astype(BF).reshape(SLOTS, OW_ROWS, dim)


def ffn(lengths, pos, x, cot, ctx, wall, g1, b1, g2, b2):
    docs, rows, dim = x.shape
    groups, _, width, _ = ctx.shape
    ff = SLOTS * UP_ROWS
    n = docs * rows
    vm = pl.BlockSpec(memory_space=pltpu.VMEM)
    sm = pl.BlockSpec(memory_space=pltpu.SMEM)
    out = [
        jax.ShapeDtypeStruct((docs, rows, dim), BF),
        jax.ShapeDtypeStruct((docs, rows, dim), F32),
        jax.ShapeDtypeStruct((groups, docs, width, rows), BF),
        jax.ShapeDtypeStruct(wall.shape, BF),
        jax.ShapeDtypeStruct((8, dim), F32),
    ]
    return pl.pallas_call(
        functools.partial(ffn_kernel, groups, docs, rows),
        out_shape=out,
        in_specs=[sm, sm] + [vm] * 8,
        out_specs=[vm] * len(out),
        scratch_shapes=[
            pltpu.VMEM((n, dim), BF),
            pltpu.VMEM((groups, n, ff), F32),
            pltpu.VMEM((groups, n, ff), BF),
            pltpu.VMEM((n, dim), F32),
            pltpu.VMEM((n, dim), F32),
            pltpu.VMEM((n, dim), F32),
        ],
        compiler_params=pltpu.CompilerParams(vmem_limit_bytes=60 * 2**20),
        cost_estimate=pl.CostEstimate(flops=int(1.8e10), bytes_accessed=int(4e7), transcendentals=0),
        name="ffn",
    )(lengths, pos, x, cot, ctx, wall, g1, b1, g2, b2)


def attn_bwd_kernel(docs, heads, seq, parts, len_ref, x_ref, wt_ref, taps_ref, rtaps_ref, qkv_ref, gctx_ref, lq_ref, lk_ref, sum_ref, mix_ref, k2_ref,
                    z_ref, p_ref, l1_ref, l3_ref, gqkv_ref, ipart_ref, gtaps_ref, g_s, ginv_s, glq_s, glk_s):
    width = heads * HD
    nblk = seq // BLK
    mask = block_mask(width)
    anti = jnp.where(
        lax.broadcasted_iota(jnp.int32, (BLK, BLK), 0) + lax.broadcasted_iota(jnp.int32, (BLK, BLK), 1) == BLK - 1, 1.0, 0.0
    ).astype(BF)
    gaccs = [None] * heads
    for d in range(docs):
        length = len_ref[d]
        live = live_lanes(length, 0, seq)
        q = qkv_ref[d, 0:width, :]
        k = qkv_ref[d, width : 2 * width, :]
        v = qkv_ref[d, 2 * width : 3 * width, :]
        gc = jnp.concatenate([gctx_ref[i, d] for i in range(parts)], axis=1)
        gc = jnp.where(live, gc, 0).astype(BF)
        lq, lk = lq_ref[d], lk_ref[d]
        s1 = (nn(lk, q) * SCALE).reshape(heads, LM, seq)
        k1 = jnp.exp(s1 - l1_ref[d].reshape(heads, 1, seq))
        gmixing = jnp.where(mask, nt(k1.reshape(width, seq).astype(BF), gc), 0.0)
        gk1 = nn(mix_ref[d], gc).reshape(heads, LM, seq)
        gs1 = (k1 * (gk1 - jnp.sum(gk1 * k1, axis=1, keepdims=True))).reshape(width, seq).astype(BF)
        ginv_s[d] = nt(gmixing, sum_ref[d], HI)
        gsum = tn(z_ref[d, NS_ITERS], gmixing, HI)
        gsum = jnp.where(mask, gsum, 0.0)
        gsum_b = gsum.astype(BF)
        s3 = jnp.where(live, nn(lq, k) * SCALE, -1e30)
        k3 = jnp.exp(s3 - l3_ref[d][:, 0:1])
        gk3 = nn(gsum_b, v)
        gs3 = (k3 * (gk3 - jnp.sum(gk3 * k3, axis=1, keepdims=True))).astype(BF)
        glq_s[d] = jnp.where(mask, nt(gs3, k), 0.0) * SCALE
        glk_s[d] = jnp.where(mask, nt(gs1, q), 0.0) * SCALE
        lq_t = lq.astype(F32).T.astype(BF)
        lk_t = lk.astype(F32).T.astype(BF)
        g_s[d, 0:width, :] = nn(lk_t, gs1) * SCALE
        g_s[d, width : 2 * width, :] = nn(lq_t, gs3) * SCALE
        gv = nn(gsum.T.astype(BF), k3.astype(BF))
        gvl = banded(gc, rtaps_ref[...], heads, seq)
        g_s[d, 2 * width : 3 * width, :] = gv + jnp.where(live, gvl, 0.0)
        vl = jnp.where(live, v, 0).astype(BF)
        for h in range(heads):
            wins = jnp.concatenate(windows(vl[h * HD : (h + 1) * HD], seq), axis=0)
            gch = gc[h * HD : (h + 1) * HD]
            stack = jnp.concatenate([gch[:, b * BLK : (b + 1) * BLK] for b in range(nblk)], axis=0)
            rev = nt(anti, stack).astype(BF)
            t = nn(rev, wins)
            gaccs[h] = t if gaccs[h] is None else gaccs[h] + t
    for h in range(heads):
        rolled = pltpu.roll(gaccs[h], 0, 1, stride=1, stride_axis=0)
        gtaps_ref[h : h + 1, :] = jnp.sum(rolled, axis=0, keepdims=True)
    gz = [ginv_s[d] for d in range(docs)]
    gk = [jnp.zeros((width, width), F32) for _ in range(docs)]
    eye = jnp.where(
        lax.broadcasted_iota(jnp.int32, (width, width), 0) == lax.broadcasted_iota(jnp.int32, (width, width), 1), 1.0, 0.0
    ).astype(F32)
    for i in reversed(range(NS_ITERS)):
        for d in range(docs):
            z, p, b, c = z_ref[d, i], p_ref[d, i, 0], p_ref[d, i, 1], p_ref[d, i, 2]
            a = 7.0 * eye - p
            g = 0.25 * gz[d]
            gc_ = tn(z, g, HI)
            gzn = nt(g, c, HI)
            gp = -nt(gc_, b, HI)
            gb = -tn(p, gc_, HI)
            gp = gp - nt(gb, a, HI)
            ga = -tn(p, gb, HI)
            gp = gp - ga
            gk[d] = gk[d] + nt(gp, z, HI)
            gz[d] = gzn + tn(k2_ref[d], gp, HI)
    for d in range(docs):
        length = len_ref[d]
        k2 = k2_ref[d]
        rows = jnp.sum(k2 * k2, axis=1, keepdims=True)
        tot = jnp.sum(rows.reshape(heads, HD, 1), axis=1, keepdims=True)
        tot = jnp.broadcast_to(tot, (heads, HD, 1)).reshape(width, 1)
        g = gz[d]
        dot = jnp.sum(g * k2.T, axis=1, keepdims=True)
        dot = jnp.sum(dot.reshape(heads, HD, 1), axis=1, keepdims=True)
        dot = jnp.broadcast_to(dot, (heads, HD, 1)).reshape(width, 1)
        gk2 = gk[d] + (g / tot).T - k2 * (2.0 * dot / (tot * tot))
        gs2 = k2 * (gk2 - jnp.sum(gk2 * k2, axis=1, keepdims=True)) * SCALE
        memb = jnp.where(members(length, 0, seq), 1.0, 0.0).astype(F32)
        counts = jnp.maximum(jnp.sum(memb, axis=1, keepdims=True), 1.0)
        counts = jnp.concatenate([counts] * heads, axis=0)
        memb3 = jnp.concatenate([memb.astype(BF)] * heads, axis=0)
        glq = (glq_s[d] + nn(gs2, lk_ref[d].astype(F32), HI)) / counts
        glk = (glk_s[d] + tn(gs2, lq_ref[d].astype(F32), HI)) / counts
        hi, lo = hi_lo(glq.T)
        gq = g_s[d, 0:width, :] + nn(hi, memb3) + nn(lo, memb3)
        hi, lo = hi_lo(glk.T)
        gkk = g_s[d, width : 2 * width, :] + nn(hi, memb3) + nn(lo, memb3)
        g_all = jnp.concatenate([gq, gkk, g_s[d, 2 * width : 3 * width, :]], axis=0).astype(BF)
        gw = nn(g_all, x_ref[d])
        if d == 0:
            gqkv_ref[...] = gw
        else:
            gqkv_ref[...] += gw
        for c in range(nblk):
            ipart_ref[d, c * BLK : (c + 1) * BLK, :] = tn(g_all[:, c * BLK : (c + 1) * BLK], wt_ref[...]).astype(BF)


def attn_bwd(lengths, x, wt, taps, rtaps, qkv, gctx, lq, lk, sm, mix, k2, z, p, l1, l3):
    docs, seq, dim = x.shape
    width = wt.shape[0] // 3
    heads = width // HD
    parts = gctx.shape[0]
    vm = pl.BlockSpec(memory_space=pltpu.VMEM)
    out = [
        jax.ShapeDtypeStruct((3 * width, dim), F32),
        jax.ShapeDtypeStruct((docs, seq, dim), BF),
        jax.ShapeDtypeStruct((heads, WIN), F32),
    ]
    return pl.pallas_call(
        functools.partial(attn_bwd_kernel, docs, heads, seq, parts),
        out_shape=out,
        in_specs=[pl.BlockSpec(memory_space=pltpu.SMEM)] + [vm] * 15,
        out_specs=[vm] * len(out),
        scratch_shapes=[
            pltpu.VMEM((docs, 3 * width, seq), F32),
            pltpu.VMEM((docs, width, width), F32),
            pltpu.VMEM((docs, width, width), F32),
            pltpu.VMEM((docs, width, width), F32),
        ],
        compiler_params=pltpu.CompilerParams(vmem_limit_bytes=60 * 2**20),
        cost_estimate=pl.CostEstimate(flops=int(1.2e10), bytes_accessed=int(3e7), transcendentals=0),
        name="attn_bwd",
    )(lengths, x, wt, taps, rtaps, qkv, gctx, lq, lk, sm, mix, k2, z, p, l1, l3)


def body_factory(dp, mp):
    def body(tokens, lengths, qkv_weight, out_weight, conv_taps, norm1_gain, norm1_bias, norm2_gain, norm2_bias, up_weight, down_weight, cotangent):
        docs, seq, dim = tokens.shape
        width = qkv_weight.shape[2]
        ff = up_weight.shape[1]
        me = lax.axis_index("mp")
        rows = seq // mp
        wt = jnp.transpose(qkv_weight, (0, 2, 1)).reshape(3 * width, dim)
        taps = jnp.pad(conv_taps, ((0, 0), (112, WIN - 112 - KSIZE)))
        rtaps = jnp.pad(conv_taps[:, ::-1], ((0, 0), (112, WIN - 112 - KSIZE)))
        qkv, ctx_rows, lq, lk, sm, mix, k2, z, p, l1, l3, wall = attn_fwd(lengths, tokens, wt, taps, out_weight, up_weight, down_weight, mp)
        first = me * rows
        x_rows = lax.dynamic_slice_in_dim(tokens, first, rows, 1)
        cot_rows = lax.dynamic_slice_in_dim(cotangent, first, rows, 1)
        pos = jnp.reshape(first, (1,)).astype(jnp.int32)
        out_rows, gmix, gctx, gw, small = ffn(
            lengths, pos, x_rows, cot_rows, ctx_rows, wall,
            norm1_gain[None], norm1_bias[None], norm2_gain[None], norm2_bias[None],
        )
        output = lax.all_gather(out_rows, "mp", axis=1, tiled=True)
        gctx_heads = lax.all_to_all(gctx, "mp", 0, 0, tiled=True)
        gw = lax.psum_scatter(gw, "mp", scatter_dimension=0, tiled=False)
        gw = lax.psum(gw, "dp").astype(F32)
        gqkv, ipart, gtaps = attn_bwd(lengths, tokens, wt, taps, rtaps, qkv, gctx_heads, lq, lk, sm, mix, k2, z, p, l1, l3)
        ipart = lax.psum_scatter(ipart, "mp", scatter_dimension=1, tiled=True).astype(F32)
        input_grad = lax.all_gather((gmix + ipart).astype(BF), "mp", axis=1, tiled=True)
        gqkv = lax.psum(gqkv.astype(BF), "dp").astype(F32)
        gqkv = jnp.transpose(gqkv.reshape(3, width, dim), (0, 2, 1))
        small = lax.psum(small, ("dp", "mp"))
        gtaps = lax.psum(gtaps, "dp")
        gtaps = lax.slice_in_dim(gtaps, 367, 367 + KSIZE, axis=1)
        return (
            output, input_grad, gqkv, gw[:, :OW_ROWS].reshape(width, dim), gtaps, small[0], small[1], small[2], small[3],
            gw[:, OW_ROWS:CUT].reshape(dim, ff), gw[:, CUT:].reshape(ff, dim),
        )
    return body


def solution(mesh):
    return jax.shard_map(
        body_factory(mesh.shape["dp"], mesh.shape["mp"]),
        mesh=mesh,
        in_specs=(
            P("dp", None, None), P("dp"), P(None, None, "mp"), P("mp", None), P("mp", None),
            P(), P(), P(), P(), P(None, "mp"), P("mp", None), P("dp", None, None),
        ),
        out_specs=(
            P("dp", None, None), P("dp", None, None), P(None, None, "mp"), P("mp", None), P("mp", None),
            P(), P(), P(), P(), P(None, "mp"), P("mp", None),
        ),
        check_vma=False,
    )
```

```python
import functools
import jax
import jax.numpy as jnp
import numpy as np
from jax import lax
from jax.experimental import pallas as pl
from jax.experimental.pallas import tpu as pltpu
from jax.sharding import PartitionSpec as P

HD = 64
LM = 64
KSIZE = 33
HALF = 16
NS_ITERS = 6
EPS = 1e-5
HI = lax.Precision.HIGHEST
BF = jnp.bfloat16
F32 = jnp.float32
SCALE = HD ** -0.5
WIN = 512
BLK = 256


def nn(a, b, precision=None):
    return lax.dot_general(a, b, (((1,), (0,)), ((), ())), precision=precision, preferred_element_type=F32)


def nt(a, b, precision=None):
    return lax.dot_general(a, b, (((1,), (1,)), ((), ())), precision=precision, preferred_element_type=F32)


def tn(a, b, precision=None):
    return lax.dot_general(a, b, (((0,), (0,)), ((), ())), precision=precision, preferred_element_type=F32)


def block_mask(width):
    r = lax.broadcasted_iota(jnp.int32, (width, width), 0) // HD
    c = lax.broadcasted_iota(jnp.int32, (width, width), 1) // HD
    return r == c


def spread(x, heads, mask):
    return jnp.where(mask, jnp.concatenate([x] * heads, axis=0), 0.0)


def members(length, first, count):
    s = lax.broadcasted_iota(jnp.int32, (LM, count), 1) + first
    j = lax.broadcasted_iota(jnp.int32, (LM, count), 0)
    s64 = s * LM
    return (j * length <= s64) & (s64 < (j + 1) * length) & (s < length)


def live_lanes(length, first, count):
    s = lax.broadcasted_iota(jnp.int32, (1, count), 1) + first
    return s < length


def toeplitz(row):
    full = jnp.broadcast_to(row, (BLK, WIN))
    return pltpu.roll(full, 0, 1, stride=1, stride_axis=0)


def windows(x, seq):
    rows = x.shape[0]
    pad = jnp.zeros((rows, 128), x.dtype)
    padded = jnp.concatenate([pad, x, pad], axis=1)
    return [padded[:, b * BLK : b * BLK + WIN] for b in range(seq // BLK)]


def hi_lo(x):
    hi = x.astype(BF)
    return hi, (x - hi.astype(F32)).astype(BF)


def banded(x, row, heads, seq):
    outs = []
    nblk = seq // BLK
    for h in range(heads):
        wins = jnp.concatenate(windows(x[h * HD : (h + 1) * HD], seq), axis=0)
        hi, lo = hi_lo(toeplitz(row[h : h + 1]))
        y = nt(wins, hi) + nt(wins, lo)
        outs.append(jnp.concatenate([y[b * HD : (b + 1) * HD] for b in range(nblk)], axis=1))
    return jnp.concatenate(outs, axis=0)


MESH = pl.DeviceIdType.MESH


def flip(i, bit):
    return i + bit * (1 - 2 * ((i // bit) % 2))


def partner(i, m):
    for bit in (1, 2, 4):
        if m & bit:
            i = flip(i, bit)
    return i


def greet(peers):
    bar = pltpu.get_barrier_semaphore()
    for p in peers:
        pl.semaphore_signal(bar, inc=1, device_id=p, device_id_type=MESH)
    pl.semaphore_wait(bar, len(peers))


def rcopy(src, dst, ss, rs, dev):
    return pltpu.make_async_remote_copy(src_ref=src, dst_ref=dst, send_sem=ss, recv_sem=rs, device_id=dev, device_id_type=MESH)


SLOTS = 8
OW_ROWS, UP_ROWS, DN_ROWS = 24, 96, 96
SLICE = OW_ROWS + UP_ROWS + DN_ROWS
CUT = OW_ROWS + UP_ROWS
PARTS = ((0, OW_ROWS), (OW_ROWS, UP_ROWS), (CUT, DN_ROWS))
TAP0 = 112


class Net:
    def __init__(self, ssem, rsem):
        self.ssem, self.rsem, self.n = ssem, rsem, 0
        self.sent = []

    def copy(self, src, dst, dev, late=True):
        i = self.n
        self.n += 1
        c = rcopy(src, dst, self.ssem.at[i], self.rsem.at[i], dev)
        if late:
            self.sent.append(c)
        return c

    def drain(self):
        for c in self.sent:
            c.wait_send()
        self.sent = []


def place_taps(ref, scratch, reverse=False):
    scratch[...] = jnp.zeros_like(scratch)
    scratch[:, TAP0 : TAP0 + KSIZE] = ref[...]
    return scratch[...]


class Gather:
    def __init__(self, mp, srcs, wall, net):
        z, d = lax.axis_index("mp"), lax.axis_index("dp")
        r = lax.rem(d, SLOTS)
        self.ms = range(1, mp)
        self.zc, self.yc, self.xc, self.yxc, self.xyc, self.cc = {}, {}, {}, {}, {}, {}
        for m in self.ms:
            w = wall.at[m - 1]
            dev = {"mp": partner(z, m)}
            self.zc[m] = [net.copy(srcs[i].at[r], w.at[r, pl.ds(*PARTS[i])], dev) for i in range(3)]
            r4, r2, r6 = flip(r, 4), flip(r, 2), partner(r, 6)
            dy, dx, dc = {"dp": flip(d, 4)}, {"dp": flip(d, 2)}, {"dp": flip(d, 1)}
            self.yc[m] = net.copy(w.at[r], w.at[r], dy)
            self.xc[m] = net.copy(w.at[r], w.at[r], dx)
            s = w.at[r4, pl.ds(0, CUT)]
            self.yxc[m] = net.copy(s, s, dx)
            s = w.at[r2, pl.ds(CUT, DN_ROWS)]
            self.xyc[m] = net.copy(s, s, dy)
            self.cc[m] = [net.copy(w.at[q], w.at[q], dc) for q in (r, r4, r2, r6)]

    def start(self):
        for m in self.ms:
            for c in self.zc[m]:
                c.start()

    def step1(self, m):
        for c in self.zc[m]:
            c.wait_recv()
        self.yc[m].start()
        self.xc[m].start()
        self.cc[m][0].start()

    def step2(self, m):
        self.yc[m].wait_recv()
        self.yxc[m].start()
        self.cc[m][1].start()
        self.xc[m].wait_recv()
        self.xyc[m].start()
        self.cc[m][2].start()

    def step3(self, m):
        self.yxc[m].wait_recv()
        self.xyc[m].wait_recv()
        self.cc[m][3].start()

    def finish(self):
        for m in self.ms:
            for c in self.cc[m]:
                c.wait_recv()


def attn_fwd_kernel(docs, heads, seq, dest, len_ref, x_ref, wt_ref, taps_ref, ow_ref, up_ref, dn_ref, qkv_ref, ctx_ref, lq_ref, lk_ref, sum_ref, mix_ref, k2_ref, z_ref, p_ref, l1_ref, l3_ref, wall_ref,
                    ctx_s, taps_s, ssem, rsem):
    width = heads * HD
    me = lax.axis_index("mp")
    dd = lax.axis_index("dp")
    greet([{"mp": partner(me, m)} for m in range(1, dest)] + [{"dp": flip(dd, b)} for b in (1, 2, 4)])
    net = Net(ssem, rsem)
    gather = Gather(dest, (ow_ref, up_ref, dn_ref), wall_ref, net)
    gather.start()

    acs = {(m, d): net.copy(ctx_s.at[partner(me, m), d], ctx_ref.at[m, d], {"mp": partner(me, m)}) for d in range(docs) for m in range(1, dest)}
    taps = place_taps(taps_ref, taps_s)
    mask = block_mask(width)
    eye = jnp.where(
        lax.broadcasted_iota(jnp.int32, (width, width), 0) == lax.broadcasted_iota(jnp.int32, (width, width), 1), 1.0, 0.0
    ).astype(F32)
    for d in range(docs):
        for c in range(seq // BLK):
            xc = x_ref[d, c * BLK : (c + 1) * BLK, :]
            qkv_ref[d, :, c * BLK : (c + 1) * BLK] = nt(wt_ref[...], xc).astype(BF)
    gather.step1(1)
    k2s = []
    for d in range(docs):
        if d == 1:
            gather.step1(2)
        length = len_ref[d]
        memb = jnp.where(members(length, 0, seq), 1.0, 0.0).astype(F32)
        counts = jnp.maximum(jnp.sum(memb, axis=1, keepdims=True), 1.0)
        memb_b = memb.astype(BF)
        q = qkv_ref[d, 0:width, :]
        k = qkv_ref[d, width : 2 * width, :]
        v = qkv_ref[d, 2 * width : 3 * width, :]
        lq = spread(nt(memb_b, q) / counts, heads, mask).astype(BF)
        lk = spread(nt(memb_b, k) / counts, heads, mask).astype(BF)
        lq_ref[d] = lq
        lk_ref[d] = lk
        s2 = jnp.where(mask, nt(lq, lk) * SCALE, -1e30)
        e2 = jnp.where(mask, jnp.exp(s2 - jnp.max(s2, axis=1, keepdims=True)), 0.0)
        k2 = e2 / jnp.sum(e2, axis=1, keepdims=True)
        k2_ref[d] = k2
        k2s.append(k2)
        s3 = jnp.where(live_lanes(length, 0, seq), nn(lq, k) * SCALE, -1e30)
        m3 = jnp.max(s3, axis=1, keepdims=True)
        e3 = jnp.exp(s3 - m3)
        t3 = jnp.sum(e3, axis=1, keepdims=True)
        l3_ref[d] = jnp.broadcast_to(m3 + jnp.log(t3), (width, 128))
        k3 = (e3 / t3).astype(BF)
        sum_ref[d] = jnp.where(mask, nt(k3, v), 0.0)
    zs = []
    for d in range(docs):
        rows = jnp.sum(k2s[d] * k2s[d], axis=1, keepdims=True)
        tot = jnp.sum(rows.reshape(heads, HD, 1), axis=1, keepdims=True)
        tot = jnp.broadcast_to(tot, (heads, HD, 1)).reshape(width, 1)
        z = k2s[d].T / tot
        z_ref[d, 0] = z
        zs.append(z)
    for i in range(NS_ITERS):
        ps = [nn(k2s[d], zs[d], HI) for d in range(docs)]
        bs = [15.0 * eye - nn(ps[d], 7.0 * eye - ps[d], HI) for d in range(docs)]
        cs = [13.0 * eye - nn(ps[d], bs[d], HI) for d in range(docs)]
        zs = [0.25 * nn(zs[d], cs[d], HI) for d in range(docs)]
        for d in range(docs):
            p_ref[d, i, 0] = ps[d]
            p_ref[d, i, 1] = bs[d]
            p_ref[d, i, 2] = cs[d]
            z_ref[d, i + 1] = zs[d]
        if i == 2:
            gather.step1(3)
        if i == 4:
            gather.step2(1)
    for d in range(docs):
        length = len_ref[d]
        q = qkv_ref[d, 0:width, :]
        v = qkv_ref[d, 2 * width : 3 * width, :]
        live = live_lanes(length, 0, seq)
        mix = jnp.where(mask, nn(zs[d], sum_ref[d], HI), 0.0)
        mix_ref[d] = mix.astype(BF)
        mix_t = mix.T.astype(BF)
        s1 = (nn(lk_ref[d], q) * SCALE).reshape(heads, LM, seq)
        m1 = jnp.max(s1, axis=1, keepdims=True)
        e1 = jnp.exp(s1 - m1)
        t1 = jnp.sum(e1, axis=1, keepdims=True)
        l1_ref[d] = (m1 + jnp.log(t1)).reshape(heads, seq)
        k1 = (e1 / t1).reshape(width, seq).astype(BF)
        vl = jnp.where(live, v, 0).astype(BF)
        ctx = nn(mix_t, k1) + banded(vl, taps, heads, seq)
        ctx = jnp.where(live, ctx, 0.0).astype(BF)
        part = seq // dest
        for i in range(dest):
            ctx_s[i, d] = ctx[:, i * part : (i + 1) * part]
        for m in range(1, dest):
            acs[m, d].start()
        ctx_ref[0, d] = ctx_s[me, d]
        if d == 0:
            gather.step2(2)
    gather.step3(1)
    gather.step2(3)
    gather.step3(2)
    gather.step3(3)
    gather.finish()
    for d in range(docs):
        for m in range(1, dest):
            acs[m, d].wait_recv()
    net.drain()


def attn_fwd(lengths, x, wt, taps, ow, up, dn, dest):
    docs, seq, dim = x.shape
    width = wt.shape[0] // 3
    heads = width // HD
    vm = pl.BlockSpec(memory_space=pltpu.VMEM)
    out = [
        jax.ShapeDtypeStruct((docs, 3 * width, seq), BF),
        jax.ShapeDtypeStruct((dest, docs, width, seq // dest), BF),
        jax.ShapeDtypeStruct((docs, width, width), BF),
        jax.ShapeDtypeStruct((docs, width, width), BF),
        jax.ShapeDtypeStruct((docs, width, width), F32),
        jax.ShapeDtypeStruct((docs, width, width), BF),
        jax.ShapeDtypeStruct((docs, width, width), F32),
        jax.ShapeDtypeStruct((docs, NS_ITERS + 1, width, width), F32),
        jax.ShapeDtypeStruct((docs, NS_ITERS, 3, width, width), F32),
        jax.ShapeDtypeStruct((docs, heads, seq), F32),
        jax.ShapeDtypeStruct((docs, width, 128), F32),
        jax.ShapeDtypeStruct((dest - 1, SLOTS, SLICE, dim), BF),
    ]
    any_ = pl.BlockSpec(memory_space=pl.ANY)
    dma = pltpu.SemaphoreType.DMA
    return pl.pallas_call(
        functools.partial(attn_fwd_kernel, docs, heads, seq, dest),
        out_shape=out,
        in_specs=[pl.BlockSpec(memory_space=pltpu.SMEM), vm, vm, vm, any_, any_, any_],
        out_specs=[vm] * (len(out) - 1) + [any_],
        scratch_shapes=[
            pltpu.VMEM((dest, docs, width, seq // dest), BF),
            pltpu.VMEM((heads, WIN), F32),
            dma((64,)),
            dma((64,)),
        ],
        compiler_params=pltpu.CompilerParams(vmem_limit_bytes=60 * 2**20, collective_id=0, has_side_effects=True),
        cost_estimate=pl.CostEstimate(flops=int(8e9), bytes_accessed=int(3e7), transcendentals=0),
        name="attn_fwd",
    )(lengths, x, wt, taps, ow, up, dn)


def ln_stats(v):
    mu = jnp.mean(v, axis=-1, keepdims=True)
    cen = v - mu
    var = jnp.mean(cen * cen, axis=-1, keepdims=True)
    r = lax.rsqrt(var + EPS)
    return cen * r, r


def ln_back(g, xhat, r):
    m1 = jnp.mean(g, axis=-1, keepdims=True)
    m2 = jnp.mean(g * xhat, axis=-1, keepdims=True)
    return r * (g - m1 - xhat * m2)


ROOT_HALF = 0.7071067811865476
INV_ROOT_2PI = 0.3989422804014327


def ffn_kernel(groups, docs, rows, len_ref, x_hbm, cot_hbm, ctx_ref, ow_hbm, up_hbm, dn_hbm, wall_hbm, g1_ref, b1_ref, g2_ref, b2_ref,
               out_ref, gmix_ref, gctx_ref, s1_ref, small_ref, x_s, cot_s, w_s, rc_s, gc_s, nb_s, fac_s, act_s, br_s, x1_s, gn_s, lsem, ssem, rsem):
    n = docs * rows
    dim = x_s.shape[-1]
    z, dd = lax.axis_index("mp"), lax.axis_index("dp")
    kk = lax.rem(dd, 2)
    loads = []
    for d in range(docs):
        loads.append(pltpu.make_async_copy(x_hbm.at[d, pl.ds(pl.multiple_of(z * rows, rows), rows)], x_s.at[pl.ds(d * rows, rows)], lsem.at[d]))
        loads.append(pltpu.make_async_copy(cot_hbm.at[d, pl.ds(pl.multiple_of(z * rows, rows), rows)], cot_s.at[pl.ds(d * rows, rows)], lsem.at[docs + d]))
    own = [pltpu.make_async_copy(src, w_s.at[0, :, :, pl.ds(*PARTS[i])], lsem.at[2 * docs + i]) for i, src in enumerate((ow_hbm, up_hbm, dn_hbm))]
    walls = [pltpu.make_async_copy(wall_hbm.at[m - 1], w_s.at[m], lsem.at[2 * docs + 2 + m]) for m in range(1, groups)]
    for c in own + walls + loads:
        c.start()
    greet([{"mp": partner(z, m)} for m in range(1, groups)] + [{"dp": flip(dd, 1)}])
    net = Net(ssem, rsem)
    dc = {"dp": flip(dd, 1)}
    ccs = {}
    for g in range(groups):
        for part, (lo, size) in enumerate(((OW_ROWS, SLICE - OW_ROWS), (0, OW_ROWS))):
            ccs[g, part] = net.copy(w_s.at[g, :, 1 - kk, pl.ds(lo, size)], rc_s.at[g, :, pl.ds(lo, size)], dc)
    gcs = {m: net.copy(gc_s.at[m - 1], gctx_ref.at[z], {"mp": partner(z, m)}) for m in range(1, groups)}

    def take(g, part):
        lo, size = PARTS[part]
        return w_s[g, :, :, lo : lo + size, :].reshape(SLOTS * size, dim)

    def put(g, part, val):
        lo, size = PARTS[part]
        w_s[g, :, :, lo : lo + size, :] = val.astype(BF).reshape(SLOTS // 2, 2, size, dim)

    first = z * rows
    live = jnp.concatenate([(lax.broadcasted_iota(jnp.int32, (rows, 1), 0) + first < len_ref[d]).astype(F32) for d in range(docs)], axis=0)
    gain1, bias1 = g1_ref[...].reshape(1, dim), b1_ref[...].reshape(1, dim)
    gain2, bias2 = g2_ref[...].reshape(1, dim), b2_ref[...].reshape(1, dim)
    for c in own + walls + loads:
        c.wait()
    parts = []
    for d in range(docs):
        acc = None
        for g in range(groups):
            t = tn(ctx_ref[g, d], take(g, 0)).astype(BF).astype(F32)
            acc = t if acc is None else acc + t
        parts.append(acc)
    mixed = x_s[...].astype(F32) + jnp.concatenate(parts, axis=0)
    xh1, r1 = ln_stats(mixed)
    x1_s[...] = xh1
    normed = xh1 * gain1 + bias1
    nb_s[...] = normed.astype(BF)
    br_s[...] = normed

    def fwd_group(g, _):
        h = nn(nb_s[...], take(g, 1))
        phi_big = 0.5 * (1.0 + lax.erf(h * ROOT_HALF))
        act = (h * phi_big).astype(BF)
        act_s[g] = act
        fac_s[g] = phi_big + h * (jnp.exp(-0.5 * h * h) * INV_ROOT_2PI)
        br_s[...] += nn(act, take(g, 2)).astype(BF).astype(F32)
        return 0

    lax.fori_loop(0, groups, fwd_group, 0)
    xh2, r2 = ln_stats(br_s[...])
    out_ref[...] = (live * (xh2 * gain2 + bias2)).astype(BF).reshape(docs, rows, dim)
    g_out = live * cot_s[...].astype(F32)
    gg2 = jnp.sum(g_out * xh2, axis=0, keepdims=True)
    gb2 = jnp.sum(g_out, axis=0, keepdims=True)
    g_res = ln_back(g_out * gain2, xh2, r2)
    gn_s[...] = g_res
    br_s[...] = g_res
    gbr_s = x_s
    gbr_s[...] = g_res.astype(BF)

    def bwd_group(g):
        gbr = gbr_s[...]
        g_pre = (nt(gbr, take(g, 2)) * fac_s[g]).astype(BF)
        put(g, 2, tn(act_s[g], gbr))
        gn_s[...] += nt(g_pre, take(g, 1))
        put(g, 1, tn(nb_s[...], g_pre))

    for g in range(groups):
        bwd_group(g)
        ccs[g, 0].start()
    g_n = gn_s[...]
    xh1 = x1_s[...]
    gg1 = jnp.sum(g_n * xh1, axis=0, keepdims=True)
    gb1 = jnp.sum(g_n, axis=0, keepdims=True)
    small_ref[...] = jnp.concatenate([gg1, gb1, gg2, gb2, jnp.zeros((4, dim), F32)], axis=0)
    g_mix = ln_back(g_n * gain1, xh1, r1)
    gmix_ref[...] = g_mix.reshape(docs, rows, dim)
    g_att = g_mix.astype(BF)
    for m in (3, 2, 1, 0) if groups == 4 else reversed(range(groups)):
        t = nt(take(m, 0), g_att).astype(BF)
        for d in range(docs):
            if m:
                gc_s[m - 1, d] = t[:, d * rows : (d + 1) * rows]
            else:
                gctx_ref[z, d] = t[:, d * rows : (d + 1) * rows]
        if m:
            gcs[m].start()
    for g in range(groups):
        acc = None
        for d in range(docs):
            t = nn(ctx_ref[g, d], g_att[d * rows : (d + 1) * rows])
            acc = t if acc is None else acc + t
        put(g, 0, acc)
        ccs[g, 1].start()
    for g in range(groups):
        ccs[g, 0].wait_recv()
        ccs[g, 1].wait_recv()
        for j in range(SLOTS // 2):
            s1_ref[g, j // 2, j % 2] = (w_s[g, j, kk].astype(F32) + rc_s[g, j].astype(F32)).astype(BF)
    for m in range(1, groups):
        gcs[m].wait_recv()
    net.drain()


def ffn(lengths, x, cot, ctx, ow, up, dn, wall, g1, b1, g2, b2):
    docs, seq, dim = x.shape
    groups, _, width, rows = ctx.shape
    ff = SLOTS * UP_ROWS
    n = docs * rows
    vm = pl.BlockSpec(memory_space=pltpu.VMEM)
    any_ = pl.BlockSpec(memory_space=pl.ANY)
    sm = pl.BlockSpec(memory_space=pltpu.SMEM)
    dma = pltpu.SemaphoreType.DMA
    out = [
        jax.ShapeDtypeStruct((docs, rows, dim), BF),
        jax.ShapeDtypeStruct((docs, rows, dim), F32),
        jax.ShapeDtypeStruct((groups, docs, width, rows), BF),
        jax.ShapeDtypeStruct((groups, 2, 2, SLICE, dim), BF),
        jax.ShapeDtypeStruct((8, dim), F32),
    ]
    wall = wall.reshape(groups - 1, SLOTS // 2, 2, SLICE, dim)
    ow, up, dn = (t.reshape(SLOTS // 2, 2, -1, dim) for t in (ow, up, dn))
    return pl.pallas_call(
        functools.partial(ffn_kernel, groups, docs, rows),
        out_shape=out,
        in_specs=[sm, any_, any_, vm, any_, any_, any_, any_, vm, vm, vm, vm],
        out_specs=[vm] * len(out),
        scratch_shapes=[
            pltpu.VMEM((n, dim), BF),
            pltpu.VMEM((n, dim), BF),
            pltpu.VMEM((groups, SLOTS // 2, 2, SLICE, dim), BF),
            pltpu.VMEM((groups, SLOTS // 2, SLICE, dim), BF),
            pltpu.VMEM((groups - 1, docs, width, rows), BF),
            pltpu.VMEM((n, dim), BF),
            pltpu.VMEM((groups, n, ff), F32),
            pltpu.VMEM((groups, n, ff), BF),
            pltpu.VMEM((n, dim), F32),
            pltpu.VMEM((n, dim), F32),
            pltpu.VMEM((n, dim), F32),
            dma((2 * docs + 2 + groups,)),
            dma((16,)),
            dma((16,)),
        ],
        compiler_params=pltpu.CompilerParams(vmem_limit_bytes=62 * 2**20, collective_id=1, has_side_effects=True),
        cost_estimate=pl.CostEstimate(flops=int(1.8e10), bytes_accessed=int(4e7), transcendentals=0),
        name="ffn",
    )(lengths, x, cot, ctx, ow, up, dn, wall, g1, b1, g2, b2)


def attn_bwd_kernel(docs, heads, seq, parts, dp, len_ref, x_ref, wt_ref, taps_ref, qkv_ref, gctx_ref, lq_ref, lk_ref, sum_ref, mix_ref, k2_ref,
                    z_ref, p_ref, l1_ref, l3_ref, s1_ref, small_in, gmix_ref, gq_ref, ig_ref, taps_out, gw_ref, small_ref,
                    g_s, ginv_s, glq_s, glk_s, taps_s, ipart_ref, gqkv_ref, ri_s, ra1, rb1, ra2, rb2, rz, fin_s, rfin, rq0, rq1, rq2, gqb, q_s, rsm, gt_s, rtp, ssem, rsem):
    width = heads * HD
    dim = x_ref.shape[-1]
    nd = net_setup(docs, seq, parts, dp, s1_ref, small_in, gq_ref, ig_ref, taps_out, gw_ref, small_ref, ipart_ref, gqkv_ref, ri_s, ra1, rb1, ra2, rb2, rz, fin_s, rfin, rq0, rq1, rq2, gqb, q_s, rsm, gt_s, rtp, ssem, rsem)
    zi = lax.axis_index("mp")
    nd.begin()
    rtaps = place_taps(taps_ref, taps_s)
    nblk = seq // BLK
    mask = block_mask(width)
    anti = jnp.where(
        lax.broadcasted_iota(jnp.int32, (BLK, BLK), 0) + lax.broadcasted_iota(jnp.int32, (BLK, BLK), 1) == BLK - 1, 1.0, 0.0
    ).astype(BF)
    gaccs = [None] * heads
    for d in range(docs):
        length = len_ref[d]
        live = live_lanes(length, 0, seq)
        q = qkv_ref[d, 0:width, :]
        k = qkv_ref[d, width : 2 * width, :]
        v = qkv_ref[d, 2 * width : 3 * width, :]
        gc = jnp.concatenate([gctx_ref[i, d] for i in range(parts)], axis=1)
        gc = jnp.where(live, gc, 0).astype(BF)
        lq, lk = lq_ref[d], lk_ref[d]
        s1 = (nn(lk, q) * SCALE).reshape(heads, LM, seq)
        k1 = jnp.exp(s1 - l1_ref[d].reshape(heads, 1, seq))
        gmixing = jnp.where(mask, nt(k1.reshape(width, seq).astype(BF), gc), 0.0)
        gk1 = nn(mix_ref[d], gc).reshape(heads, LM, seq)
        gs1 = (k1 * (gk1 - jnp.sum(gk1 * k1, axis=1, keepdims=True))).reshape(width, seq).astype(BF)
        ginv_s[d] = nt(gmixing, sum_ref[d], HI)
        gsum = tn(z_ref[d, NS_ITERS], gmixing, HI)
        gsum = jnp.where(mask, gsum, 0.0)
        gsum_b = gsum.astype(BF)
        s3 = jnp.where(live, nn(lq, k) * SCALE, -1e30)
        k3 = jnp.exp(s3 - l3_ref[d][:, 0:1])
        gk3 = nn(gsum_b, v)
        gs3 = (k3 * (gk3 - jnp.sum(gk3 * k3, axis=1, keepdims=True))).astype(BF)
        glq_s[d] = jnp.where(mask, nt(gs3, k), 0.0) * SCALE
        glk_s[d] = jnp.where(mask, nt(gs1, q), 0.0) * SCALE
        lq_t = lq.astype(F32).T.astype(BF)
        lk_t = lk.astype(F32).T.astype(BF)
        g_s[d, 0:width, :] = nn(lk_t, gs1) * SCALE
        g_s[d, width : 2 * width, :] = nn(lq_t, gs3) * SCALE
        gv = nn(gsum.T.astype(BF), k3.astype(BF))
        gvl = banded(gc, rtaps, heads, seq)
        g_s[d, 2 * width : 3 * width, :] = gv + jnp.where(live, gvl, 0.0)
        vl = jnp.where(live, v, 0).astype(BF)
        for h in range(heads):
            wins = jnp.concatenate(windows(vl[h * HD : (h + 1) * HD], seq), axis=0)
            gch = gc[h * HD : (h + 1) * HD]
            stack = jnp.concatenate([gch[:, b * BLK : (b + 1) * BLK] for b in range(nblk)], axis=0)
            rev = nt(anti, stack).astype(BF)
            t = nn(rev, wins)
            gaccs[h] = t if gaccs[h] is None else gaccs[h] + t
    for h in range(heads):
        rolled = pltpu.roll(gaccs[h], 0, 1, stride=1, stride_axis=0)
        gt_s[h : h + 1, :] = jnp.sum(rolled, axis=0, keepdims=True)
    gz = [ginv_s[d] for d in range(docs)]
    gk = [jnp.zeros((width, width), F32) for _ in range(docs)]
    eye = jnp.where(
        lax.broadcasted_iota(jnp.int32, (width, width), 0) == lax.broadcasted_iota(jnp.int32, (width, width), 1), 1.0, 0.0
    ).astype(F32)
    for i in reversed(range(NS_ITERS)):
        if i < NS_ITERS - 1:
            nd.small_step()
        for d in range(docs):
            z, p, b, c = z_ref[d, i], p_ref[d, i, 0], p_ref[d, i, 1], p_ref[d, i, 2]
            a = 7.0 * eye - p
            g = 0.25 * gz[d]
            gc_ = tn(z, g, HI)
            gzn = nt(g, c, HI)
            gp = -nt(gc_, b, HI)
            gb = -tn(p, gc_, HI)
            gp = gp - nt(gb, a, HI)
            ga = -tn(p, gb, HI)
            gp = gp - ga
            gk[d] = gk[d] + nt(gp, z, HI)
            gz[d] = gzn + tn(k2_ref[d], gp, HI)
    nd.g_step1()
    for d in range(docs):
        length = len_ref[d]
        k2 = k2_ref[d]
        rows = jnp.sum(k2 * k2, axis=1, keepdims=True)
        tot = jnp.sum(rows.reshape(heads, HD, 1), axis=1, keepdims=True)
        tot = jnp.broadcast_to(tot, (heads, HD, 1)).reshape(width, 1)
        g = gz[d]
        dot = jnp.sum(g * k2.T, axis=1, keepdims=True)
        dot = jnp.sum(dot.reshape(heads, HD, 1), axis=1, keepdims=True)
        dot = jnp.broadcast_to(dot, (heads, HD, 1)).reshape(width, 1)
        gk2 = gk[d] + (g / tot).T - k2 * (2.0 * dot / (tot * tot))
        gs2 = k2 * (gk2 - jnp.sum(gk2 * k2, axis=1, keepdims=True)) * SCALE
        memb = jnp.where(members(length, 0, seq), 1.0, 0.0).astype(F32)
        counts = jnp.maximum(jnp.sum(memb, axis=1, keepdims=True), 1.0)
        counts = jnp.concatenate([counts] * heads, axis=0)
        memb3 = jnp.concatenate([memb.astype(BF)] * heads, axis=0)
        glq = (glq_s[d] + nn(gs2, lk_ref[d].astype(F32), HI)) / counts
        glk = (glk_s[d] + tn(gs2, lq_ref[d].astype(F32), HI)) / counts
        hi, lo = hi_lo(glq.T)
        gq = g_s[d, 0:width, :] + nn(hi, memb3) + nn(lo, memb3)
        hi, lo = hi_lo(glk.T)
        gkk = g_s[d, width : 2 * width, :] + nn(hi, memb3) + nn(lo, memb3)
        g_all = jnp.concatenate([gq, gkk, g_s[d, 2 * width : 3 * width, :]], axis=0).astype(BF)
        gw = nn(g_all, x_ref[d])
        if d == 0:
            gqkv_ref[...] = gw
        else:
            gqkv_ref[...] += gw
        for c in range(nblk):
            t = tn(g_all[:, c * BLK : (c + 1) * BLK], wt_ref[...])
            ipart_ref[d, c] = (t + jnp.where(zi == c, 1.0, 0.0) * gmix_ref[d]).astype(BF)
    nd.tail()


class net_setup:
    def __init__(self, docs, seq, parts, dp, s1, small_in, gq, ig, taps_out, gw, small, ipart, gqkv, ri, ra1, rb1, ra2, rb2, rz, fin, rfin, rq0, rq1, rq2, gqb, q, rsm, gt, rtp, ssem, rsem):
        self.__dict__.update({k: v for k, v in locals().items() if k != "self"})
        self.z, self.d = lax.axis_index("mp"), lax.axis_index("dp")
        self.r = lax.rem(self.d, SLOTS)
        self.y, self.x, self.k = self.r // 4, lax.rem(self.r // 2, 2), lax.rem(self.r, 2)
        self.net = Net(ssem, rsem)
        self.extra = [b for b in (8, 16, 32, 64, 128) if b < dp]
        self.low = (1, 2, 4)
        self.bits = list(self.low) + self.extra

    def dev(self, bit):
        return {"dp": flip(self.d, bit)}

    def zdev(self, m):
        return {"mp": partner(self.z, m)}

    def begin(self):
        greet([self.zdev(m) for m in range(1, self.parts)] + [self.dev(b) for b in self.bits])
        c = self.net.copy
        self.a1 = c(self.s1.at[:, 1 - self.y, :, pl.ds(0, CUT)], self.ra1, self.dev(4))
        self.b1 = c(self.s1.at[:, :, 1 - self.x, pl.ds(CUT, DN_ROWS)], self.rb1, self.dev(2))
        self.a1.start()
        self.b1.start()
        self.small[...] = self.small_in[...]
        self.smalls = self.chain(self.small, self.rsm, [self.dev(b) for b in self.bits] + [self.zdev(1 << j) for j in range(self.parts.bit_length() - 1)])
        self.small_step()

    def double(self, buf, recv, bit_dev):
        c = self.net.copy(buf, recv, bit_dev, late=False)
        c.start()
        c.wait()
        buf[...] = (buf[...].astype(F32) + recv[...].astype(F32)).astype(buf.dtype)

    def chain(self, buf, recv, devs):
        for i, dev in enumerate(devs):
            c = self.net.copy(buf, recv.at[i], dev, late=False)
            c.start()
            yield
            c.wait()
            buf[...] = buf[...] + recv[i]
        while True:
            yield

    def small_step(self):
        next(self.smalls)

    def g_step1(self):
        c = self.net.copy
        self.a1.wait_recv()
        self.b1.wait_recv()
        for g in range(self.parts):
            for j in range(2):
                self.ra1[g, j] = (self.ra1[g, j].astype(F32) + self.s1[g, self.y, j, 0:CUT].astype(F32)).astype(BF)
                self.rb1[g, j] = (self.rb1[g, j].astype(F32) + self.s1[g, j, self.x, CUT:SLICE].astype(F32)).astype(BF)
        self.a2 = c(self.ra1.at[:, 1 - self.x], self.ra2, self.dev(2))
        self.b2 = c(self.rb1.at[:, 1 - self.y], self.rb2, self.dev(4))
        self.a2.start()
        self.b2.start()

    def g_step2(self):
        c = self.net.copy
        self.a2.wait_recv()
        self.b2.wait_recv()
        for g in range(self.parts):
            self.ra2[g] = (self.ra2[g].astype(F32) + self.ra1[g, self.x].astype(F32)).astype(BF)
            self.rb2[g] = (self.rb2[g].astype(F32) + self.rb1[g, self.y].astype(F32)).astype(BF)
        self.zs = []
        for m in range(1, self.parts):
            self.zs.append(c(self.ra2.at[m], self.rz.at[m - 1, pl.ds(0, CUT)], self.zdev(m)))
            self.zs.append(c(self.rb2.at[m], self.rz.at[m - 1, pl.ds(CUT, DN_ROWS)], self.zdev(m)))
        for s in self.zs:
            s.start()

    def g_step3(self):
        c = self.net.copy
        for s in self.zs:
            s.wait_recv()
        top, bot = self.ra2[0].astype(F32), self.rb2[0].astype(F32)
        for m in range(1, self.parts):
            top = top + self.rz[m - 1, 0:CUT].astype(F32)
            bot = bot + self.rz[m - 1, CUT:SLICE].astype(F32)
        self.fin[0:CUT] = top.astype(BF)
        self.fin[CUT:SLICE] = bot.astype(BF)
        for i, b in enumerate(self.extra):
            self.double(self.fin, self.rfin.at[i], self.dev(b))
        r, gw = self.r, self.gw
        gw[r] = self.fin[...]
        r4, r2, r6 = flip(r, 4), flip(r, 2), partner(r, 6)
        self.gy = c(gw.at[r], gw.at[r], self.dev(4))
        self.gx = c(gw.at[r], gw.at[r], self.dev(2))
        self.gyx = c(gw.at[r4, pl.ds(0, CUT)], gw.at[r4, pl.ds(0, CUT)], self.dev(2))
        self.gxy = c(gw.at[r2, pl.ds(CUT, DN_ROWS)], gw.at[r2, pl.ds(CUT, DN_ROWS)], self.dev(4))
        self.gc = [c(gw.at[q], gw.at[q], self.dev(1)) for q in (r, r4, r2, r6)]
        self.gy.start()
        self.gx.start()
        self.gc[0].start()

    def g_step4(self):
        self.gy.wait_recv()
        self.gyx.start()
        self.gc[1].start()
        self.gx.wait_recv()
        self.gxy.start()
        self.gc[2].start()

    def g_step5(self):
        self.gyx.wait_recv()
        self.gxy.wait_recv()
        self.gc[3].start()
        for s in self.gc:
            s.wait_recv()

    def q_step0(self):
        self.half = self.gqkv.shape[0] // 2
        self.gqb[...] = self.gqkv[...].astype(BF)
        h = self.half
        self.q0 = self.net.copy(self.gqb.at[pl.ds(pl.multiple_of((1 - self.k) * h, 8), h)], self.rq0, self.dev(1))
        self.q0.start()

    def q_step1(self):
        h = self.half
        self.q0.wait_recv()
        self.q[...] = (self.gqb[pl.ds(pl.multiple_of(self.k * h, 8), h)].astype(F32) + self.rq0[...].astype(F32)).astype(BF)
        self.qa = [self.net.copy(self.q.at[pl.ds(0, h // 2)], self.rq1.at[pl.ds(0, h // 2)], self.dev(4), late=False),
                   self.net.copy(self.q.at[pl.ds(h // 2, h // 2)], self.rq1.at[pl.ds(h // 2, h // 2)], self.dev(2), late=False)]
        for s in self.qa:
            s.start()

    def q_step2(self):
        h = self.half
        for s in self.qa:
            s.wait()
        self.q[...] = (self.q[...].astype(F32) + self.rq1[...].astype(F32)).astype(BF)
        self.qb = [self.net.copy(self.q.at[pl.ds(0, h // 2)], self.rq2.at[0, pl.ds(0, h // 2)], self.dev(2), late=False),
                   self.net.copy(self.q.at[pl.ds(h // 2, h // 2)], self.rq2.at[0, pl.ds(h // 2, h // 2)], self.dev(4), late=False)]
        for s in self.qb:
            s.start()

    def q_step3(self):
        h = self.half
        for s in self.qb:
            s.wait()
        self.q[...] = (self.q[...].astype(F32) + self.rq2[0].astype(F32)).astype(BF)
        for i, b in enumerate(self.extra):
            self.double(self.q, self.rq2.at[1 + i], self.dev(b))
        mine = pl.ds(pl.multiple_of(self.k * h, 8), h)
        self.gq[mine] = self.q[...]
        self.qc = self.net.copy(self.gq.at[mine], self.gq.at[mine], self.dev(1))
        self.qc.start()

    def taps_step(self):
        next(self.taps)

    def i_setup(self):
        last = self.parts - 1
        self.chunks = self.ipart.shape[1]
        rows = self.ipart.shape[2]
        self.pos, self.red, self.bc = [], {}, {}
        for d in range(self.docs):
            p = self.z if d % 2 == 0 else last - self.z
            step = 1 if d % 2 == 0 else -1
            self.pos.append(p)
            lower = {"mp": lax.rem(self.z - step + self.parts, self.parts)}
            upper = {"mp": lax.rem(self.z + step + self.parts, self.parts)}
            for c in range(self.chunks):
                self.red[d, c] = self.net.copy(self.ipart.at[d, c], self.ri.at[d, c], lower, late=False)
                out = self.ig.at[d, pl.ds(c * rows, rows)]
                self.bc[d, c] = self.net.copy(out, out, upper, late=False)

    def i_reduce(self, d, c):
        last = self.parts - 1
        p = self.pos[d]
        rows = self.ipart.shape[2]

        @pl.when(p < last)
        def _():
            self.red[d, c].wait_recv()
            self.ipart[d, c] = (self.ipart[d, c].astype(F32) + self.ri[d, c].astype(F32)).astype(BF)

        @pl.when(p > 0)
        def _():
            self.red[d, c].start()

        @pl.when(p == 0)
        def _():
            self.ig[d, c * rows : (c + 1) * rows] = self.ipart[d, c]
            self.bc[d, c].start()

    def i_back(self, d, c):
        last = self.parts - 1
        p = self.pos[d]

        @pl.when(p > 0)
        def _():
            self.bc[d, c].wait_recv()

        @pl.when((p > 0) & (p < last))
        def _():
            self.bc[d, c].start()

    def i_end(self):
        last = self.parts - 1
        for d in range(self.docs):
            p = self.pos[d]
            for c in range(self.chunks):

                @pl.when(p > 0)
                def _():
                    self.red[d, c].wait_send()

                @pl.when(p < last)
                def _():
                    self.bc[d, c].wait_send()

    def tail(self):
        self.i_setup()
        self.taps_out[...] = self.gt[...]
        self.taps = self.chain(self.taps_out, self.rtp, [self.dev(b) for b in self.bits])
        two = range(self.docs)

        def red(c):
            for d in two:
                self.i_reduce(d, c)

        def back(c):
            for d in two:
                self.i_back(d, c)

        self.q_step0()
        self.taps_step()
        red(0)
        self.q_step1()
        self.g_step2()
        self.taps_step()
        red(1)
        self.q_step2()
        self.taps_step()
        red(2)
        self.q_step3()
        self.taps_step()
        back(0)
        for _ in self.extra:
            self.taps_step()
            self.small_step()
        red(3)
        self.g_step3()
        back(1)
        self.g_step4()
        back(2)
        self.g_step5()
        back(3)
        self.qc.wait_recv()
        self.i_end()
        self.net.drain()


def attn_bwd(dp, lengths, x, wt, taps, qkv, gctx, lq, lk, sm, mix, k2, z, p, l1, l3, s1, small, gmix):
    docs, seq, dim = x.shape
    width = wt.shape[0] // 3
    heads = width // HD
    parts = gctx.shape[0]
    nblk = seq // BLK
    more = max(1, dp.bit_length() - 4)
    steps = dp.bit_length() + parts.bit_length()
    vm = pl.BlockSpec(memory_space=pltpu.VMEM)
    dma = pltpu.SemaphoreType.DMA
    out = [
        jax.ShapeDtypeStruct((3 * width, dim), BF),
        jax.ShapeDtypeStruct((docs, seq, dim), BF),
        jax.ShapeDtypeStruct((heads, WIN), F32),
        jax.ShapeDtypeStruct((SLOTS, SLICE, dim), BF),
        jax.ShapeDtypeStruct((8, dim), F32),
    ]
    h = 3 * width // 2
    return pl.pallas_call(
        functools.partial(attn_bwd_kernel, docs, heads, seq, parts, dp),
        out_shape=out,
        in_specs=[pl.BlockSpec(memory_space=pltpu.SMEM)] + [vm] * 17,
        out_specs=[vm] * len(out),
        scratch_shapes=[
            pltpu.VMEM((docs, 3 * width, seq), F32),
            pltpu.VMEM((docs, width, width), F32),
            pltpu.VMEM((docs, width, width), F32),
            pltpu.VMEM((docs, width, width), F32),
            pltpu.VMEM((heads, WIN), F32),
            pltpu.VMEM((docs, nblk, BLK, dim), BF),
            pltpu.VMEM((3 * width, dim), F32),
            pltpu.VMEM((docs, nblk, BLK, dim), BF),
            pltpu.VMEM((parts, 2, CUT, dim), BF),
            pltpu.VMEM((parts, 2, DN_ROWS, dim), BF),
            pltpu.VMEM((parts, CUT, dim), BF),
            pltpu.VMEM((parts, DN_ROWS, dim), BF),
            pltpu.VMEM((parts - 1, SLICE, dim), BF),
            pltpu.VMEM((SLICE, dim), BF),
            pltpu.VMEM((more, SLICE, dim), BF),
            pltpu.VMEM((h, dim), BF),
            pltpu.VMEM((h, dim), BF),
            pltpu.VMEM((1 + more, h, dim), BF),
            pltpu.VMEM((3 * width, dim), BF),
            pltpu.VMEM((h, dim), BF),
            pltpu.VMEM((steps, 8, dim), F32),
            pltpu.VMEM((heads, WIN), F32),
            pltpu.VMEM((steps, heads, WIN), F32),
            dma((96,)),
            dma((96,)),
        ],
        compiler_params=pltpu.CompilerParams(vmem_limit_bytes=62 * 2**20, collective_id=2, has_side_effects=True),
        cost_estimate=pl.CostEstimate(flops=int(1.2e10), bytes_accessed=int(3e7), transcendentals=0),
        name="attn_bwd",
    )(lengths, x, wt, taps, qkv, gctx, lq, lk, sm, mix, k2, z, p, l1, l3, s1, small, gmix)


def body_factory(dp, mp):
    def body(tokens, lengths, qkv_weight, out_weight, conv_taps, norm1_gain, norm1_bias, norm2_gain, norm2_bias, up_weight, down_weight, cotangent):
        docs, seq, dim = tokens.shape
        width = qkv_weight.shape[2]
        ff = up_weight.shape[1]
        wt = jnp.transpose(qkv_weight, (0, 2, 1)).reshape(3 * width, dim)
        ow, up, dn = (t.reshape(SLOTS, -1, dim) for t in (out_weight, up_weight, down_weight))
        qkv, ctx, lq, lk, sm, mix, k2, z, p, l1, l3, wall = attn_fwd(lengths, tokens, wt, conv_taps, ow, up, dn, mp)
        out_rows, gmix, gctx, s1, small = ffn(lengths, tokens, cotangent, ctx, ow, up, dn, wall, norm1_gain, norm1_bias, norm2_gain, norm2_bias)
        output = lax.all_gather(out_rows, "mp", axis=1, tiled=True)
        rtaps = conv_taps[:, ::-1]
        gqkv, input_grad, gtaps, gw, small = attn_bwd(dp, lengths, tokens, wt, rtaps, qkv, gctx, lq, lk, sm, mix, k2, z, p, l1, l3, s1, small, gmix)
        gqkv = jnp.transpose(gqkv.astype(F32).reshape(3, width, dim), (0, 2, 1))
        gtaps = lax.slice_in_dim(gtaps, 367, 367 + KSIZE, axis=1)
        gw = gw.astype(F32)
        return (
            output, input_grad, gqkv, gw[:, :OW_ROWS].reshape(width, dim), gtaps, small[0], small[1], small[2], small[3],
            gw[:, OW_ROWS:CUT].reshape(dim, ff), gw[:, CUT:].reshape(ff, dim),
        )
    return body


def solution(mesh):
    return jax.shard_map(
        body_factory(mesh.shape["dp"], mesh.shape["mp"]),
        mesh=mesh,
        in_specs=(
            P("dp", None, None), P("dp"), P(None, None, "mp"), P("mp", None), P("mp", None),
            P(), P(), P(), P(), P(None, "mp"), P("mp", None), P("dp", None, None),
        ),
        out_specs=(
            P("dp", None, None), P("dp", None, None), P(None, None, "mp"), P("mp", None), P("mp", None),
            P(), P(), P(), P(), P(None, "mp"), P("mp", None),
        ),
        check_vma=False,
    )
```

```python
import functools
import jax
import jax.numpy as jnp
import numpy as np
from jax import lax
from jax.experimental import pallas as pl
from jax.experimental.pallas import tpu as pltpu
from jax.sharding import PartitionSpec as P

HD = 64
LM = 64
KSIZE = 33
HALF = 16
NS_ITERS = 6
EPS = 1e-5
HI = lax.Precision.HIGHEST
BF = jnp.bfloat16
F32 = jnp.float32
SCALE = HD ** -0.5
WIN = 512
BLK = 256


def nn(a, b, precision=None):
    return lax.dot_general(a, b, (((1,), (0,)), ((), ())), precision=precision, preferred_element_type=F32)


def nt(a, b, precision=None):
    return lax.dot_general(a, b, (((1,), (1,)), ((), ())), precision=precision, preferred_element_type=F32)


def tn(a, b, precision=None):
    return lax.dot_general(a, b, (((0,), (0,)), ((), ())), precision=precision, preferred_element_type=F32)


def block_mask(width):
    r = lax.broadcasted_iota(jnp.int32, (width, width), 0) // HD
    c = lax.broadcasted_iota(jnp.int32, (width, width), 1) // HD
    return r == c


def spread(x, heads, mask):
    return jnp.where(mask, jnp.concatenate([x] * heads, axis=0), 0.0)


def members(length, first, count):
    s = lax.broadcasted_iota(jnp.int32, (LM, count), 1) + first
    j = lax.broadcasted_iota(jnp.int32, (LM, count), 0)
    s64 = s * LM
    return (j * length <= s64) & (s64 < (j + 1) * length) & (s < length)


def live_lanes(length, first, count):
    s = lax.broadcasted_iota(jnp.int32, (1, count), 1) + first
    return s < length


def toeplitz(row):
    full = jnp.broadcast_to(row, (BLK, WIN))
    return pltpu.roll(full, 0, 1, stride=1, stride_axis=0)


def windows(x, seq):
    rows = x.shape[0]
    pad = jnp.zeros((rows, 128), x.dtype)
    padded = jnp.concatenate([pad, x, pad], axis=1)
    return [padded[:, b * BLK : b * BLK + WIN] for b in range(seq // BLK)]


def hi_lo(x):
    hi = x.astype(BF)
    return hi, (x - hi.astype(F32)).astype(BF)


def banded(x, row, heads, seq):
    outs = []
    nblk = seq // BLK
    for h in range(heads):
        wins = jnp.concatenate(windows(x[h * HD : (h + 1) * HD], seq), axis=0)
        hi, lo = hi_lo(toeplitz(row[h : h + 1]))
        y = nt(wins, hi) + nt(wins, lo)
        outs.append(jnp.concatenate([y[b * HD : (b + 1) * HD] for b in range(nblk)], axis=1))
    return jnp.concatenate(outs, axis=0)


MESH = pl.DeviceIdType.MESH


def flip(i, bit):
    return i + bit * (1 - 2 * ((i // bit) % 2))


def partner(i, m):
    for bit in (1, 2, 4):
        if m & bit:
            i = flip(i, bit)
    return i


def greet(peers):
    bar = pltpu.get_barrier_semaphore()
    for p in peers:
        pl.semaphore_signal(bar, inc=1, device_id=p, device_id_type=MESH)
    pl.semaphore_wait(bar, len(peers))


def rcopy(src, dst, ss, rs, dev):
    return pltpu.make_async_remote_copy(src_ref=src, dst_ref=dst, send_sem=ss, recv_sem=rs, device_id=dev, device_id_type=MESH)


SLOTS = 8
OW_ROWS, UP_ROWS, DN_ROWS = 24, 96, 96
SLICE = OW_ROWS + UP_ROWS + DN_ROWS
CUT = OW_ROWS + UP_ROWS
PARTS = ((0, OW_ROWS), (OW_ROWS, UP_ROWS), (CUT, DN_ROWS))
TAP0 = 112
CHUNK = 128


class Net:
    def __init__(self, ssem, rsem):
        self.ssem, self.rsem, self.n = ssem, rsem, 0
        self.sent = []

    def copy(self, src, dst, dev, late=True):
        i = self.n
        self.n += 1
        c = rcopy(src, dst, self.ssem.at[i], self.rsem.at[i], dev)
        if late:
            self.sent.append(c)
        return c

    def drain(self):
        for c in self.sent:
            c.wait_send()
        self.sent = []


def place_taps(ref, scratch, reverse=False):
    scratch[...] = jnp.zeros_like(scratch)
    scratch[:, TAP0 : TAP0 + KSIZE] = ref[...]
    return scratch[...]


class Gather:
    def __init__(self, mp, srcs, wall, net):
        z, d = lax.axis_index("mp"), lax.axis_index("dp")
        r = lax.rem(d, SLOTS)
        self.ms = range(1, mp)
        self.zc, self.yc, self.xc, self.yxc, self.xyc, self.cc = {}, {}, {}, {}, {}, {}
        for m in self.ms:
            w = wall.at[m - 1]
            dev = {"mp": partner(z, m)}
            self.zc[m] = [net.copy(srcs[i].at[r], w.at[r, pl.ds(*PARTS[i])], dev) for i in range(3)]
            r4, r2, r6 = flip(r, 4), flip(r, 2), partner(r, 6)
            dy, dx, dc = {"dp": flip(d, 4)}, {"dp": flip(d, 2)}, {"dp": flip(d, 1)}
            self.yc[m] = net.copy(w.at[r], w.at[r], dy)
            self.xc[m] = net.copy(w.at[r], w.at[r], dx)
            s = w.at[r4, pl.ds(0, CUT)]
            self.yxc[m] = net.copy(s, s, dx)
            s = w.at[r2, pl.ds(CUT, DN_ROWS)]
            self.xyc[m] = net.copy(s, s, dy)
            self.cc[m] = [net.copy(w.at[q], w.at[q], dc) for q in (r, r4, r2, r6)]

    def start(self):
        for m in self.ms:
            for c in self.zc[m]:
                c.start()

    def step1(self, m):
        for c in self.zc[m]:
            c.wait_recv()
        self.yc[m].start()
        self.xc[m].start()
        self.cc[m][0].start()

    def step2(self, m):
        self.yc[m].wait_recv()
        self.yxc[m].start()
        self.cc[m][1].start()
        self.xc[m].wait_recv()
        self.xyc[m].start()
        self.cc[m][2].start()

    def step3(self, m):
        self.yxc[m].wait_recv()
        self.xyc[m].wait_recv()
        self.cc[m][3].start()

    def finish(self):
        for m in self.ms:
            for c in self.cc[m]:
                c.wait_recv()


def attn_fwd_kernel(docs, heads, seq, dest, len_ref, x_ref, wt_ref, taps_ref, ow_ref, up_ref, dn_ref, qkv_ref, ctx_ref, lq_ref, lk_ref, sum_ref, mix_ref, k2_ref, z_ref, p_ref, l1_ref, l3_ref, wall_ref,
                    ctx_s, taps_s, ssem, rsem):
    width = heads * HD
    me = lax.axis_index("mp")
    dd = lax.axis_index("dp")
    greet([{"mp": partner(me, m)} for m in range(1, dest)] + [{"dp": flip(dd, b)} for b in (1, 2, 4)])
    net = Net(ssem, rsem)
    gather = Gather(dest, (ow_ref, up_ref, dn_ref), wall_ref, net)
    gather.start()

    acs = {(m, d): net.copy(ctx_s.at[partner(me, m), d], ctx_ref.at[m, d], {"mp": partner(me, m)}) for d in range(docs) for m in range(1, dest)}
    taps = place_taps(taps_ref, taps_s)
    mask = block_mask(width)
    eye = jnp.where(
        lax.broadcasted_iota(jnp.int32, (width, width), 0) == lax.broadcasted_iota(jnp.int32, (width, width), 1), 1.0, 0.0
    ).astype(F32)
    for d in range(docs):
        for c in range(seq // BLK):
            xc = x_ref[d, c * BLK : (c + 1) * BLK, :]
            qkv_ref[d, :, c * BLK : (c + 1) * BLK] = nt(wt_ref[...], xc).astype(BF)
    gather.step1(1)
    k2s = []
    for d in range(docs):
        if d == 1:
            gather.step1(2)
        length = len_ref[d]
        memb = jnp.where(members(length, 0, seq), 1.0, 0.0).astype(F32)
        counts = jnp.maximum(jnp.sum(memb, axis=1, keepdims=True), 1.0)
        memb_b = memb.astype(BF)
        q = qkv_ref[d, 0:width, :]
        k = qkv_ref[d, width : 2 * width, :]
        v = qkv_ref[d, 2 * width : 3 * width, :]
        lq = spread(nt(memb_b, q) / counts, heads, mask).astype(BF)
        lk = spread(nt(memb_b, k) / counts, heads, mask).astype(BF)
        lq_ref[d] = lq
        lk_ref[d] = lk
        s2 = jnp.where(mask, nt(lq, lk) * SCALE, -1e30)
        e2 = jnp.where(mask, jnp.exp(s2 - jnp.max(s2, axis=1, keepdims=True)), 0.0)
        k2 = e2 / jnp.sum(e2, axis=1, keepdims=True)
        k2_ref[d] = k2
        k2s.append(k2)
        s3 = jnp.where(live_lanes(length, 0, seq), nn(lq, k) * SCALE, -1e30)
        m3 = jnp.max(s3, axis=1, keepdims=True)
        e3 = jnp.exp(s3 - m3)
        t3 = jnp.sum(e3, axis=1, keepdims=True)
        l3_ref[d] = jnp.broadcast_to(m3 + jnp.log(t3), (width, 128))
        k3 = (e3 / t3).astype(BF)
        sum_ref[d] = jnp.where(mask, nt(k3, v), 0.0)
    zs = []
    for d in range(docs):
        rows = jnp.sum(k2s[d] * k2s[d], axis=1, keepdims=True)
        tot = jnp.sum(rows.reshape(heads, HD, 1), axis=1, keepdims=True)
        tot = jnp.broadcast_to(tot, (heads, HD, 1)).reshape(width, 1)
        z = k2s[d].T / tot
        z_ref[d, 0] = z
        zs.append(z)
    for i in range(NS_ITERS):
        ps = [nn(k2s[d], zs[d], HI) for d in range(docs)]
        bs = [15.0 * eye - nn(ps[d], 7.0 * eye - ps[d], HI) for d in range(docs)]
        cs = [13.0 * eye - nn(ps[d], bs[d], HI) for d in range(docs)]
        zs = [0.25 * nn(zs[d], cs[d], HI) for d in range(docs)]
        for d in range(docs):
            p_ref[d, i, 0] = ps[d]
            p_ref[d, i, 1] = bs[d]
            p_ref[d, i, 2] = cs[d]
            z_ref[d, i + 1] = zs[d]
        if i == 2:
            gather.step1(3)
        if i == 4:
            gather.step2(1)
    for d in range(docs):
        length = len_ref[d]
        q = qkv_ref[d, 0:width, :]
        v = qkv_ref[d, 2 * width : 3 * width, :]
        live = live_lanes(length, 0, seq)
        mix = jnp.where(mask, nn(zs[d], sum_ref[d], HI), 0.0)
        mix_ref[d] = mix.astype(BF)
        mix_t = mix.T.astype(BF)
        s1 = (nn(lk_ref[d], q) * SCALE).reshape(heads, LM, seq)
        m1 = jnp.max(s1, axis=1, keepdims=True)
        e1 = jnp.exp(s1 - m1)
        t1 = jnp.sum(e1, axis=1, keepdims=True)
        l1_ref[d] = (m1 + jnp.log(t1)).reshape(heads, seq)
        k1 = (e1 / t1).reshape(width, seq).astype(BF)
        vl = jnp.where(live, v, 0).astype(BF)
        ctx = nn(mix_t, k1) + banded(vl, taps, heads, seq)
        ctx = jnp.where(live, ctx, 0.0).astype(BF)
        part = seq // dest
        for i in range(dest):
            ctx_s[i, d] = ctx[:, i * part : (i + 1) * part]
        for m in range(1, dest):
            acs[m, d].start()
        ctx_ref[0, d] = ctx_s[me, d]
        if d == 0:
            gather.step2(2)
    gather.step3(1)
    gather.step2(3)
    gather.step3(2)
    gather.step3(3)
    gather.finish()
    for d in range(docs):
        for m in range(1, dest):
            acs[m, d].wait_recv()
    net.drain()


def attn_fwd(lengths, x, wt, taps, ow, up, dn, dest):
    docs, seq, dim = x.shape
    width = wt.shape[0] // 3
    heads = width // HD
    vm = pl.BlockSpec(memory_space=pltpu.VMEM)
    out = [
        jax.ShapeDtypeStruct((docs, 3 * width, seq), BF),
        jax.ShapeDtypeStruct((dest, docs, width, seq // dest), BF),
        jax.ShapeDtypeStruct((docs, width, width), BF),
        jax.ShapeDtypeStruct((docs, width, width), BF),
        jax.ShapeDtypeStruct((docs, width, width), F32),
        jax.ShapeDtypeStruct((docs, width, width), BF),
        jax.ShapeDtypeStruct((docs, width, width), F32),
        jax.ShapeDtypeStruct((docs, NS_ITERS + 1, width, width), F32),
        jax.ShapeDtypeStruct((docs, NS_ITERS, 3, width, width), F32),
        jax.ShapeDtypeStruct((docs, heads, seq), F32),
        jax.ShapeDtypeStruct((docs, width, 128), F32),
        jax.ShapeDtypeStruct((dest - 1, SLOTS, SLICE, dim), BF),
    ]
    any_ = pl.BlockSpec(memory_space=pl.ANY)
    dma = pltpu.SemaphoreType.DMA
    return pl.pallas_call(
        functools.partial(attn_fwd_kernel, docs, heads, seq, dest),
        out_shape=out,
        in_specs=[pl.BlockSpec(memory_space=pltpu.SMEM), vm, vm, vm, any_, any_, any_],
        out_specs=[vm] * (len(out) - 1) + [any_],
        scratch_shapes=[
            pltpu.VMEM((dest, docs, width, seq // dest), BF),
            pltpu.VMEM((heads, WIN), F32),
            dma((64,)),
            dma((64,)),
        ],
        compiler_params=pltpu.CompilerParams(vmem_limit_bytes=60 * 2**20, collective_id=0, has_side_effects=True),
        cost_estimate=pl.CostEstimate(flops=int(8e9), bytes_accessed=int(3e7), transcendentals=0),
        name="attn_fwd",
    )(lengths, x, wt, taps, ow, up, dn)


def ln_stats(v):
    mu = jnp.mean(v, axis=-1, keepdims=True)
    cen = v - mu
    var = jnp.mean(cen * cen, axis=-1, keepdims=True)
    r = lax.rsqrt(var + EPS)
    return cen * r, r


def ln_back(g, xhat, r):
    m1 = jnp.mean(g, axis=-1, keepdims=True)
    m2 = jnp.mean(g * xhat, axis=-1, keepdims=True)
    return r * (g - m1 - xhat * m2)


ROOT_HALF = 0.7071067811865476
INV_ROOT_2PI = 0.3989422804014327


def ffn_kernel(groups, docs, rows, len_ref, x_hbm, cot_hbm, ctx_ref, ow_hbm, up_hbm, dn_hbm, wall_hbm, g1_ref, b1_ref, g2_ref, b2_ref,
               out_ref, gmix_ref, gctx_ref, s1_ref, small_ref, x_s, cot_s, w_s, rc_s, gc_s, nb_s, fac_s, act_s, br_s, x1_s, gn_s, lsem, ssem, rsem):
    n = docs * rows
    dim = x_s.shape[-1]
    z, dd = lax.axis_index("mp"), lax.axis_index("dp")
    kk = lax.rem(dd, 2)
    loads = []
    for d in range(docs):
        loads.append(pltpu.make_async_copy(x_hbm.at[d, pl.ds(pl.multiple_of(z * rows, rows), rows)], x_s.at[pl.ds(d * rows, rows)], lsem.at[d]))
        loads.append(pltpu.make_async_copy(cot_hbm.at[d, pl.ds(pl.multiple_of(z * rows, rows), rows)], cot_s.at[pl.ds(d * rows, rows)], lsem.at[docs + d]))
    own = [pltpu.make_async_copy(src, w_s.at[0, :, :, pl.ds(*PARTS[i])], lsem.at[2 * docs + i]) for i, src in enumerate((ow_hbm, up_hbm, dn_hbm))]
    walls = [pltpu.make_async_copy(wall_hbm.at[m - 1], w_s.at[m], lsem.at[2 * docs + 2 + m]) for m in range(1, groups)]
    for c in own + walls + loads:
        c.start()
    greet([{"mp": partner(z, m)} for m in range(1, groups)] + [{"dp": flip(dd, 1)}])
    net = Net(ssem, rsem)
    dc = {"dp": flip(dd, 1)}
    ccs = {}
    for g in range(groups):
        for part, (lo, size) in enumerate(((OW_ROWS, SLICE - OW_ROWS), (0, OW_ROWS))):
            ccs[g, part] = net.copy(w_s.at[g, :, 1 - kk, pl.ds(lo, size)], rc_s.at[g, :, pl.ds(lo, size)], dc)
    gcs = {m: net.copy(gc_s.at[m - 1], gctx_ref.at[z], {"mp": partner(z, m)}) for m in range(1, groups)}

    def take(g, part):
        lo, size = PARTS[part]
        return w_s[g, :, :, lo : lo + size, :].reshape(SLOTS * size, dim)

    def put(g, part, val):
        lo, size = PARTS[part]
        w_s[g, :, :, lo : lo + size, :] = val.astype(BF).reshape(SLOTS // 2, 2, size, dim)

    first = z * rows
    live = jnp.concatenate([(lax.broadcasted_iota(jnp.int32, (rows, 1), 0) + first < len_ref[d]).astype(F32) for d in range(docs)], axis=0)
    gain1, bias1 = g1_ref[...].reshape(1, dim), b1_ref[...].reshape(1, dim)
    gain2, bias2 = g2_ref[...].reshape(1, dim), b2_ref[...].reshape(1, dim)
    for c in own + walls + loads:
        c.wait()
    parts = []
    for d in range(docs):
        acc = None
        for g in range(groups):
            t = tn(ctx_ref[g, d], take(g, 0)).astype(BF).astype(F32)
            acc = t if acc is None else acc + t
        parts.append(acc)
    mixed = x_s[...].astype(F32) + jnp.concatenate(parts, axis=0)
    xh1, r1 = ln_stats(mixed)
    x1_s[...] = xh1
    normed = xh1 * gain1 + bias1
    nb_s[...] = normed.astype(BF)
    br_s[...] = normed

    def fwd_group(g, _):
        h = nn(nb_s[...], take(g, 1))
        phi_big = 0.5 * (1.0 + lax.erf(h * ROOT_HALF))
        act = (h * phi_big).astype(BF)
        act_s[g] = act
        fac_s[g] = phi_big + h * (jnp.exp(-0.5 * h * h) * INV_ROOT_2PI)
        br_s[...] += nn(act, take(g, 2)).astype(BF).astype(F32)
        return 0

    lax.fori_loop(0, groups, fwd_group, 0)
    xh2, r2 = ln_stats(br_s[...])
    out_ref[...] = (live * (xh2 * gain2 + bias2)).astype(BF).reshape(docs, rows, dim)
    g_out = live * cot_s[...].astype(F32)
    gg2 = jnp.sum(g_out * xh2, axis=0, keepdims=True)
    gb2 = jnp.sum(g_out, axis=0, keepdims=True)
    g_res = ln_back(g_out * gain2, xh2, r2)
    gn_s[...] = g_res
    br_s[...] = g_res
    gbr_s = x_s
    gbr_s[...] = g_res.astype(BF)

    def bwd_group(g):
        gbr = gbr_s[...]
        g_pre = (nt(gbr, take(g, 2)) * fac_s[g]).astype(BF)
        put(g, 2, tn(act_s[g], gbr))
        gn_s[...] += nt(g_pre, take(g, 1))
        put(g, 1, tn(nb_s[...], g_pre))

    for g in range(groups):
        bwd_group(g)
        ccs[g, 0].start()
    g_n = gn_s[...]
    xh1 = x1_s[...]
    gg1 = jnp.sum(g_n * xh1, axis=0, keepdims=True)
    gb1 = jnp.sum(g_n, axis=0, keepdims=True)
    small_ref[...] = jnp.concatenate([gg1, gb1, gg2, gb2, jnp.zeros((4, dim), F32)], axis=0)
    g_mix = ln_back(g_n * gain1, xh1, r1)
    gmix_ref[...] = g_mix.reshape(docs, rows, dim)
    g_att = g_mix.astype(BF)
    for m in (3, 2, 1, 0) if groups == 4 else reversed(range(groups)):
        t = nt(take(m, 0), g_att).astype(BF)
        for d in range(docs):
            if m:
                gc_s[m - 1, d] = t[:, d * rows : (d + 1) * rows]
            else:
                gctx_ref[z, d] = t[:, d * rows : (d + 1) * rows]
        if m:
            gcs[m].start()
    for g in range(groups):
        acc = None
        for d in range(docs):
            t = nn(ctx_ref[g, d], g_att[d * rows : (d + 1) * rows])
            acc = t if acc is None else acc + t
        put(g, 0, acc)
        ccs[g, 1].start()
    for g in range(groups):
        ccs[g, 0].wait_recv()
        ccs[g, 1].wait_recv()
        for j in range(SLOTS // 2):
            s1_ref[g, j // 2, j % 2] = (w_s[g, j, kk].astype(F32) + rc_s[g, j].astype(F32)).astype(BF)
    for m in range(1, groups):
        gcs[m].wait_recv()
    net.drain()


def ffn(lengths, x, cot, ctx, ow, up, dn, wall, g1, b1, g2, b2):
    docs, seq, dim = x.shape
    groups, _, width, rows = ctx.shape
    ff = SLOTS * UP_ROWS
    n = docs * rows
    vm = pl.BlockSpec(memory_space=pltpu.VMEM)
    any_ = pl.BlockSpec(memory_space=pl.ANY)
    sm = pl.BlockSpec(memory_space=pltpu.SMEM)
    dma = pltpu.SemaphoreType.DMA
    out = [
        jax.ShapeDtypeStruct((docs, rows, dim), BF),
        jax.ShapeDtypeStruct((docs, rows, dim), F32),
        jax.ShapeDtypeStruct((groups, docs, width, rows), BF),
        jax.ShapeDtypeStruct((groups, 2, 2, SLICE, dim), BF),
        jax.ShapeDtypeStruct((8, dim), F32),
    ]
    wall = wall.reshape(groups - 1, SLOTS // 2, 2, SLICE, dim)
    ow, up, dn = (t.reshape(SLOTS // 2, 2, -1, dim) for t in (ow, up, dn))
    return pl.pallas_call(
        functools.partial(ffn_kernel, groups, docs, rows),
        out_shape=out,
        in_specs=[sm, any_, any_, vm, any_, any_, any_, any_, vm, vm, vm, vm],
        out_specs=[vm] * len(out),
        scratch_shapes=[
            pltpu.VMEM((n, dim), BF),
            pltpu.VMEM((n, dim), BF),
            pltpu.VMEM((groups, SLOTS // 2, 2, SLICE, dim), BF),
            pltpu.VMEM((groups, SLOTS // 2, SLICE, dim), BF),
            pltpu.VMEM((groups - 1, docs, width, rows), BF),
            pltpu.VMEM((n, dim), BF),
            pltpu.VMEM((groups, n, ff), F32),
            pltpu.VMEM((groups, n, ff), BF),
            pltpu.VMEM((n, dim), F32),
            pltpu.VMEM((n, dim), F32),
            pltpu.VMEM((n, dim), F32),
            dma((2 * docs + 2 + groups,)),
            dma((16,)),
            dma((16,)),
        ],
        compiler_params=pltpu.CompilerParams(vmem_limit_bytes=62 * 2**20, collective_id=1, has_side_effects=True),
        cost_estimate=pl.CostEstimate(flops=int(1.8e10), bytes_accessed=int(4e7), transcendentals=0),
        name="ffn",
    )(lengths, x, cot, ctx, ow, up, dn, wall, g1, b1, g2, b2)


def attn_bwd_kernel(docs, heads, seq, parts, dp, len_ref, x_ref, wt_ref, taps_ref, qkv_ref, gctx_ref, lq_ref, lk_ref, sum_ref, mix_ref, k2_ref,
                    z_ref, p_ref, l1_ref, l3_ref, s1_ref, small_in, gmix_ref, gq_ref, ig_ref, taps_out, gw_ref, small_ref,
                    g_s, ginv_s, glq_s, glk_s, taps_s, ipart_ref, gqkv_ref, ri_s, ra1, rb1, ra2, rb2, rz, fin_s, rfin, rq0, rq1, rq2, gqb, q_s, rsm, gt_s, rtp, ssem, rsem, isem):
    width = heads * HD
    dim = x_ref.shape[-1]
    nd = net_setup(docs, seq, parts, dp, s1_ref, small_in, gq_ref, ig_ref, taps_out, gw_ref, small_ref, ipart_ref, gqkv_ref, ri_s, ra1, rb1, ra2, rb2, rz, fin_s, rfin, rq0, rq1, rq2, gqb, q_s, rsm, gt_s, rtp, ssem, rsem, isem)
    zi = lax.axis_index("mp")
    nd.begin()
    rtaps = place_taps(taps_ref, taps_s)
    nblk = seq // BLK
    mask = block_mask(width)
    anti = jnp.where(
        lax.broadcasted_iota(jnp.int32, (BLK, BLK), 0) + lax.broadcasted_iota(jnp.int32, (BLK, BLK), 1) == BLK - 1, 1.0, 0.0
    ).astype(BF)
    gaccs = [None] * heads
    for d in range(docs):
        length = len_ref[d]
        live = live_lanes(length, 0, seq)
        q = qkv_ref[d, 0:width, :]
        k = qkv_ref[d, width : 2 * width, :]
        v = qkv_ref[d, 2 * width : 3 * width, :]
        gc = jnp.concatenate([gctx_ref[i, d] for i in range(parts)], axis=1)
        gc = jnp.where(live, gc, 0).astype(BF)
        lq, lk = lq_ref[d], lk_ref[d]
        s1 = (nn(lk, q) * SCALE).reshape(heads, LM, seq)
        k1 = jnp.exp(s1 - l1_ref[d].reshape(heads, 1, seq))
        gmixing = jnp.where(mask, nt(k1.reshape(width, seq).astype(BF), gc), 0.0)
        gk1 = nn(mix_ref[d], gc).reshape(heads, LM, seq)
        gs1 = (k1 * (gk1 - jnp.sum(gk1 * k1, axis=1, keepdims=True))).reshape(width, seq).astype(BF)
        ginv_s[d] = nt(gmixing, sum_ref[d], HI)
        gsum = tn(z_ref[d, NS_ITERS], gmixing, HI)
        gsum = jnp.where(mask, gsum, 0.0)
        gsum_b = gsum.astype(BF)
        s3 = jnp.where(live, nn(lq, k) * SCALE, -1e30)
        k3 = jnp.exp(s3 - l3_ref[d][:, 0:1])
        gk3 = nn(gsum_b, v)
        gs3 = (k3 * (gk3 - jnp.sum(gk3 * k3, axis=1, keepdims=True))).astype(BF)
        glq_s[d] = jnp.where(mask, nt(gs3, k), 0.0) * SCALE
        glk_s[d] = jnp.where(mask, nt(gs1, q), 0.0) * SCALE
        lq_t = lq.astype(F32).T.astype(BF)
        lk_t = lk.astype(F32).T.astype(BF)
        g_s[d, 0:width, :] = nn(lk_t, gs1) * SCALE
        g_s[d, width : 2 * width, :] = nn(lq_t, gs3) * SCALE
        gv = nn(gsum.T.astype(BF), k3.astype(BF))
        gvl = banded(gc, rtaps, heads, seq)
        g_s[d, 2 * width : 3 * width, :] = gv + jnp.where(live, gvl, 0.0)
        vl = jnp.where(live, v, 0).astype(BF)
        for h in range(heads):
            wins = jnp.concatenate(windows(vl[h * HD : (h + 1) * HD], seq), axis=0)
            gch = gc[h * HD : (h + 1) * HD]
            stack = jnp.concatenate([gch[:, b * BLK : (b + 1) * BLK] for b in range(nblk)], axis=0)
            rev = nt(anti, stack).astype(BF)
            t = nn(rev, wins)
            gaccs[h] = t if gaccs[h] is None else gaccs[h] + t
    for h in range(heads):
        rolled = pltpu.roll(gaccs[h], 0, 1, stride=1, stride_axis=0)
        gt_s[h : h + 1, :] = jnp.sum(rolled, axis=0, keepdims=True)
    gz = [ginv_s[d] for d in range(docs)]
    gk = [jnp.zeros((width, width), F32) for _ in range(docs)]
    eye = jnp.where(
        lax.broadcasted_iota(jnp.int32, (width, width), 0) == lax.broadcasted_iota(jnp.int32, (width, width), 1), 1.0, 0.0
    ).astype(F32)
    for i in reversed(range(NS_ITERS)):
        if i < NS_ITERS - 1:
            nd.small_step()
        for d in range(docs):
            z, p, b, c = z_ref[d, i], p_ref[d, i, 0], p_ref[d, i, 1], p_ref[d, i, 2]
            a = 7.0 * eye - p
            g = 0.25 * gz[d]
            gc_ = tn(z, g, HI)
            gzn = nt(g, c, HI)
            gp = -nt(gc_, b, HI)
            gb = -tn(p, gc_, HI)
            gp = gp - nt(gb, a, HI)
            ga = -tn(p, gb, HI)
            gp = gp - ga
            gk[d] = gk[d] + nt(gp, z, HI)
            gz[d] = gzn + tn(k2_ref[d], gp, HI)
    nd.g_step1()
    for d in range(docs):
        length = len_ref[d]
        k2 = k2_ref[d]
        rows = jnp.sum(k2 * k2, axis=1, keepdims=True)
        tot = jnp.sum(rows.reshape(heads, HD, 1), axis=1, keepdims=True)
        tot = jnp.broadcast_to(tot, (heads, HD, 1)).reshape(width, 1)
        g = gz[d]
        dot = jnp.sum(g * k2.T, axis=1, keepdims=True)
        dot = jnp.sum(dot.reshape(heads, HD, 1), axis=1, keepdims=True)
        dot = jnp.broadcast_to(dot, (heads, HD, 1)).reshape(width, 1)
        gk2 = gk[d] + (g / tot).T - k2 * (2.0 * dot / (tot * tot))
        gs2 = k2 * (gk2 - jnp.sum(gk2 * k2, axis=1, keepdims=True)) * SCALE
        memb = jnp.where(members(length, 0, seq), 1.0, 0.0).astype(F32)
        counts = jnp.maximum(jnp.sum(memb, axis=1, keepdims=True), 1.0)
        counts = jnp.concatenate([counts] * heads, axis=0)
        memb3 = jnp.concatenate([memb.astype(BF)] * heads, axis=0)
        glq = (glq_s[d] + nn(gs2, lk_ref[d].astype(F32), HI)) / counts
        glk = (glk_s[d] + tn(gs2, lq_ref[d].astype(F32), HI)) / counts
        hi, lo = hi_lo(glq.T)
        gq = g_s[d, 0:width, :] + nn(hi, memb3) + nn(lo, memb3)
        hi, lo = hi_lo(glk.T)
        gkk = g_s[d, width : 2 * width, :] + nn(hi, memb3) + nn(lo, memb3)
        g_all = jnp.concatenate([gq, gkk, g_s[d, 2 * width : 3 * width, :]], axis=0).astype(BF)
        gw = nn(g_all, x_ref[d])
        if d == 0:
            gqkv_ref[...] = gw
        else:
            gqkv_ref[...] += gw
        for c in range(nblk):
            t = tn(g_all[:, c * BLK : (c + 1) * BLK], wt_ref[...])
            t = (t + jnp.where(zi == c, 1.0, 0.0) * gmix_ref[d]).astype(BF)
            per = BLK // CHUNK
            ipart_ref[d, c * per : (c + 1) * per] = t.reshape(per, CHUNK, dim)
    nd.tail()


class net_setup:
    def __init__(self, docs, seq, parts, dp, s1, small_in, gq, ig, taps_out, gw, small, ipart, gqkv, ri, ra1, rb1, ra2, rb2, rz, fin, rfin, rq0, rq1, rq2, gqb, q, rsm, gt, rtp, ssem, rsem, isem):
        self.__dict__.update({k: v for k, v in locals().items() if k != "self"})
        self.z, self.d = lax.axis_index("mp"), lax.axis_index("dp")
        self.r = lax.rem(self.d, SLOTS)
        self.y, self.x, self.k = self.r // 4, lax.rem(self.r // 2, 2), lax.rem(self.r, 2)
        self.net = Net(ssem, rsem)
        self.extra = [b for b in (8, 16, 32, 64, 128) if b < dp]
        self.low = (1, 2, 4)
        self.bits = list(self.low) + self.extra

    def dev(self, bit):
        return {"dp": flip(self.d, bit)}

    def zdev(self, m):
        return {"mp": partner(self.z, m)}

    def begin(self):
        greet([self.zdev(m) for m in range(1, self.parts)] + [self.dev(b) for b in self.bits])
        c = self.net.copy
        self.a1 = c(self.s1.at[:, 1 - self.y, :, pl.ds(0, CUT)], self.ra1, self.dev(4))
        self.b1 = c(self.s1.at[:, :, 1 - self.x, pl.ds(CUT, DN_ROWS)], self.rb1, self.dev(2))
        self.a1.start()
        self.b1.start()
        self.small[...] = self.small_in[...]
        self.smalls = self.chain(self.small, self.rsm, [self.dev(b) for b in self.bits] + [self.zdev(1 << j) for j in range(self.parts.bit_length() - 1)])
        self.small_step()

    def double(self, buf, recv, bit_dev):
        c = self.net.copy(buf, recv, bit_dev, late=False)
        c.start()
        c.wait()
        buf[...] = (buf[...].astype(F32) + recv[...].astype(F32)).astype(buf.dtype)

    def chain(self, buf, recv, devs):
        for i, dev in enumerate(devs):
            c = self.net.copy(buf, recv.at[i], dev, late=False)
            c.start()
            yield
            c.wait()
            buf[...] = buf[...] + recv[i]
        while True:
            yield

    def small_step(self):
        next(self.smalls)

    def g_step1(self):
        c = self.net.copy
        self.a1.wait_recv()
        self.b1.wait_recv()
        for g in range(self.parts):
            for j in range(2):
                self.ra1[g, j] = (self.ra1[g, j].astype(F32) + self.s1[g, self.y, j, 0:CUT].astype(F32)).astype(BF)
                self.rb1[g, j] = (self.rb1[g, j].astype(F32) + self.s1[g, j, self.x, CUT:SLICE].astype(F32)).astype(BF)
        self.a2 = c(self.ra1.at[:, 1 - self.x], self.ra2, self.dev(2))
        self.b2 = c(self.rb1.at[:, 1 - self.y], self.rb2, self.dev(4))
        self.a2.start()
        self.b2.start()

    def g_step2(self):
        c = self.net.copy
        self.a2.wait_recv()
        self.b2.wait_recv()
        for g in range(self.parts):
            self.ra2[g] = (self.ra2[g].astype(F32) + self.ra1[g, self.x].astype(F32)).astype(BF)
            self.rb2[g] = (self.rb2[g].astype(F32) + self.rb1[g, self.y].astype(F32)).astype(BF)
        self.zs = []
        for m in range(1, self.parts):
            self.zs.append(c(self.ra2.at[m], self.rz.at[m - 1, pl.ds(0, CUT)], self.zdev(m)))
            self.zs.append(c(self.rb2.at[m], self.rz.at[m - 1, pl.ds(CUT, DN_ROWS)], self.zdev(m)))
        for s in self.zs:
            s.start()

    def g_step3(self):
        c = self.net.copy
        for s in self.zs:
            s.wait_recv()
        top, bot = self.ra2[0].astype(F32), self.rb2[0].astype(F32)
        for m in range(1, self.parts):
            top = top + self.rz[m - 1, 0:CUT].astype(F32)
            bot = bot + self.rz[m - 1, CUT:SLICE].astype(F32)
        self.fin[0:CUT] = top.astype(BF)
        self.fin[CUT:SLICE] = bot.astype(BF)
        for i, b in enumerate(self.extra):
            self.double(self.fin, self.rfin.at[i], self.dev(b))
        r, gw = self.r, self.gw
        gw[r] = self.fin[...]
        r4, r2, r6 = flip(r, 4), flip(r, 2), partner(r, 6)
        self.gy = c(gw.at[r], gw.at[r], self.dev(4))
        self.gx = c(gw.at[r], gw.at[r], self.dev(2))
        self.gyx = c(gw.at[r4, pl.ds(0, CUT)], gw.at[r4, pl.ds(0, CUT)], self.dev(2))
        self.gxy = c(gw.at[r2, pl.ds(CUT, DN_ROWS)], gw.at[r2, pl.ds(CUT, DN_ROWS)], self.dev(4))
        self.gc = [c(gw.at[q], gw.at[q], self.dev(1)) for q in (r, r4, r2, r6)]
        self.gy.start()
        self.gx.start()
        self.gc[0].start()

    def g_step4(self):
        self.gy.wait_recv()
        self.gyx.start()
        self.gc[1].start()
        self.gx.wait_recv()
        self.gxy.start()
        self.gc[2].start()

    def g_step5(self):
        self.gyx.wait_recv()
        self.gxy.wait_recv()
        self.gc[3].start()
        for s in self.gc:
            s.wait_recv()

    def q_step0(self):
        self.half = self.gqkv.shape[0] // 2
        self.gqb[...] = self.gqkv[...].astype(BF)
        h = self.half
        self.q0 = self.net.copy(self.gqb.at[pl.ds(pl.multiple_of((1 - self.k) * h, 8), h)], self.rq0, self.dev(1))
        self.q0.start()

    def q_step1(self):
        h = self.half
        self.q0.wait_recv()
        self.q[...] = (self.gqb[pl.ds(pl.multiple_of(self.k * h, 8), h)].astype(F32) + self.rq0[...].astype(F32)).astype(BF)
        self.qa = [self.net.copy(self.q.at[pl.ds(0, h // 2)], self.rq1.at[pl.ds(0, h // 2)], self.dev(4), late=False),
                   self.net.copy(self.q.at[pl.ds(h // 2, h // 2)], self.rq1.at[pl.ds(h // 2, h // 2)], self.dev(2), late=False)]
        for s in self.qa:
            s.start()

    def q_step2(self):
        h = self.half
        for s in self.qa:
            s.wait()
        self.q[...] = (self.q[...].astype(F32) + self.rq1[...].astype(F32)).astype(BF)
        self.qb = [self.net.copy(self.q.at[pl.ds(0, h // 2)], self.rq2.at[0, pl.ds(0, h // 2)], self.dev(2), late=False),
                   self.net.copy(self.q.at[pl.ds(h // 2, h // 2)], self.rq2.at[0, pl.ds(h // 2, h // 2)], self.dev(4), late=False)]
        for s in self.qb:
            s.start()

    def q_step3(self):
        h = self.half
        for s in self.qb:
            s.wait()
        self.q[...] = (self.q[...].astype(F32) + self.rq2[0].astype(F32)).astype(BF)
        for i, b in enumerate(self.extra):
            self.double(self.q, self.rq2.at[1 + i], self.dev(b))
        mine = pl.ds(pl.multiple_of(self.k * h, 8), h)
        self.gq[mine] = self.q[...]
        self.qc = self.net.copy(self.gq.at[mine], self.gq.at[mine], self.dev(1))
        self.qc.start()

    def taps_step(self):
        next(self.taps)

    def i_setup(self):
        last = self.parts - 1
        self.chunks = self.ipart.shape[1]
        self.pos, self.lower, self.upper = [], [], []
        for d in range(self.docs):
            step = 1 if d % 2 == 0 else -1
            self.pos.append(self.z if d % 2 == 0 else last - self.z)
            self.lower.append({"mp": lax.rem(self.z - step + self.parts, self.parts)})
            self.upper.append({"mp": lax.rem(self.z + step + self.parts, self.parts)})

    def red(self, d, c):
        return rcopy(self.ipart.at[d, c], self.ri.at[d, c], self.isem.at[0, d, c], self.isem.at[1, d, c], self.lower[d])

    def bc(self, d, c):
        return rcopy(self.ig.at[d, c], self.ig.at[d, c], self.isem.at[2, d, c], self.isem.at[3, d, c], self.upper[d])

    def i_time(self, t):
        last = self.parts - 1
        for d in range(self.docs):
            p = self.pos[d]
            c = t - last + p
            ok = (c >= 0) & (c < self.chunks)

            @pl.when(ok & (p < last))
            def _():
                self.red(d, c).wait_recv()
                self.ipart[d, c] = (self.ipart[d, c].astype(F32) + self.ri[d, c].astype(F32)).astype(BF)

            @pl.when(ok & (p > 0))
            def _():
                self.red(d, c).start()

            @pl.when(ok & (p == 0))
            def _():
                self.ig[d, c] = self.ipart[d, c]
                self.bc(d, c).start()

        for d in range(self.docs):
            p = self.pos[d]
            c = t - last - p
            ok = (c >= 0) & (c < self.chunks) & (p > 0)

            @pl.when(ok)
            def _():
                self.bc(d, c).wait_recv()

            @pl.when(ok & (p < last))
            def _():
                self.bc(d, c).start()

    def i_end(self):
        last = self.parts - 1
        for d in range(self.docs):
            p = self.pos[d]

            @pl.when(p > 0)
            def _():
                for c in range(self.chunks):
                    self.red(d, c).wait_send()

            @pl.when(p < last)
            def _():
                for c in range(self.chunks):
                    self.bc(d, c).wait_send()

    def tail(self):
        self.i_setup()
        self.taps_out[...] = self.gt[...]
        self.taps = self.chain(self.taps_out, self.rtp, [self.dev(b) for b in self.bits])
        todo = [(self.q_step0, self.taps_step), (), (self.q_step1, self.g_step2, self.taps_step), (), (self.q_step2, self.taps_step), (),
                (self.q_step3, self.taps_step), (self.taps_step, self.small_step) * len(self.extra), (), (self.g_step3,), (), (self.g_step4,), (), (self.g_step5,)]
        steps = self.chunks + 2 * (self.parts - 1)
        for t in range(max(steps, len(todo))):
            if t < steps:
                self.i_time(t)
            for f in todo[t] if t < len(todo) else ():
                f()
        self.qc.wait_recv()
        self.i_end()
        self.net.drain()


def attn_bwd(dp, lengths, x, wt, taps, qkv, gctx, lq, lk, sm, mix, k2, z, p, l1, l3, s1, small, gmix):
    docs, seq, dim = x.shape
    width = wt.shape[0] // 3
    heads = width // HD
    parts = gctx.shape[0]
    nblk = seq // BLK
    nchunk = seq // CHUNK
    more = max(1, dp.bit_length() - 4)
    steps = dp.bit_length() + parts.bit_length()
    vm = pl.BlockSpec(memory_space=pltpu.VMEM)
    dma = pltpu.SemaphoreType.DMA
    out = [
        jax.ShapeDtypeStruct((3 * width, dim), BF),
        jax.ShapeDtypeStruct((docs, nchunk, CHUNK, dim), BF),
        jax.ShapeDtypeStruct((heads, WIN), F32),
        jax.ShapeDtypeStruct((SLOTS, SLICE, dim), BF),
        jax.ShapeDtypeStruct((8, dim), F32),
    ]
    h = 3 * width // 2
    return pl.pallas_call(
        functools.partial(attn_bwd_kernel, docs, heads, seq, parts, dp),
        out_shape=out,
        in_specs=[pl.BlockSpec(memory_space=pltpu.SMEM)] + [vm] * 17,
        out_specs=[vm] * len(out),
        scratch_shapes=[
            pltpu.VMEM((docs, 3 * width, seq), F32),
            pltpu.VMEM((docs, width, width), F32),
            pltpu.VMEM((docs, width, width), F32),
            pltpu.VMEM((docs, width, width), F32),
            pltpu.VMEM((heads, WIN), F32),
            pltpu.VMEM((docs, nchunk, CHUNK, dim), BF),
            pltpu.VMEM((3 * width, dim), F32),
            pltpu.VMEM((docs, nchunk, CHUNK, dim), BF),
            pltpu.VMEM((parts, 2, CUT, dim), BF),
            pltpu.VMEM((parts, 2, DN_ROWS, dim), BF),
            pltpu.VMEM((parts, CUT, dim), BF),
            pltpu.VMEM((parts, DN_ROWS, dim), BF),
            pltpu.VMEM((parts - 1, SLICE, dim), BF),
            pltpu.VMEM((SLICE, dim), BF),
            pltpu.VMEM((more, SLICE, dim), BF),
            pltpu.VMEM((h, dim), BF),
            pltpu.VMEM((h, dim), BF),
            pltpu.VMEM((1 + more, h, dim), BF),
            pltpu.VMEM((3 * width, dim), BF),
            pltpu.VMEM((h, dim), BF),
            pltpu.VMEM((steps, 8, dim), F32),
            pltpu.VMEM((heads, WIN), F32),
            pltpu.VMEM((steps, heads, WIN), F32),
            dma((96,)),
            dma((96,)),
            dma((4, docs, nchunk)),
        ],
        compiler_params=pltpu.CompilerParams(vmem_limit_bytes=62 * 2**20, collective_id=2, has_side_effects=True),
        cost_estimate=pl.CostEstimate(flops=int(1.2e10), bytes_accessed=int(3e7), transcendentals=0),
        name="attn_bwd",
    )(lengths, x, wt, taps, qkv, gctx, lq, lk, sm, mix, k2, z, p, l1, l3, s1, small, gmix)


def body_factory(dp, mp):
    def body(tokens, lengths, qkv_weight, out_weight, conv_taps, norm1_gain, norm1_bias, norm2_gain, norm2_bias, up_weight, down_weight, cotangent):
        docs, seq, dim = tokens.shape
        width = qkv_weight.shape[2]
        ff = up_weight.shape[1]
        wt = jnp.transpose(qkv_weight, (0, 2, 1)).reshape(3 * width, dim)
        ow, up, dn = (t.reshape(SLOTS, -1, dim) for t in (out_weight, up_weight, down_weight))
        qkv, ctx, lq, lk, sm, mix, k2, z, p, l1, l3, wall = attn_fwd(lengths, tokens, wt, conv_taps, ow, up, dn, mp)
        out_rows, gmix, gctx, s1, small = ffn(lengths, tokens, cotangent, ctx, ow, up, dn, wall, norm1_gain, norm1_bias, norm2_gain, norm2_bias)
        output = lax.all_gather(out_rows, "mp", axis=1, tiled=True)
        rtaps = conv_taps[:, ::-1]
        gqkv, input_grad, gtaps, gw, small = attn_bwd(dp, lengths, tokens, wt, rtaps, qkv, gctx, lq, lk, sm, mix, k2, z, p, l1, l3, s1, small, gmix)
        input_grad = input_grad.reshape(docs, seq, dim)
        gqkv = jnp.transpose(gqkv.astype(F32).reshape(3, width, dim), (0, 2, 1))
        gtaps = lax.slice_in_dim(gtaps, 367, 367 + KSIZE, axis=1)
        gw = gw.astype(F32)
        return (
            output, input_grad, gqkv, gw[:, :OW_ROWS].reshape(width, dim), gtaps, small[0], small[1], small[2], small[3],
            gw[:, OW_ROWS:CUT].reshape(dim, ff), gw[:, CUT:].reshape(ff, dim),
        )
    return body


def solution(mesh):
    return jax.shard_map(
        body_factory(mesh.shape["dp"], mesh.shape["mp"]),
        mesh=mesh,
        in_specs=(
            P("dp", None, None), P("dp"), P(None, None, "mp"), P("mp", None), P("mp", None),
            P(), P(), P(), P(), P(None, "mp"), P("mp", None), P("dp", None, None),
        ),
        out_specs=(
            P("dp", None, None), P("dp", None, None), P(None, None, "mp"), P("mp", None), P("mp", None),
            P(), P(), P(), P(), P(None, "mp"), P("mp", None),
        ),
        check_vma=False,
    )
```

```python
import functools

import jax
import jax.numpy as jnp
from jax import lax
from jax.experimental import pallas as pl
from jax.experimental.pallas import tpu as pltpu
from jax.sharding import PartitionSpec as P

HD = 64
LM = 64
KSIZE = 33
NS_ITERS = 6
EPS = 1e-5
HI = lax.Precision.HIGHEST
BF = jnp.bfloat16
F32 = jnp.float32
SCALE = HD**-0.5
WIN = 512
BLK = 256
CHUNK = 128
TAP0 = 112
TAP_END = TAP0 + BLK - 1
ROOT_HALF = 0.7071067811865476
INV_ROOT_2PI = 0.3989422804014327
MESH = pl.DeviceIdType.MESH
SLOTS = 8
OW_ROWS, UP_ROWS, DN_ROWS = 24, 96, 96
SLICE = OW_ROWS + UP_ROWS + DN_ROWS
CUT = OW_ROWS + UP_ROWS
GCUT = 112
PARTS = ((0, OW_ROWS), (OW_ROWS, UP_ROWS), (CUT, DN_ROWS))
VM = pl.BlockSpec(memory_space=pltpu.VMEM)
SM = pl.BlockSpec(memory_space=pltpu.SMEM)
ANY = pl.BlockSpec(memory_space=pl.ANY)
DMA = pltpu.SemaphoreType.DMA


def nn(a, b, precision=None):
    return lax.dot_general(a, b, (((1,), (0,)), ((), ())), precision=precision, preferred_element_type=F32)


def nt(a, b, precision=None):
    return lax.dot_general(a, b, (((1,), (1,)), ((), ())), precision=precision, preferred_element_type=F32)


def tn(a, b, precision=None):
    return lax.dot_general(a, b, (((0,), (0,)), ((), ())), precision=precision, preferred_element_type=F32)


def block_mask(width):
    r = lax.broadcasted_iota(jnp.int32, (width, width), 0) // HD
    c = lax.broadcasted_iota(jnp.int32, (width, width), 1) // HD
    return r == c


def identity(width):
    r = lax.broadcasted_iota(jnp.int32, (width, width), 0)
    c = lax.broadcasted_iota(jnp.int32, (width, width), 1)
    return jnp.where(r == c, 1.0, 0.0).astype(F32)


def spread(x, heads, mask):
    return jnp.where(mask, jnp.concatenate([x] * heads, axis=0), 0.0)


def per_head_total(col, heads):
    tot = jnp.sum(col.reshape(heads, HD, 1), axis=1, keepdims=True)
    return jnp.broadcast_to(tot, (heads, HD, 1)).reshape(heads * HD, 1)


def members(length, count):
    s = lax.broadcasted_iota(jnp.int32, (LM, count), 1)
    j = lax.broadcasted_iota(jnp.int32, (LM, count), 0)
    s64 = s * LM
    return (j * length <= s64) & (s64 < (j + 1) * length) & (s < length)


def live_lanes(length, count):
    return lax.broadcasted_iota(jnp.int32, (1, count), 1) < length


def toeplitz(row):
    return pltpu.roll(jnp.broadcast_to(row, (BLK, WIN)), 0, 1, stride=1, stride_axis=0)


def windows(x, seq):
    pad = jnp.zeros((x.shape[0], 128), x.dtype)
    padded = jnp.concatenate([pad, x, pad], axis=1)
    return jnp.concatenate([padded[:, b * BLK : b * BLK + WIN] for b in range(seq // BLK)], axis=0)


def hi_lo(x):
    hi = x.astype(BF)
    return hi, (x - hi.astype(F32)).astype(BF)


def banded(x, row, heads, seq):
    outs = []
    for h in range(heads):
        wins = windows(x[h * HD : (h + 1) * HD], seq)
        hi, lo = hi_lo(toeplitz(row[h : h + 1]))
        y = nt(wins, hi) + nt(wins, lo)
        outs.append(jnp.concatenate([y[b * HD : (b + 1) * HD] for b in range(seq // BLK)], axis=1))
    return jnp.concatenate(outs, axis=0)


def flip(i, bit):
    return i + bit * (1 - 2 * ((i // bit) % 2))


def partner(i, m):
    for bit in (1, 2, 4):
        if m & bit:
            i = flip(i, bit)
    return i


def greet(peers):
    bar = pltpu.get_barrier_semaphore()
    for p in peers:
        pl.semaphore_signal(bar, inc=1, device_id=p, device_id_type=MESH)
    pl.semaphore_wait(bar, len(peers))


def rcopy(src, dst, ss, rs, dev):
    return pltpu.make_async_remote_copy(src_ref=src, dst_ref=dst, send_sem=ss, recv_sem=rs, device_id=dev, device_id_type=MESH)


class Net:
    def __init__(self, ssem, rsem):
        self.ssem, self.rsem, self.n = ssem, rsem, 0
        self.sent = []

    def copy(self, src, dst, dev, late=True):
        i = self.n
        self.n += 1
        c = rcopy(src, dst, self.ssem.at[i], self.rsem.at[i], dev)
        if late:
            self.sent.append(c)
        return c

    def drain(self):
        for c in self.sent:
            c.wait_send()
        self.sent = []


def at(i, steps):
    for k, f in steps.items():

        @pl.when(i == k)
        def _():
            f()


class Local:
    def __init__(self, sem):
        self.sem, self.n, self.open = sem, 0, []

    def start(self, src, dst):
        c = pltpu.make_async_copy(src, dst, self.sem.at[self.n])
        self.n += 1
        c.start()
        self.open.append(c)
        return c

    def finish(self):
        for c in self.open:
            c.wait()
        self.open = []


class Line:
    def __init__(self, parts):
        self.last, self.z = parts - 1, lax.axis_index("mp")

    def sends(self, way, s):
        z = self.z
        return (z < self.last) & (z >= s) if way == 0 else (z > 0) & (z + s <= self.last)

    def gets(self, way, s):
        z = self.z
        return z - 1 >= s if way == 0 else z + 1 + s <= self.last

    def sent_from(self, way, s):
        return self.z - (1 - 2 * way) * s

    def got_from(self, way, s):
        return self.z - (1 - 2 * way) * (s + 1)

    def ahead(self, way):
        size = self.last + 1
        return {"mp": lax.rem(self.z + (1 - 2 * way) + size, size)}


class Gather:
    def __init__(self, mp, srcs, wall, zsem, psem):
        self.line = Line(mp)
        self.srcs, self.wall, self.zsem, self.psem = srcs, wall, zsem, psem
        self.d = lax.axis_index("dp")
        r = lax.rem(self.d, SLOTS)
        self.rs = (r, flip(r, 4), flip(r, 2), partner(r, 6))
        self.steps = mp - 1

    def z(self, way, s, origin):
        dev = self.line.ahead(way)
        r = self.rs[0]
        out = []
        for i, (lo, size) in enumerate(PARTS):
            dst = self.wall.at[origin, r, pl.ds(lo, size)]
            src = self.srcs[i].at[r] if s == 0 else dst
            out.append(rcopy(src, dst, self.zsem.at[0, way, s, i], self.zsem.at[1, way, s, i], dev))
        return out

    def plane(self, way, s, k):
        w = self.wall.at[self.line.got_from(way, s)]
        q, rows, bit = (
            (0, (0, SLICE), 4),
            (0, (0, SLICE), 2),
            (1, (0, CUT), 2),
            (2, (CUT, DN_ROWS), 4),
            (0, (0, SLICE), 1),
            (1, (0, SLICE), 1),
            (2, (0, SLICE), 1),
            (3, (0, SLICE), 1),
        )[k]
        ref = w.at[self.rs[q], pl.ds(*rows)]
        return rcopy(ref, ref, self.psem.at[0, way, s, k], self.psem.at[1, way, s, k], {"dp": flip(self.d, bit)})

    def send(self, s):
        for way in range(2):

            @pl.when(self.line.sends(way, s))
            def _():
                for c in self.z(way, s, self.line.sent_from(way, s)):
                    c.start()

    def got(self, s, f):
        for way in range(2):
            pl.when(self.line.gets(way, s))(functools.partial(f, way, s))

    def step1(self, s):
        def arrive(way, s):
            for c in self.z(way, s, self.line.got_from(way, s)):
                c.wait_recv()

        self.got(s, arrive)
        if s + 1 < self.steps:
            self.send(s + 1)

        def pass_on(way, s):
            for k in (0, 1, 4):
                self.plane(way, s, k).start()

        self.got(s, pass_on)

    def step2(self, s):
        def f(way, s):
            self.plane(way, s, 0).wait_recv()
            self.plane(way, s, 2).start()
            self.plane(way, s, 5).start()
            self.plane(way, s, 1).wait_recv()
            self.plane(way, s, 3).start()
            self.plane(way, s, 6).start()

        self.got(s, f)

    def step3(self, s):
        def f(way, s):
            self.plane(way, s, 2).wait_recv()
            self.plane(way, s, 3).wait_recv()
            self.plane(way, s, 7).start()

        self.got(s, f)

    def finish(self):
        def f(way, s):
            for k in range(8):
                if k >= 4:
                    self.plane(way, s, k).wait_recv()
                self.plane(way, s, k).wait_send()

        for s in range(self.steps):
            self.got(s, f)
            for way in range(2):

                @pl.when(self.line.sends(way, s))
                def _():
                    for c in self.z(way, s, self.line.sent_from(way, s)):
                        c.wait_send()


def attn_fwd_kernel(docs, heads, seq, dest, len_ref, x_hbm, wt_ref, taps_ref, ow_ref, up_ref, dn_ref,
                    qkv_hbm, ctx_ref, lq_hbm, lk_hbm, sum_hbm, mix_hbm, k2_hbm, z_hbm, p_hbm, l1_ref, l3_ref, wall_ref,
                    x_s, qkv_s, lq_s, lk_s, sum_s, mix_s, k2_s, z_s, p_s, ctx_s, taps_s, lsem, asem, zsem, psem):
    width = heads * HD
    me, dd = lax.axis_index("mp"), lax.axis_index("dp")
    local = Local(lsem)
    loads = [local.start(x_hbm.at[d], x_s.at[d]) for d in range(docs)]
    local.open = []
    greet([{"mp": partner(me, m)} for m in range(1, dest)] + [{"dp": flip(dd, b)} for b in (1, 2, 4)])
    gather = Gather(dest, (ow_ref, up_ref, dn_ref), wall_ref, zsem, psem)
    gather.send(0)

    def a_copy(m, d):
        return rcopy(ctx_s.at[partner(me, m), d], ctx_ref.at[me, d], asem.at[0, m - 1, d], asem.at[1, m - 1, d], {"mp": partner(me, m)})

    taps_s[...] = jnp.zeros_like(taps_s)
    taps_s[:, TAP0 : TAP0 + KSIZE] = taps_ref[...]
    mask = block_mask(width)
    eye = identity(width)
    for c in loads:
        c.wait()

    def project(i, _):
        d, c = i // (seq // BLK), lax.rem(i, seq // BLK)
        rows = pl.ds(pl.multiple_of(c * BLK, BLK), BLK)
        qkv_s[d, :, rows] = nt(wt_ref[...], x_s[d, rows, :]).astype(BF)
        return 0

    lax.fori_loop(0, docs * (seq // BLK), project, 0)
    local.start(qkv_s, qkv_hbm)

    def landmarks(d, _):
        length = len_ref[d]
        memb = jnp.where(members(length, seq), 1.0, 0.0).astype(F32)
        counts = jnp.maximum(jnp.sum(memb, axis=1, keepdims=True), 1.0)
        memb_b = memb.astype(BF)
        q = qkv_s[d, 0:width, :]
        k = qkv_s[d, width : 2 * width, :]
        v = qkv_s[d, 2 * width : 3 * width, :]
        lq = spread(nt(memb_b, q) / counts, heads, mask).astype(BF)
        lk = spread(nt(memb_b, k) / counts, heads, mask).astype(BF)
        lq_s[d] = lq
        lk_s[d] = lk
        s2 = jnp.where(mask, nt(lq, lk) * SCALE, -1e30)
        e2 = jnp.where(mask, jnp.exp(s2 - jnp.max(s2, axis=1, keepdims=True)), 0.0)
        k2_s[d] = e2 / jnp.sum(e2, axis=1, keepdims=True)
        s3 = jnp.where(live_lanes(length, seq), nn(lq, k) * SCALE, -1e30)
        m3 = jnp.max(s3, axis=1, keepdims=True)
        e3 = jnp.exp(s3 - m3)
        t3 = jnp.sum(e3, axis=1, keepdims=True)
        l3_ref[d] = jnp.broadcast_to(m3 + jnp.log(t3), (width, 128))
        k3 = (e3 / t3).astype(BF)
        sum_s[d] = jnp.where(mask, nt(k3, v), 0.0)
        at(d, {0: lambda: gather.step1(0)})
        return 0

    lax.fori_loop(0, docs, landmarks, 0)
    for src, dst in ((lq_s, lq_hbm), (lk_s, lk_hbm), (k2_s, k2_hbm), (sum_s, sum_hbm)):
        local.start(src, dst)
    for d in range(docs):
        k2 = k2_s[d]
        z_s[d, 0] = k2.T / per_head_total(jnp.sum(k2 * k2, axis=1, keepdims=True), heads)

    def newton(i, _):
        k2s = [k2_s[d] for d in range(docs)]
        zs = [z_s[d, i] for d in range(docs)]
        ps = [nn(k2s[d], zs[d], HI) for d in range(docs)]
        bs = [15.0 * eye - nn(ps[d], 7.0 * eye - ps[d], HI) for d in range(docs)]
        cs = [13.0 * eye - nn(ps[d], bs[d], HI) for d in range(docs)]
        zs = [0.25 * nn(zs[d], cs[d], HI) for d in range(docs)]
        for d in range(docs):
            p_s[d, i, 0] = ps[d]
            p_s[d, i, 1] = bs[d]
            p_s[d, i, 2] = cs[d]
            z_s[d, i + 1] = zs[d]
        at(i, {1: lambda: gather.step1(1), 2: lambda: gather.step2(0), 3: lambda: (gather.step3(0), gather.step1(2)), 4: lambda: gather.step2(1), 5: lambda: gather.step3(1)})
        return 0

    lax.fori_loop(0, NS_ITERS, newton, 0)
    local.start(z_s, z_hbm)
    local.start(p_s, p_hbm)
    part = seq // dest

    def contexts(d, _):
        length = len_ref[d]
        q = qkv_s[d, 0:width, :]
        v = qkv_s[d, 2 * width : 3 * width, :]
        live = live_lanes(length, seq)
        mix = jnp.where(mask, nn(z_s[d, NS_ITERS], sum_s[d], HI), 0.0)
        mix_s[d] = mix.astype(BF)
        s1 = (nn(lk_s[d], q) * SCALE).reshape(heads, LM, seq)
        m1 = jnp.max(s1, axis=1, keepdims=True)
        e1 = jnp.exp(s1 - m1)
        t1 = jnp.sum(e1, axis=1, keepdims=True)
        l1_ref[d] = (m1 + jnp.log(t1)).reshape(heads, seq)
        k1 = (e1 / t1).reshape(width, seq).astype(BF)
        vl = jnp.where(live, v, 0).astype(BF)
        ctx = nn(mix.T.astype(BF), k1) + banded(vl, taps_s[...], heads, seq)
        ctx = jnp.where(live, ctx, 0.0).astype(BF)
        for i in range(dest):
            ctx_s[i, d] = ctx[:, i * part : (i + 1) * part]
        for m in range(1, dest):
            a_copy(m, d).start()
        ctx_ref[me, d] = ctx_s[me, d]
        at(d, {0: lambda: gather.step2(2)})
        return 0

    lax.fori_loop(0, docs, contexts, 0)
    local.start(mix_s, mix_hbm)
    gather.step3(2)
    gather.finish()
    for d in range(docs):
        for m in range(1, dest):
            a_copy(m, d).wait()
    local.finish()


def attn_fwd(lengths, x, wt, taps, ow, up, dn, dest):
    docs, seq, dim = x.shape
    width = wt.shape[0] // 3
    heads = width // HD
    sds = jax.ShapeDtypeStruct
    kept = [
        sds((docs, 3 * width, seq), BF),
        sds((docs, width, width), BF),
        sds((docs, width, width), BF),
        sds((docs, width, width), F32),
        sds((docs, width, width), BF),
        sds((docs, width, width), F32),
        sds((docs, NS_ITERS + 1, width, width), F32),
        sds((docs, NS_ITERS, 3, width, width), F32),
    ]
    out = [kept[0], sds((dest, docs, width, seq // dest), BF)] + kept[1:] + [
        sds((docs, heads, seq), F32),
        sds((docs, width, 128), F32),
        sds((dest, SLOTS, SLICE, dim), BF),
    ]
    return pl.pallas_call(
        functools.partial(attn_fwd_kernel, docs, heads, seq, dest),
        out_shape=out,
        in_specs=[SM, ANY, VM, VM, ANY, ANY, ANY],
        out_specs=[ANY, VM] + [ANY] * 7 + [VM, VM, ANY],
        scratch_shapes=[pltpu.VMEM((docs, seq, dim), BF)]
        + [pltpu.VMEM(t.shape, t.dtype) for t in kept]
        + [
            pltpu.VMEM((dest, docs, width, seq // dest), BF),
            pltpu.VMEM((heads, WIN), F32),
            DMA((16,)),
            DMA((2, dest - 1, docs)),
            DMA((2, 2, dest - 1, 3)),
            DMA((2, 2, dest - 1, 8)),
        ],
        compiler_params=pltpu.CompilerParams(vmem_limit_bytes=60 * 2**20, collective_id=0, has_side_effects=True),
        cost_estimate=pl.CostEstimate(flops=int(8e9), bytes_accessed=int(3e7), transcendentals=0),
        name="attn_fwd",
    )(lengths, x, wt, taps, ow, up, dn)


def ln_stats(v):
    mu = jnp.mean(v, axis=-1, keepdims=True)
    cen = v - mu
    var = jnp.mean(cen * cen, axis=-1, keepdims=True)
    r = lax.rsqrt(var + EPS)
    return cen * r, r


def ln_back(g, xhat, r):
    m1 = jnp.mean(g, axis=-1, keepdims=True)
    m2 = jnp.mean(g * xhat, axis=-1, keepdims=True)
    return r * (g - m1 - xhat * m2)


class Spread:
    def __init__(self, parts, buf, sem):
        self.line, self.buf, self.sem = Line(parts), buf, sem

    def one(self, way, s, d, origin, src=None):
        dst = self.buf.at[d, origin]
        return rcopy(dst if src is None else src, dst, self.sem.at[way, 0, s, d], self.sem.at[way, 1, s, d], self.line.ahead(way))

    def start(self, s, d, src=None):
        for way in range(2):

            @pl.when(self.line.sends(way, s))
            def _():
                self.one(way, s, d, self.line.sent_from(way, s), src).start()

    def wait(self, s, d):
        for way in range(2):

            @pl.when(self.line.gets(way, s))
            def _():
                self.one(way, s, d, self.line.got_from(way, s)).wait_recv()

    def sent(self, s, d, src=None):
        for way in range(2):

            @pl.when(self.line.sends(way, s))
            def _():
                self.one(way, s, d, self.line.sent_from(way, s), src).wait_send()


def ffn_kernel(groups, docs, rows, len_ref, x_hbm, cot_hbm, ctx_ref, ow_hbm, up_hbm, dn_hbm, wall_hbm, g1_ref, b1_ref, g2_ref, b2_ref,
               out_hbm, gmix_ref, gctx_ref, s1_hbm, small_ref,
               x_s, cot_s, w_s, rc_s, gc_s, nb_s, fac_s, act_s, gp_s, br_s, x1_s, gn_s, ga_s, o_s, s1_s, lsem, csem, osem, asem):
    n = docs * rows
    dim = x_s.shape[-1]
    z, dd = lax.axis_index("mp"), lax.axis_index("dp")
    kk = lax.rem(dd, 2)
    local = Local(lsem)
    mine = pl.ds(pl.multiple_of(z * rows, rows), rows)
    others = [partner(z, m) for m in range(1, groups)]
    heads_first = [local.start(ow_hbm, w_s.at[z, :, :, pl.ds(*PARTS[0])])]
    heads_first += [local.start(wall_hbm.at[g, :, :, pl.ds(*PARTS[0])], w_s.at[g, :, :, pl.ds(*PARTS[0])]) for g in others]
    heads_first += [local.start(x_hbm.at[d, mine], x_s.at[pl.ds(d * rows, rows)]) for d in range(docs)]
    rest = [local.start(up_hbm, w_s.at[z, :, :, pl.ds(*PARTS[1])]), local.start(dn_hbm, w_s.at[z, :, :, pl.ds(*PARTS[2])])]
    body = pl.ds(OW_ROWS, SLICE - OW_ROWS)
    rest += [local.start(wall_hbm.at[g, :, :, body], w_s.at[g, :, :, body]) for g in others]
    rest += [local.start(cot_hbm.at[d, mine], cot_s.at[pl.ds(d * rows, rows)]) for d in range(docs)]
    local.open = []
    greet([{"mp": partner(z, m)} for m in range(1, groups)] + [{"dp": flip(dd, 1)}])

    def back_copy(m, d):
        return rcopy(gc_s.at[m - 1, d], gctx_ref.at[z, d], asem.at[0, m - 1, d], asem.at[1, m - 1, d], {"mp": partner(z, m)})

    spread_out = Spread(groups, out_hbm, osem)

    def core_copy(g, part):
        lo, size = ((OW_ROWS, SLICE - OW_ROWS), (0, OW_ROWS))[part]
        return rcopy(w_s.at[g, :, 1 - kk, pl.ds(lo, size)], rc_s.at[g, :, pl.ds(lo, size)], csem.at[0, g, part], csem.at[1, g, part], {"dp": flip(dd, 1)})

    def take(g, part):
        lo, size = PARTS[part]
        return w_s[g, :, :, lo : lo + size, :].reshape(SLOTS * size, dim)

    def put(g, part, val):
        lo, size = PARTS[part]
        w_s[g, :, :, lo : lo + size, :] = val.astype(BF).reshape(SLOTS // 2, 2, size, dim)

    first = z * rows
    gain1, bias1 = g1_ref[...].reshape(1, dim), b1_ref[...].reshape(1, dim)
    gain2, bias2 = g2_ref[...].reshape(1, dim), b2_ref[...].reshape(1, dim)
    for c in heads_first:
        c.wait()
    small_ref[...] = jnp.zeros_like(small_ref)

    def doc(d, _):
        here = pl.ds(pl.multiple_of(d * rows, rows), rows)
        live = (lax.broadcasted_iota(jnp.int32, (rows, 1), 0) + first < len_ref[d]).astype(F32)
        mixed = x_s[here].astype(F32)
        for g in range(groups):
            mixed = mixed + tn(ctx_ref[g, d], take(g, 0)).astype(BF).astype(F32)
        xh1, r1 = ln_stats(mixed)
        x1_s[...] = xh1
        normed = xh1 * gain1 + bias1
        nb_s[here] = normed.astype(BF)
        br_s[...] = normed

        @pl.when(d == 0)
        def _():
            for c in rest:
                c.wait()

        def fwd_group(g, _):
            h = nn(nb_s[here], take(g, 1))
            phi_big = 0.5 * (1.0 + lax.erf(h * ROOT_HALF))
            act = (h * phi_big).astype(BF)
            act_s[g, here] = act
            fac_s[g] = phi_big + h * (jnp.exp(-0.5 * h * h) * INV_ROOT_2PI)
            br_s[...] += nn(act, take(g, 2)).astype(BF).astype(F32)
            return 0

        lax.fori_loop(0, groups, fwd_group, 0)
        xh2, r2 = ln_stats(br_s[...])
        o_s[d] = (live * (xh2 * gain2 + bias2)).astype(BF)

        @pl.when(d == 0)
        def _():
            spread_out.start(0, 0, o_s.at[0])

        g_out = live * cot_s[here].astype(F32)
        gg2 = jnp.sum(g_out * xh2, axis=0, keepdims=True)
        gb2 = jnp.sum(g_out, axis=0, keepdims=True)
        g_res = ln_back(g_out * gain2, xh2, r2)
        gn_s[...] = g_res
        gbr_s[here] = g_res.astype(BF)

        def back_group(g, _):
            g_pre = (nt(gbr_s[here], take(g, 2)) * fac_s[g]).astype(BF)
            gp_s[g, here] = g_pre
            gn_s[...] += nt(g_pre, take(g, 1))
            return 0

        lax.fori_loop(0, groups, back_group, 0)
        g_n = gn_s[...]
        xh1 = x1_s[...]
        gg1 = jnp.sum(g_n * xh1, axis=0, keepdims=True)
        gb1 = jnp.sum(g_n, axis=0, keepdims=True)
        small_ref[...] += jnp.concatenate([gg1, gb1, gg2, gb2, jnp.zeros((4, dim), F32)], axis=0)
        g_mix = ln_back(g_n * gain1, xh1, r1)
        gmix_ref[d] = g_mix
        g_att = g_mix.astype(BF)
        ga_s[here] = g_att
        for m in reversed(range(groups)):
            t = nt(take(partner(z, m), 0), g_att).astype(BF)
            if m:
                gc_s[m - 1, d] = t
                back_copy(m, d).start()
            else:
                gctx_ref[z, d] = t
        return 0

    gbr_s = cot_s
    lax.fori_loop(0, docs, doc, 0)
    for d in range(docs):
        local.start(o_s.at[d], out_hbm.at[d, z])

    def weight_group(g, _):
        put(g, 2, tn(act_s[g], gbr_s[...]))
        put(g, 1, tn(nb_s[...], gp_s[g]))
        core_copy(g, 0).start()
        return 0

    lax.fori_loop(0, groups, weight_group, 0)
    for g in range(groups):
        acc = None
        for d in range(docs):
            t = nn(ctx_ref[g, d], ga_s[d * rows : (d + 1) * rows])
            acc = t if acc is None else acc + t
        put(g, 0, acc)
        core_copy(g, 1).start()

    def add_group(g, _):
        core_copy(g, 0).wait_recv()
        core_copy(g, 1).wait_recv()

        def add_slot(j, _):
            s1_s[g, j // 2, j % 2] = (w_s[g, j, kk].astype(F32) + rc_s[g, j].astype(F32)).astype(BF)
            return 0

        lax.fori_loop(0, SLOTS // 2, add_slot, 0)
        return 0

    lax.fori_loop(0, groups, add_group, 0)
    local.start(s1_s, s1_hbm)
    for m in range(1, groups):
        for d in range(docs):
            back_copy(m, d).wait()
    spread_out.wait(0, 0)
    spread_out.sent(0, 0, o_s.at[0])
    for g in range(groups):
        for part in range(2):
            core_copy(g, part).wait_send()
    local.finish()


def ffn(lengths, x, cot, ctx, ow, up, dn, wall, g1, b1, g2, b2):
    docs, seq, dim = x.shape
    groups, _, width, rows = ctx.shape
    ff = SLOTS * UP_ROWS
    n = docs * rows
    sds = jax.ShapeDtypeStruct
    out = [
        sds((docs, groups, rows, dim), BF),
        sds((docs, rows, dim), F32),
        sds((groups, docs, width, rows), BF),
        sds((groups, 2, 2, SLICE, dim), BF),
        sds((8, dim), F32),
    ]
    wall = wall.reshape(groups, SLOTS // 2, 2, SLICE, dim)
    ow, up, dn = (t.reshape(SLOTS // 2, 2, -1, dim) for t in (ow, up, dn))
    return pl.pallas_call(
        functools.partial(ffn_kernel, groups, docs, rows),
        out_shape=out,
        in_specs=[SM, ANY, ANY, VM, ANY, ANY, ANY, ANY, VM, VM, VM, VM],
        out_specs=[ANY, VM, VM, ANY, VM],
        scratch_shapes=[
            pltpu.VMEM((n, dim), BF),
            pltpu.VMEM((n, dim), BF),
            pltpu.VMEM((groups, SLOTS // 2, 2, SLICE, dim), BF),
            pltpu.VMEM((groups, SLOTS // 2, SLICE, dim), BF),
            pltpu.VMEM((groups - 1, docs, width, rows), BF),
            pltpu.VMEM((n, dim), BF),
            pltpu.VMEM((groups, rows, ff), F32),
            pltpu.VMEM((groups, n, ff), BF),
            pltpu.VMEM((groups, n, ff), BF),
            pltpu.VMEM((rows, dim), F32),
            pltpu.VMEM((rows, dim), F32),
            pltpu.VMEM((rows, dim), F32),
            pltpu.VMEM((n, dim), BF),
            pltpu.VMEM((docs, rows, dim), BF),
            pltpu.VMEM((groups, 2, 2, SLICE, dim), BF),
            DMA((24,)),
            DMA((2, groups, 2)),
            DMA((2, 2, groups - 1, docs)),
            DMA((2, groups - 1, docs)),
        ],
        compiler_params=pltpu.CompilerParams(vmem_limit_bytes=62 * 2**20, collective_id=1, has_side_effects=True),
        cost_estimate=pl.CostEstimate(flops=int(1.8e10), bytes_accessed=int(4e7), transcendentals=0),
        name="ffn",
    )(lengths, x, cot, ctx, ow, up, dn, wall, g1, b1, g2, b2)


def attn_bwd_kernel(docs, heads, seq, parts, dp, len_ref, x_hbm, wt_ref, taps_ref, qkv_ref, gctx_ref, lq_ref, lk_ref, sum_ref, mix_ref, k2_ref,
                    z_hbm, p_hbm, l1_ref, l3_ref, s1, small_in, gmix_hbm, out_in, gq, ig, taps_out, gw, small, out_hbm,
                    x_s, z_s, p_s, gmix_s, g_s, gs1_s, gs3_s, ginv_s, glq_s, glk_s, gz_s, gk_s, taps_s, gacc_s,
                    ipart, ri, ra1, rb1, rz, fin, rfin, rq0, rq1, rq2, gqb, q, rsm, rtp, lsem, ssem, rsem, isem, osem, pz, acc, gsem):
    width = heads * HD
    nblk = seq // BLK
    dim = x_s.shape[-1]
    zi = lax.axis_index("mp")
    local = Local(lsem)
    loads = [local.start(a, b) for a, b in ((z_hbm, z_s), (p_hbm, p_s), (x_hbm, x_s), (gmix_hbm, gmix_s))]
    local.open = []
    nd = Sums(docs, seq, parts, dp, locals())
    nd.begin()
    out = Spread(parts, out_hbm, osem)
    left = [(s, d) for s in range(parts - 1) for d in range(docs) if (s, d) != (0, 0)]
    waves = [[(0, d) for d in range(1, docs)] + [(1, 0)]]
    waves += [[(s, d) for d in range(1, docs)] + [(s + 1, 0)] for s in range(1, parts - 2)] + [[(parts - 2, d) for d in range(1, docs)]]

    def out_step(i):
        for s, d in waves[i] if i < len(waves) else ():
            if s > 0 and (s - 1, d) != (0, 0):
                out.wait(s - 1, d)
            out.start(s, d)

    out_step(0)
    taps_s[...] = jnp.zeros_like(taps_s)
    taps_s[:, TAP0 : TAP0 + KSIZE] = taps_ref[...]
    mask = block_mask(width)
    eye = identity(width)
    anti = jnp.where(
        lax.broadcasted_iota(jnp.int32, (BLK, BLK), 0) + lax.broadcasted_iota(jnp.int32, (BLK, BLK), 1) == BLK - 1, 1.0, 0.0
    ).astype(BF)
    gacc_s[...] = jnp.zeros_like(gacc_s)

    def doc(d, _):
        length = len_ref[d]
        live = live_lanes(length, seq)
        q_ = qkv_ref[d, 0:width, :]
        k = qkv_ref[d, width : 2 * width, :]
        v = qkv_ref[d, 2 * width : 3 * width, :]
        gc = jnp.concatenate([gctx_ref[i, d] for i in range(parts)], axis=1)
        gc = jnp.where(live, gc, 0).astype(BF)
        lq, lk = lq_ref[d], lk_ref[d]
        s1_ = (nn(lk, q_) * SCALE).reshape(heads, LM, seq)
        k1 = jnp.exp(s1_ - l1_ref[d].reshape(heads, 1, seq))
        gmixing = jnp.where(mask, nt(k1.reshape(width, seq).astype(BF), gc), 0.0)
        gk1 = nn(mix_ref[d], gc).reshape(heads, LM, seq)
        gs1 = (k1 * (gk1 - jnp.sum(gk1 * k1, axis=1, keepdims=True))).reshape(width, seq).astype(BF)
        gz_s[d] = nt(gmixing, sum_ref[d], HI)
        gk_s[d] = jnp.zeros((width, width), F32)
        gsum = jnp.where(mask, tn(ginv_s[d], gmixing, HI), 0.0)
        gsum_b = gsum.astype(BF)
        s3 = jnp.where(live, nn(lq, k) * SCALE, -1e30)
        k3 = jnp.exp(s3 - l3_ref[d][:, 0:1])
        gk3 = nn(gsum_b, v)
        gs3 = (k3 * (gk3 - jnp.sum(gk3 * k3, axis=1, keepdims=True))).astype(BF)
        glq_s[d] = jnp.where(mask, nt(gs3, k), 0.0) * SCALE
        glk_s[d] = jnp.where(mask, nt(gs1, q_), 0.0) * SCALE
        gs1_s[d] = gs1
        gs3_s[d] = gs3
        gv = nn(gsum.T.astype(BF), k3.astype(BF))
        gvl = banded(gc, taps_s[...], heads, seq)
        g_s[d, 2 * width : 3 * width, :] = (gv + jnp.where(live, gvl, 0.0)).astype(BF)
        vl = jnp.where(live, v, 0).astype(BF)
        for h in range(heads):
            wins = windows(vl[h * HD : (h + 1) * HD], seq)
            gch = gc[h * HD : (h + 1) * HD]
            stack = jnp.concatenate([gch[:, b * BLK : (b + 1) * BLK] for b in range(nblk)], axis=0)
            gacc_s[h] += nn(nt(anti, stack).astype(BF), wins)
        at(d, {i: functools.partial(nd.small_step, 1 + i) for i in range(docs)})
        return 0

    loads[0].wait()
    for d in range(docs):
        ginv_s[d] = z_s[d, NS_ITERS]
    lax.fori_loop(0, docs, doc, 0)
    out_step(1)
    for h in range(heads):
        rolled = pltpu.roll(gacc_s[h], 0, 1, stride=1, stride_axis=0)
        taps_out[h : h + 1, :] = jnp.sum(rolled, axis=0, keepdims=True)
    loads[1].wait()

    def newton_back(j, _):
        i = NS_ITERS - 1 - j
        for d in range(docs):
            z, p, b, c = z_s[d, i], p_s[d, i, 0], p_s[d, i, 1], p_s[d, i, 2]
            a = 7.0 * eye - p
            g = 0.25 * gz_s[d]
            gc_ = tn(z, g, HI)
            gp = -nt(gc_, b, HI)
            gb = -tn(p, gc_, HI)
            gp = gp - nt(gb, a, HI)
            ga = -tn(p, gb, HI)
            gp = gp - ga
            gk_s[d] += nt(gp, z, HI)
            gz_s[d] = nt(g, c, HI) + tn(k2_ref[d], gp, HI)
        base = 1 + docs
        at(j, {
            1: lambda: (nd.small_step(base), nd.taps_step(0)),
            3: lambda: (nd.small_step(base + 1), nd.taps_step(1), nd.g_step1()),
            5: lambda: (nd.small_step(base + 2), nd.taps_step(2), out_step(2)),
        })
        return 0

    lax.fori_loop(0, NS_ITERS, newton_back, 0)
    for c in loads[2:]:
        c.wait()

    def finish(d, _):
        length = len_ref[d]
        k2 = k2_ref[d]
        tot = per_head_total(jnp.sum(k2 * k2, axis=1, keepdims=True), heads)
        g = gz_s[d]
        dot = per_head_total(jnp.sum(g * k2.T, axis=1, keepdims=True), heads)
        gk2 = gk_s[d] + (g / tot).T - k2 * (2.0 * dot / (tot * tot))
        gs2 = k2 * (gk2 - jnp.sum(gk2 * k2, axis=1, keepdims=True)) * SCALE
        memb = jnp.where(members(length, seq), 1.0, 0.0).astype(F32)
        counts = jnp.maximum(jnp.sum(memb, axis=1, keepdims=True), 1.0)
        counts = jnp.concatenate([counts] * heads, axis=0)
        memb3 = jnp.concatenate([memb.astype(BF)] * heads, axis=0)
        lq, lk = lq_ref[d].astype(F32), lk_ref[d].astype(F32)
        glq = (glq_s[d] + nn(gs2, lk, HI)) / counts
        glk = (glk_s[d] + tn(gs2, lq, HI)) / counts
        hi, lo = hi_lo(glq.T)
        gq_ = nn(lk.T.astype(BF), gs1_s[d]) * SCALE + nn(hi, memb3) + nn(lo, memb3)
        hi, lo = hi_lo(glk.T)
        gk_ = nn(lq.T.astype(BF), gs3_s[d]) * SCALE + nn(hi, memb3) + nn(lo, memb3)
        g_s[d, 0:width, :] = gq_.astype(BF)
        g_s[d, width : 2 * width, :] = gk_.astype(BF)

        def inputs(c, _):
            rows = pl.ds(pl.multiple_of(c * BLK, BLK), BLK)
            t = tn(g_s[d, :, rows], wt_ref[...])
            t = (t + jnp.where(zi == c, 1.0, 0.0) * gmix_s[d]).astype(BF)
            per = BLK // CHUNK
            ipart[d, pl.ds(c * per, per)] = t.reshape(per, CHUNK, dim)
            return 0

        lax.fori_loop(0, nblk, inputs, 0)
        return 0

    lax.fori_loop(0, docs, finish, 0)
    for i in range(3, len(waves)):
        out_step(i)
    nd.i_time(0)

    def weights(c, _):
        rows = pl.ds(pl.multiple_of(c * width, width), width)
        acc_q = nn(g_s[0, rows], x_s[0])
        for d in range(1, docs):
            acc_q = acc_q + nn(g_s[d, rows], x_s[d])
        gqb[rows] = acc_q.astype(BF)
        return 0

    lax.fori_loop(0, 3, weights, 0)
    nd.tail()
    for s, d in left:
        if s == parts - 2:
            out.wait(s, d)
    for s, d in left:
        out.sent(s, d)


class Sums:
    def __init__(self, docs, seq, parts, dp, refs):
        for name in ("pz", "acc", "gsem", "s1", "small_in", "gq", "ig", "taps_out", "gw", "small", "ipart", "ri", "ra1", "rb1", "rz", "fin", "rfin", "rq0", "rq1", "rq2", "gqb", "q", "rsm", "rtp", "ssem", "rsem", "isem"):
            setattr(self, name, refs[name])
        self.docs, self.parts = docs, parts
        self.z, self.d = lax.axis_index("mp"), lax.axis_index("dp")
        self.r = lax.rem(self.d, SLOTS)
        self.y, self.x, self.k = self.r // 4, lax.rem(self.r // 2, 2), lax.rem(self.r, 2)
        self.net = Net(self.ssem, self.rsem)
        self.extra = [b for b in (8, 16, 32, 64, 128) if b < dp]
        self.bits = [1, 2, 4] + self.extra

    def dev(self, bit):
        return {"dp": flip(self.d, bit)}

    def zdev(self, m):
        return {"mp": partner(self.z, m)}

    def begin(self):
        greet([self.zdev(m) for m in range(1, self.parts)] + [self.dev(b) for b in self.bits])
        self.i_setup()
        self.line = Line(self.parts)
        c = self.net.copy
        low, high = pl.ds(0, GCUT), pl.ds(GCUT, SLICE - GCUT)
        self.a1 = c(self.s1.at[:, 1 - self.y, :, low], self.ra1, self.dev(4))
        self.b1 = c(self.s1.at[:, :, 1 - self.x, high], self.rb1, self.dev(2))
        self.a1.start()
        self.b1.start()
        self.a2 = c(self.ra1.at[:, 1 - self.x], self.pz.at[:, low], self.dev(2))
        self.b2 = c(self.rb1.at[:, 1 - self.y], self.pz.at[:, high], self.dev(4))
        r, gw = self.r, self.gw
        r4, r2, r6 = flip(r, 4), flip(r, 2), partner(r, 6)
        self.gy = c(gw.at[r], gw.at[r], self.dev(4))
        self.gx = c(gw.at[r], gw.at[r], self.dev(2))
        self.gyx = c(gw.at[r4, low], gw.at[r4, low], self.dev(2))
        self.gxy = c(gw.at[r2, high], gw.at[r2, high], self.dev(4))
        self.gc = [c(gw.at[i], gw.at[i], self.dev(1)) for i in (r, r4, r2, r6)]
        h = self.gqb.shape[0] // 2
        self.half = h
        mine, other = (pl.ds(pl.multiple_of(k * h, 8), h) for k in (self.k, 1 - self.k))
        self.mine = mine
        self.q0 = c(self.gqb.at[other], self.rq0, self.dev(1))
        self.qa = self.q_pair(self.rq1, 4, 2)
        self.qb = self.q_pair(self.rq2.at[0], 2, 4)
        self.qc = c(self.gq.at[mine], self.gq.at[mine], self.dev(1))
        self.extras = [(c(self.fin, self.rfin.at[i], self.dev(b), late=False), c(self.q, self.rq2.at[1 + i], self.dev(b), late=False)) for i, b in enumerate(self.extra)]
        self.small[...] = self.small_in[...]
        zs = [self.zdev(1 << j) for j in range(self.parts.bit_length() - 1)]
        self.smalls = [c(self.small, self.rsm.at[i], dev, late=False) for i, dev in enumerate([self.dev(b) for b in self.bits] + zs)]
        self.tapsums = [c(self.taps_out, self.rtp.at[i], self.dev(b), late=False) for i, b in enumerate(self.bits)]
        self.small_step(0)

    def exchange(self, copies, buf, recv, i):
        if 0 < i <= len(copies):
            copies[i - 1].wait()
            buf[...] = buf[...] + recv[i - 1]
        if i < len(copies):
            copies[i].start()

    def small_step(self, i):
        self.exchange(self.smalls, self.small, self.rsm, i)

    def taps_step(self, i):
        self.exchange(self.tapsums, self.taps_out, self.rtp, i)

    def double(self, c, buf, recv):
        c.start()
        c.wait()
        buf[...] = (buf[...].astype(F32) + recv[...].astype(F32)).astype(buf.dtype)

    def g_step1(self):
        self.a1.wait_recv()
        self.b1.wait_recv()

        def add(i, _):
            g, j = i // 2, i % 2
            self.ra1[g, j] = (self.ra1[g, j].astype(F32) + self.s1[g, self.y, j, 0:GCUT].astype(F32)).astype(BF)
            self.rb1[g, j] = (self.rb1[g, j].astype(F32) + self.s1[g, j, self.x, GCUT:SLICE].astype(F32)).astype(BF)
            return 0

        lax.fori_loop(0, 2 * self.parts, add, 0)
        self.a2.start()
        self.b2.start()

    def g_step2(self):
        self.a2.wait_recv()
        self.b2.wait_recv()

        def add(g, _):
            self.pz[g, 0:GCUT] = (self.pz[g, 0:GCUT].astype(F32) + self.ra1[g, self.x].astype(F32)).astype(BF)
            self.pz[g, GCUT:SLICE] = (self.pz[g, GCUT:SLICE].astype(F32) + self.rb1[g, self.y].astype(F32)).astype(BF)
            return 0

        lax.fori_loop(0, self.parts, add, 0)
        self.z_hop(0)

    def z_piece(self, way, s):
        last = self.parts - 1
        g = last - s + self.z if way == 0 else s - last + self.z
        return g, (self.z <= s) & (self.z < last) if way == 0 else (last - self.z <= s) & (self.z > 0)

    def z_copy(self, way, s, g):
        return rcopy(self.pz.at[g], self.rz.at[way, s], self.gsem.at[0, way, s], self.gsem.at[1, way, s], self.line.ahead(way))

    def z_hop(self, s):
        last = self.parts - 1
        for way in range(2):
            g, ok = self.z_piece(way, s)
            inner = self.z > 0 if way == 0 else self.z < last

            if s > 0:

                @pl.when(ok & inner)
                def _():
                    self.z_copy(way, s - 1, 0).wait_recv()
                    self.pz[g] = (self.pz[g].astype(F32) + self.rz[way, s - 1].astype(F32)).astype(BF)

            @pl.when(ok)
            def _():
                self.z_copy(way, s, g).start()

    def z_done(self):
        last = self.parts - 1
        for way in range(2):
            for s in range(last):
                g, ok = self.z_piece(way, s)

                @pl.when(ok)
                def _():
                    self.z_copy(way, s, g).wait_send()

    def g_step3(self):
        last = self.parts - 1
        self.acc[...] = self.pz[self.z].astype(F32)
        for way in range(2):

            @pl.when(self.z > 0 if way == 0 else self.z < last)
            def _():
                self.z_copy(way, last - 1, 0).wait_recv()
                self.acc[...] += self.rz[way, last - 1].astype(F32)

        self.fin[...] = self.acc[...].astype(BF)
        for i, (c, _) in enumerate(self.extras):
            self.double(c, self.fin, self.rfin.at[i])
        self.gw[self.r] = self.fin[...]
        self.gy.start()
        self.gx.start()
        self.gc[0].start()

    def g_step4(self):
        self.gy.wait_recv()
        self.gyx.start()
        self.gc[1].start()
        self.gx.wait_recv()
        self.gxy.start()
        self.gc[2].start()

    def g_step5(self):
        self.gyx.wait_recv()
        self.gxy.wait_recv()
        self.gc[3].start()
        for s in self.gc:
            s.wait_recv()

    def q_pair(self, recv, a, b):
        h = self.half // 2
        return [
            self.net.copy(self.q.at[pl.ds(0, h)], recv.at[pl.ds(0, h)], self.dev(a), late=False),
            self.net.copy(self.q.at[pl.ds(h, h)], recv.at[pl.ds(h, h)], self.dev(b), late=False),
        ]

    def q_step0(self):
        self.q0.start()

    def q_step1(self):
        self.q0.wait_recv()
        self.q[...] = (self.gqb[self.mine].astype(F32) + self.rq0[...].astype(F32)).astype(BF)
        for s in self.qa:
            s.start()

    def q_step2(self):
        for s in self.qa:
            s.wait()
        self.q[...] = (self.q[...].astype(F32) + self.rq1[...].astype(F32)).astype(BF)
        for s in self.qb:
            s.start()

    def q_step3(self):
        for s in self.qb:
            s.wait()
        self.q[...] = (self.q[...].astype(F32) + self.rq2[0].astype(F32)).astype(BF)
        for i, (_, c) in enumerate(self.extras):
            self.double(c, self.q, self.rq2.at[1 + i])
        self.gq[self.mine] = self.q[...]
        self.qc.start()

    def i_setup(self):
        last = self.parts - 1
        self.chunks = self.ipart.shape[1]
        self.pos, self.lower, self.upper = [], [], []
        for d in range(self.docs):
            step = 1 if d % 2 == 0 else -1
            self.pos.append(self.z if d % 2 == 0 else last - self.z)
            self.lower.append({"mp": lax.rem(self.z - step + self.parts, self.parts)})
            self.upper.append({"mp": lax.rem(self.z + step + self.parts, self.parts)})

    def red(self, d, c):
        return rcopy(self.ipart.at[d, c], self.ri.at[d, c], self.isem.at[0, d, c], self.isem.at[1, d, c], self.lower[d])

    def bc(self, d, c):
        return rcopy(self.ig.at[d, c], self.ig.at[d, c], self.isem.at[2, d, c], self.isem.at[3, d, c], self.upper[d])

    def i_time(self, t):
        last = self.parts - 1
        for d in range(self.docs):
            p = self.pos[d]
            c = t - last + p
            ok = (c >= 0) & (c < self.chunks)

            @pl.when(ok & (p < last))
            def _():
                self.red(d, c).wait_recv()
                self.ipart[d, c] = (self.ipart[d, c].astype(F32) + self.ri[d, c].astype(F32)).astype(BF)

            @pl.when(ok & (p > 0))
            def _():
                self.red(d, c).start()

            @pl.when(ok & (p == 0))
            def _():
                self.ig[d, c] = self.ipart[d, c]
                self.bc(d, c).start()

        for d in range(self.docs):
            p = self.pos[d]
            c = t - last - p
            ok = (c >= 0) & (c < self.chunks) & (p > 0)

            @pl.when(ok)
            def _():
                self.bc(d, c).wait_recv()

            @pl.when(ok & (p < last))
            def _():
                self.bc(d, c).start()

    def i_end(self):
        last = self.parts - 1
        for d in range(self.docs):
            p = self.pos[d]

            def sent(c, _, d=d):
                self.red(d, c).wait_send()
                return 0

            def back(c, _, d=d):
                self.bc(d, c).wait_send()
                return 0

            @pl.when(p > 0)
            def _():
                lax.fori_loop(0, self.chunks, sent, 0)

            @pl.when(p < last)
            def _():
                lax.fori_loop(0, self.chunks, back, 0)

    def tail(self):
        done = 3 + self.docs
        rest = [functools.partial(self.small_step, i) for i in range(done + 1, len(self.smalls) + 1)]
        rest += [functools.partial(self.taps_step, i) for i in range(3, len(self.tapsums) + 1)]

        def run(*fs):
            def go():
                for f in fs:
                    f()

            return go

        todo = {
            1: run(self.g_step2),
            2: run(self.q_step1),
            3: run(lambda: self.z_hop(1)),
            4: run(self.q_step2),
            5: run(lambda: self.z_hop(2)),
            6: run(self.q_step3, *rest),
            8: run(self.g_step3),
            10: run(self.g_step4),
            12: run(self.g_step5),
        }
        self.q_step0()

        def step(t, _):
            self.i_time(t)
            at(t, todo)
            return 0

        lax.fori_loop(1, self.chunks + 2 * (self.parts - 1), step, 0)
        self.qc.wait_recv()
        self.i_end()
        self.z_done()
        self.net.drain()


def attn_bwd(dp, lengths, x, wt, taps, qkv, gctx, lq, lk, sm, mix, k2, z, p, l1, l3, s1, small, gmix, out_rows):
    docs, seq, dim = x.shape
    width = wt.shape[0] // 3
    heads = width // HD
    parts = gctx.shape[0]
    nchunk = seq // CHUNK
    more = max(1, dp.bit_length() - 4)
    steps = dp.bit_length() + parts.bit_length()
    sds = jax.ShapeDtypeStruct
    vmem = pltpu.VMEM
    out = [
        sds((3 * width, dim), BF),
        sds((docs, nchunk, CHUNK, dim), BF),
        sds((heads, WIN), F32),
        sds((SLOTS, SLICE, dim), BF),
        sds((8, dim), F32),
        sds(out_rows.shape, BF),
    ]
    h = 3 * width // 2
    sq = (docs, width, width)
    return pl.pallas_call(
        functools.partial(attn_bwd_kernel, docs, heads, seq, parts, dp),
        out_shape=out,
        in_specs=[SM, ANY, VM, VM, VM, VM, VM, VM, VM, VM, VM, ANY, ANY, VM, VM, VM, VM, ANY, ANY],
        out_specs=[VM] * 5 + [ANY],
        input_output_aliases={18: 5},
        scratch_shapes=[
            vmem(x.shape, BF),
            vmem(z.shape, F32),
            vmem(p.shape, F32),
            vmem(gmix.shape, F32),
            vmem((docs, 3 * width, seq), BF),
            vmem((docs, width, seq), BF),
            vmem((docs, width, seq), BF),
            vmem(sq, F32),
            vmem(sq, F32),
            vmem(sq, F32),
            vmem(sq, F32),
            vmem(sq, F32),
            vmem((heads, WIN), F32),
            vmem((heads, BLK, WIN), F32),
            vmem((docs, nchunk, CHUNK, dim), BF),
            vmem((docs, nchunk, CHUNK, dim), BF),
            vmem((parts, 2, GCUT, dim), BF),
            vmem((parts, 2, SLICE - GCUT, dim), BF),
            vmem((2, parts - 1, SLICE, dim), BF),
            vmem((SLICE, dim), BF),
            vmem((more, SLICE, dim), BF),
            vmem((h, dim), BF),
            vmem((h, dim), BF),
            vmem((1 + more, h, dim), BF),
            vmem((3 * width, dim), BF),
            vmem((h, dim), BF),
            vmem((steps, 8, dim), F32),
            vmem((steps, heads, WIN), F32),
            DMA((4,)),
            DMA((64,)),
            DMA((64,)),
            DMA((4, docs, nchunk)),
            DMA((2, 2, parts - 1, docs)),
            vmem((parts, SLICE, dim), BF),
            vmem((SLICE, dim), F32),
            DMA((2, 2, parts - 1)),
        ],
        compiler_params=pltpu.CompilerParams(vmem_limit_bytes=62 * 2**20, collective_id=2, has_side_effects=True),
        cost_estimate=pl.CostEstimate(flops=int(1.2e10), bytes_accessed=int(3e7), transcendentals=0),
        name="attn_bwd",
    )(lengths, x, wt, taps, qkv, gctx, lq, lk, sm, mix, k2, z, p, l1, l3, s1, small, gmix, out_rows)


def finish_kernel(gw_ref, gq_ref, ig_ref, out_ref, small_ref, taps_ref, ow_o, up_o, dn_o, q_o, ig_o, out_o, g1_o, b1_o, g2_o, b2_o, taps_o):
    for i, o in enumerate((ow_o, up_o, dn_o)):
        lo, size = PARTS[i]
        o[...] = gw_ref[0, lo : lo + size].astype(F32)
    q_o[...] = gq_ref[...].astype(F32)
    ig_o[...] = ig_ref[:, 0]
    out_o[...] = out_ref[...]

    @pl.when(pl.program_id(0) == 0)
    def _():
        for i, o in enumerate((g1_o, b1_o, g2_o, b2_o)):
            o[...] = small_ref[i]
        taps_o[...] = taps_ref[:, TAP_END : TAP_END + KSIZE]


def finish_up(gw, gq, ig, out_rows, small, taps):
    docs, nchunk, chunk, dim = ig.shape
    groups, rows = out_rows.shape[1:3]
    seq = nchunk * chunk
    heads = taps.shape[0]
    qrows = gq.shape[0] // SLOTS
    per = seq // SLOTS
    ratio = rows // per
    sds = jax.ShapeDtypeStruct
    whole = lambda shape: pl.BlockSpec(shape, lambda i: (0,) * len(shape))
    return pl.pallas_call(
        finish_kernel,
        grid=(SLOTS,),
        out_shape=[sds((SLOTS * t, dim), F32) for t in (OW_ROWS, UP_ROWS, DN_ROWS)]
        + [sds(gq.shape, F32), sds((docs, seq, dim), BF), sds((docs, seq, dim), BF)]
        + [sds((dim,), F32)] * 4
        + [sds((heads, KSIZE), F32)],
        in_specs=[
            pl.BlockSpec((1, SLICE, dim), lambda i: (i, 0, 0)),
            pl.BlockSpec((qrows, dim), lambda i: (i, 0)),
            pl.BlockSpec((docs, 1, chunk, dim), lambda i: (0, i, 0, 0)),
            pl.BlockSpec((docs, pl.Squeezed(), per, dim), lambda i: (0, i // ratio, i % ratio, 0)),
            whole(small.shape),
            whole(taps.shape),
        ],
        out_specs=[pl.BlockSpec((t, dim), lambda i: (i, 0)) for t in (OW_ROWS, UP_ROWS, DN_ROWS, qrows)]
        + [pl.BlockSpec((docs, per, dim), lambda i: (0, i, 0))] * 2
        + [whole((dim,))] * 4
        + [whole((heads, KSIZE))],
        compiler_params=pltpu.CompilerParams(vmem_limit_bytes=62 * 2**20),
        name="finish",
    )(gw, gq, ig, out_rows, small, taps)


def body_of(dp, mp):
    def body(tokens, lengths, qkv_weight, out_weight, conv_taps, norm1_gain, norm1_bias, norm2_gain, norm2_bias, up_weight, down_weight, cotangent):
        dim = tokens.shape[2]
        width = qkv_weight.shape[2]
        wt = jnp.transpose(qkv_weight, (0, 2, 1)).reshape(3 * width, dim)
        ow, up, dn = (t.reshape(SLOTS, -1, dim) for t in (out_weight, up_weight, down_weight))
        qkv, ctx, lq, lk, sm, mix, k2, z, p, l1, l3, wall = attn_fwd(lengths, tokens, wt, conv_taps, ow, up, dn, mp)
        out_rows, gmix, gctx, s1, small = ffn(lengths, tokens, cotangent, ctx, ow, up, dn, wall, norm1_gain, norm1_bias, norm2_gain, norm2_bias)
        gq, ig, gtaps, gw, small, out_rows = attn_bwd(
            dp, lengths, tokens, wt, conv_taps[:, ::-1], qkv, gctx, lq, lk, sm, mix, k2, z, p, l1, l3, s1, small, gmix, out_rows
        )
        g_ow, g_up, g_dn, gq, input_grad, output, g1, b1, g2, b2, g_taps = finish_up(gw, gq, ig, out_rows, small, gtaps)
        gqkv = jnp.transpose(gq.reshape(3, width, dim), (0, 2, 1))
        return output, input_grad, gqkv, g_ow, g_taps, g1, b1, g2, b2, g_up, g_dn

    return body


def solution(mesh):
    rep, rows = P(), P("mp", None)
    docs, cols, qkv = P("dp", None, None), P(None, "mp"), P(None, None, "mp")
    return jax.shard_map(
        body_of(mesh.shape["dp"], mesh.shape["mp"]),
        mesh=mesh,
        in_specs=(docs, P("dp"), qkv, rows, rows, rep, rep, rep, rep, cols, rows, docs),
        out_specs=(docs, docs, qkv, rows, rows, rep, rep, rep, rep, cols, rows),
        check_vma=False,
    )
```

```python
import functools

import jax
import jax.numpy as jnp
from jax import lax
from jax.experimental import pallas as pl
from jax.experimental.pallas import tpu as pltpu
from jax.sharding import PartitionSpec as P

HD = 64
LM = 64
KSIZE = 33
NS_ITERS = 6
EPS = 1e-5
HI = lax.Precision.HIGHEST
BF = jnp.bfloat16
F32 = jnp.float32
SCALE = HD**-0.5
WIN = 512
BLK = 256
CHUNK = 128
TAP0 = 112
TAP_END = TAP0 + BLK - 1
ROOT_HALF = 0.7071067811865476
INV_ROOT_2PI = 0.3989422804014327
MESH = pl.DeviceIdType.MESH
SLOTS = 8
OW_ROWS, UP_ROWS, DN_ROWS = 24, 96, 96
SLICE = OW_ROWS + UP_ROWS + DN_ROWS
CUT = OW_ROWS + UP_ROWS
GCUT = 112
PARTS = ((0, OW_ROWS), (OW_ROWS, UP_ROWS), (CUT, DN_ROWS))
VM = pl.BlockSpec(memory_space=pltpu.VMEM)
SM = pl.BlockSpec(memory_space=pltpu.SMEM)
ANY = pl.BlockSpec(memory_space=pl.ANY)
DMA = pltpu.SemaphoreType.DMA


def nn(a, b, precision=None):
    return lax.dot_general(a, b, (((1,), (0,)), ((), ())), precision=precision, preferred_element_type=F32)


def nt(a, b, precision=None):
    return lax.dot_general(a, b, (((1,), (1,)), ((), ())), precision=precision, preferred_element_type=F32)


def tn(a, b, precision=None):
    return lax.dot_general(a, b, (((0,), (0,)), ((), ())), precision=precision, preferred_element_type=F32)


def block_mask(width):
    r = lax.broadcasted_iota(jnp.int32, (width, width), 0) // HD
    c = lax.broadcasted_iota(jnp.int32, (width, width), 1) // HD
    return r == c


def identity(width):
    r = lax.broadcasted_iota(jnp.int32, (width, width), 0)
    c = lax.broadcasted_iota(jnp.int32, (width, width), 1)
    return jnp.where(r == c, 1.0, 0.0).astype(F32)


def spread(x, heads, mask):
    return jnp.where(mask, jnp.concatenate([x] * heads, axis=0), 0.0)


def per_head_total(col, heads):
    tot = jnp.sum(col.reshape(heads, HD, 1), axis=1, keepdims=True)
    return jnp.broadcast_to(tot, (heads, HD, 1)).reshape(heads * HD, 1)


def members(length, count):
    s = lax.broadcasted_iota(jnp.int32, (LM, count), 1)
    j = lax.broadcasted_iota(jnp.int32, (LM, count), 0)
    s64 = s * LM
    return (j * length <= s64) & (s64 < (j + 1) * length) & (s < length)


def live_lanes(length, count):
    return lax.broadcasted_iota(jnp.int32, (1, count), 1) < length


def toeplitz(row):
    return pltpu.roll(jnp.broadcast_to(row, (BLK, WIN)), 0, 1, stride=1, stride_axis=0)


def windows(x, seq):
    pad = jnp.zeros((x.shape[0], 128), x.dtype)
    padded = jnp.concatenate([pad, x, pad], axis=1)
    return jnp.concatenate([padded[:, b * BLK : b * BLK + WIN] for b in range(seq // BLK)], axis=0)


def hi_lo(x):
    hi = x.astype(BF)
    return hi, (x - hi.astype(F32)).astype(BF)


def banded(x, row, heads, seq):
    outs = []
    for h in range(heads):
        wins = windows(x[h * HD : (h + 1) * HD], seq)
        hi, lo = hi_lo(toeplitz(row[h : h + 1]))
        y = nt(wins, hi) + nt(wins, lo)
        outs.append(jnp.concatenate([y[b * HD : (b + 1) * HD] for b in range(seq // BLK)], axis=1))
    return jnp.concatenate(outs, axis=0)


def flip(i, bit):
    return i + bit * (1 - 2 * ((i // bit) % 2))


def partner(i, m):
    for bit in (1, 2, 4):
        if m & bit:
            i = flip(i, bit)
    return i


def greet(peers):
    bar = pltpu.get_barrier_semaphore()
    for p in peers:
        pl.semaphore_signal(bar, inc=1, device_id=p, device_id_type=MESH)
    pl.semaphore_wait(bar, len(peers))


def rcopy(src, dst, ss, rs, dev):
    return pltpu.make_async_remote_copy(src_ref=src, dst_ref=dst, send_sem=ss, recv_sem=rs, device_id=dev, device_id_type=MESH)


class Net:
    def __init__(self, ssem, rsem):
        self.ssem, self.rsem, self.n = ssem, rsem, 0
        self.sent = []

    def copy(self, src, dst, dev, late=True):
        i = self.n
        self.n += 1
        c = rcopy(src, dst, self.ssem.at[i], self.rsem.at[i], dev)
        if late:
            self.sent.append(c)
        return c

    def drain(self):
        for c in self.sent:
            c.wait_send()
        self.sent = []


def at(i, steps):
    for k, f in steps.items():

        @pl.when(i == k)
        def _():
            f()


class Local:
    def __init__(self, sem):
        self.sem, self.n, self.open = sem, 0, []

    def start(self, src, dst):
        c = pltpu.make_async_copy(src, dst, self.sem.at[self.n])
        self.n += 1
        c.start()
        self.open.append(c)
        return c

    def finish(self):
        for c in self.open:
            c.wait()
        self.open = []


class Line:
    def __init__(self, parts):
        self.last, self.z = parts - 1, lax.axis_index("mp")

    def sends(self, way, s):
        z = self.z
        return (z < self.last) & (z >= s) if way == 0 else (z > 0) & (z + s <= self.last)

    def gets(self, way, s):
        z = self.z
        return z - 1 >= s if way == 0 else z + 1 + s <= self.last

    def sent_from(self, way, s):
        return self.z - (1 - 2 * way) * s

    def got_from(self, way, s):
        return self.z - (1 - 2 * way) * (s + 1)

    def ahead(self, way):
        size = self.last + 1
        return {"mp": lax.rem(self.z + (1 - 2 * way) + size, size)}


class Gather:
    def __init__(self, mp, srcs, wall, zsem, psem):
        self.line = Line(mp)
        self.srcs, self.wall, self.zsem, self.psem = srcs, wall, zsem, psem
        self.d = lax.axis_index("dp")
        r = lax.rem(self.d, SLOTS)
        self.rs = (r, flip(r, 4), flip(r, 2), partner(r, 6))
        self.steps = mp - 1

    def z(self, way, s, origin):
        dev = self.line.ahead(way)
        r = self.rs[0]
        out = []
        for i, (lo, size) in enumerate(PARTS):
            dst = self.wall.at[origin, r, pl.ds(lo, size)]
            src = self.srcs[i].at[r] if s == 0 else dst
            out.append(rcopy(src, dst, self.zsem.at[0, way, s, i], self.zsem.at[1, way, s, i], dev))
        return out

    def plane(self, way, s, k):
        w = self.wall.at[self.line.got_from(way, s)]
        q, rows, bit = (
            (0, (0, SLICE), 4),
            (0, (0, SLICE), 2),
            (1, (0, CUT), 2),
            (2, (CUT, DN_ROWS), 4),
            (0, (0, SLICE), 1),
            (1, (0, SLICE), 1),
            (2, (0, SLICE), 1),
            (3, (0, SLICE), 1),
        )[k]
        ref = w.at[self.rs[q], pl.ds(*rows)]
        return rcopy(ref, ref, self.psem.at[0, way, s, k], self.psem.at[1, way, s, k], {"dp": flip(self.d, bit)})

    def send(self, s):
        for way in range(2):

            @pl.when(self.line.sends(way, s))
            def _():
                for c in self.z(way, s, self.line.sent_from(way, s)):
                    c.start()

    def got(self, s, f):
        for way in range(2):
            pl.when(self.line.gets(way, s))(functools.partial(f, way, s))

    def step1(self, s):
        def arrive(way, s):
            for c in self.z(way, s, self.line.got_from(way, s)):
                c.wait_recv()

        self.got(s, arrive)
        if s + 1 < self.steps:
            self.send(s + 1)

        def pass_on(way, s):
            for k in (0, 1, 4):
                self.plane(way, s, k).start()

        self.got(s, pass_on)

    def step2(self, s):
        def f(way, s):
            self.plane(way, s, 0).wait_recv()
            self.plane(way, s, 2).start()
            self.plane(way, s, 5).start()
            self.plane(way, s, 1).wait_recv()
            self.plane(way, s, 3).start()
            self.plane(way, s, 6).start()

        self.got(s, f)

    def step3(self, s):
        def f(way, s):
            self.plane(way, s, 2).wait_recv()
            self.plane(way, s, 3).wait_recv()
            self.plane(way, s, 7).start()

        self.got(s, f)

    def finish(self):
        def f(way, s):
            for k in range(8):
                if k >= 4:
                    self.plane(way, s, k).wait_recv()
                self.plane(way, s, k).wait_send()

        for s in range(self.steps):
            self.got(s, f)
            for way in range(2):

                @pl.when(self.line.sends(way, s))
                def _():
                    for c in self.z(way, s, self.line.sent_from(way, s)):
                        c.wait_send()


def attn_fwd_kernel(docs, heads, seq, dest, len_ref, x_hbm, wt_ref, taps_ref, ow_ref, up_ref, dn_ref,
                    qkv_hbm, ctx_ref, lq_hbm, lk_hbm, sum_hbm, mix_hbm, k2_hbm, z_hbm, p_hbm, l1_ref, l3_ref, wall_ref,
                    x_s, qkv_s, lq_s, lk_s, sum_s, mix_s, k2_s, z_s, p_s, ctx_s, taps_s, lsem, asem, zsem, psem):
    width = heads * HD
    me, dd = lax.axis_index("mp"), lax.axis_index("dp")
    local = Local(lsem)
    loads = [local.start(x_hbm.at[d], x_s.at[d]) for d in range(docs)]
    local.open = []
    greet([{"mp": partner(me, m)} for m in range(1, dest)] + [{"dp": flip(dd, b)} for b in (1, 2, 4)])
    gather = Gather(dest, (ow_ref, up_ref, dn_ref), wall_ref, zsem, psem)
    gather.send(0)

    def a_copy(m, d):
        return rcopy(ctx_s.at[partner(me, m), d], ctx_ref.at[me, d], asem.at[0, m - 1, d], asem.at[1, m - 1, d], {"mp": partner(me, m)})

    taps_s[...] = jnp.zeros_like(taps_s)
    taps_s[:, TAP0 : TAP0 + KSIZE] = taps_ref[...]
    mask = block_mask(width)
    eye = identity(width)
    for c in loads:
        c.wait()

    def project(i, _):
        d, c = i // (seq // BLK), lax.rem(i, seq // BLK)
        rows = pl.ds(pl.multiple_of(c * BLK, BLK), BLK)
        qkv_s[d, :, rows] = nt(wt_ref[...], x_s[d, rows, :]).astype(BF)
        return 0

    lax.fori_loop(0, docs * (seq // BLK), project, 0)
    local.start(qkv_s, qkv_hbm)

    def landmarks(d, _):
        length = len_ref[d]
        memb = jnp.where(members(length, seq), 1.0, 0.0).astype(F32)
        counts = jnp.maximum(jnp.sum(memb, axis=1, keepdims=True), 1.0)
        memb_b = memb.astype(BF)
        q = qkv_s[d, 0:width, :]
        k = qkv_s[d, width : 2 * width, :]
        v = qkv_s[d, 2 * width : 3 * width, :]
        lq = spread(nt(memb_b, q) / counts, heads, mask).astype(BF)
        lk = spread(nt(memb_b, k) / counts, heads, mask).astype(BF)
        lq_s[d] = lq
        lk_s[d] = lk
        s2 = jnp.where(mask, nt(lq, lk) * SCALE, -1e30)
        e2 = jnp.where(mask, jnp.exp(s2 - jnp.max(s2, axis=1, keepdims=True)), 0.0)
        k2_s[d] = e2 / jnp.sum(e2, axis=1, keepdims=True)
        s3 = jnp.where(live_lanes(length, seq), nn(lq, k) * SCALE, -1e30)
        m3 = jnp.max(s3, axis=1, keepdims=True)
        e3 = jnp.exp(s3 - m3)
        t3 = jnp.sum(e3, axis=1, keepdims=True)
        l3_ref[d] = jnp.broadcast_to(m3 + jnp.log(t3), (width, 128))
        k3 = (e3 / t3).astype(BF)
        sum_s[d] = jnp.where(mask, nt(k3, v), 0.0)
        at(d, {0: lambda: (gather.step1(0),), 1: lambda: (gather.step1(1),)})
        return 0

    lax.fori_loop(0, docs, landmarks, 0)
    for src, dst in ((lq_s, lq_hbm), (lk_s, lk_hbm), (k2_s, k2_hbm), (sum_s, sum_hbm)):
        local.start(src, dst)
    for d in range(docs):
        k2 = k2_s[d]
        z_s[d, 0] = k2.T / per_head_total(jnp.sum(k2 * k2, axis=1, keepdims=True), heads)

    def newton(i, _):
        k2s = [k2_s[d] for d in range(docs)]
        zs = [z_s[d, i] for d in range(docs)]
        ps = [nn(k2s[d], zs[d], HI) for d in range(docs)]
        bs = [15.0 * eye - nn(ps[d], 7.0 * eye - ps[d], HI) for d in range(docs)]
        cs = [13.0 * eye - nn(ps[d], bs[d], HI) for d in range(docs)]
        zs = [0.25 * nn(zs[d], cs[d], HI) for d in range(docs)]
        for d in range(docs):
            p_s[d, i, 0] = ps[d]
            p_s[d, i, 1] = bs[d]
            p_s[d, i, 2] = cs[d]
            z_s[d, i + 1] = zs[d]
        at(i, {3: lambda: (gather.step1(2), gather.step2(0),)})
        return 0

    lax.fori_loop(0, NS_ITERS, newton, 0)
    local.start(z_s, z_hbm)
    local.start(p_s, p_hbm)
    part = seq // dest

    def contexts(d, _):
        length = len_ref[d]
        q = qkv_s[d, 0:width, :]
        v = qkv_s[d, 2 * width : 3 * width, :]
        live = live_lanes(length, seq)
        mix = jnp.where(mask, nn(z_s[d, NS_ITERS], sum_s[d], HI), 0.0)
        mix_s[d] = mix.astype(BF)
        s1 = (nn(lk_s[d], q) * SCALE).reshape(heads, LM, seq)
        m1 = jnp.max(s1, axis=1, keepdims=True)
        e1 = jnp.exp(s1 - m1)
        t1 = jnp.sum(e1, axis=1, keepdims=True)
        l1_ref[d] = (m1 + jnp.log(t1)).reshape(heads, seq)
        k1 = (e1 / t1).reshape(width, seq).astype(BF)
        vl = jnp.where(live, v, 0).astype(BF)
        ctx = nn(mix.T.astype(BF), k1) + banded(vl, taps_s[...], heads, seq)
        ctx = jnp.where(live, ctx, 0.0).astype(BF)
        for i in range(dest):
            ctx_s[i, d] = ctx[:, i * part : (i + 1) * part]
        for m in range(1, dest):
            a_copy(m, d).start()
        ctx_ref[me, d] = ctx_s[me, d]
        at(d, {0: lambda: (gather.step3(0), gather.step2(1), gather.step2(2),)})
        return 0

    lax.fori_loop(0, docs, contexts, 0)
    local.start(mix_s, mix_hbm)
    gather.step3(1)
    gather.step3(2)
    gather.finish()
    for d in range(docs):
        for m in range(1, dest):
            a_copy(m, d).wait()
    local.finish()


def attn_fwd(lengths, x, wt, taps, ow, up, dn, dest):
    docs, seq, dim = x.shape
    width = wt.shape[0] // 3
    heads = width // HD
    sds = jax.ShapeDtypeStruct
    kept = [
        sds((docs, 3 * width, seq), BF),
        sds((docs, width, width), BF),
        sds((docs, width, width), BF),
        sds((docs, width, width), F32),
        sds((docs, width, width), BF),
        sds((docs, width, width), F32),
        sds((docs, NS_ITERS + 1, width, width), F32),
        sds((docs, NS_ITERS, 3, width, width), F32),
    ]
    out = [kept[0], sds((dest, docs, width, seq // dest), BF)] + kept[1:] + [
        sds((docs, heads, seq), F32),
        sds((docs, width, 128), F32),
        sds((dest, SLOTS, SLICE, dim), BF),
    ]
    return pl.pallas_call(
        functools.partial(attn_fwd_kernel, docs, heads, seq, dest),
        out_shape=out,
        in_specs=[SM, ANY, VM, VM, ANY, ANY, ANY],
        out_specs=[ANY, VM] + [ANY] * 7 + [VM, VM, ANY],
        scratch_shapes=[pltpu.VMEM((docs, seq, dim), BF)]
        + [pltpu.VMEM(t.shape, t.dtype) for t in kept]
        + [
            pltpu.VMEM((dest, docs, width, seq // dest), BF),
            pltpu.VMEM((heads, WIN), F32),
            DMA((16,)),
            DMA((2, dest - 1, docs)),
            DMA((2, 2, dest - 1, 3)),
            DMA((2, 2, dest - 1, 8)),
        ],
        compiler_params=pltpu.CompilerParams(vmem_limit_bytes=60 * 2**20, collective_id=0, has_side_effects=True),
        cost_estimate=pl.CostEstimate(flops=int(8e9), bytes_accessed=int(3e7), transcendentals=0),
        name="attn_fwd",
    )(lengths, x, wt, taps, ow, up, dn)


def ln_stats(v):
    mu = jnp.mean(v, axis=-1, keepdims=True)
    cen = v - mu
    var = jnp.mean(cen * cen, axis=-1, keepdims=True)
    r = lax.rsqrt(var + EPS)
    return cen * r, r


def ln_back(g, xhat, r):
    m1 = jnp.mean(g, axis=-1, keepdims=True)
    m2 = jnp.mean(g * xhat, axis=-1, keepdims=True)
    return r * (g - m1 - xhat * m2)


class Spread:
    def __init__(self, parts, buf, sem):
        self.line, self.buf, self.sem = Line(parts), buf, sem

    def one(self, way, s, d, origin, src=None):
        dst = self.buf.at[d, origin]
        return rcopy(dst if src is None else src, dst, self.sem.at[way, 0, s, d], self.sem.at[way, 1, s, d], self.line.ahead(way))

    def start(self, s, d, src=None):
        for way in range(2):

            @pl.when(self.line.sends(way, s))
            def _():
                self.one(way, s, d, self.line.sent_from(way, s), src).start()

    def wait(self, s, d):
        for way in range(2):

            @pl.when(self.line.gets(way, s))
            def _():
                self.one(way, s, d, self.line.got_from(way, s)).wait_recv()

    def sent(self, s, d, src=None):
        for way in range(2):

            @pl.when(self.line.sends(way, s))
            def _():
                self.one(way, s, d, self.line.sent_from(way, s), src).wait_send()


def ffn_kernel(groups, docs, rows, len_ref, x_hbm, cot_hbm, ctx_ref, ow_hbm, up_hbm, dn_hbm, wall_hbm, g1_ref, b1_ref, g2_ref, b2_ref,
               out_hbm, gmix_ref, gctx_ref, s1_hbm, small_ref,
               x_s, cot_s, w_s, rc_s, gc_s, nb_s, fac_s, act_s, gp_s, br_s, x1_s, gn_s, ga_s, o_s, s1_s, lsem, csem, osem, asem):
    n = docs * rows
    dim = x_s.shape[-1]
    z, dd = lax.axis_index("mp"), lax.axis_index("dp")
    kk = lax.rem(dd, 2)
    local = Local(lsem)
    mine = pl.ds(pl.multiple_of(z * rows, rows), rows)
    others = [partner(z, m) for m in range(1, groups)]
    heads_first = [local.start(ow_hbm, w_s.at[z, :, :, pl.ds(*PARTS[0])])]
    heads_first += [local.start(wall_hbm.at[g, :, :, pl.ds(*PARTS[0])], w_s.at[g, :, :, pl.ds(*PARTS[0])]) for g in others]
    heads_first += [local.start(x_hbm.at[d, mine], x_s.at[pl.ds(d * rows, rows)]) for d in range(docs)]
    rest = [local.start(up_hbm, w_s.at[z, :, :, pl.ds(*PARTS[1])]), local.start(dn_hbm, w_s.at[z, :, :, pl.ds(*PARTS[2])])]
    body = pl.ds(OW_ROWS, SLICE - OW_ROWS)
    rest += [local.start(wall_hbm.at[g, :, :, body], w_s.at[g, :, :, body]) for g in others]
    rest += [local.start(cot_hbm.at[d, mine], cot_s.at[pl.ds(d * rows, rows)]) for d in range(docs)]
    local.open = []
    greet([{"mp": partner(z, m)} for m in range(1, groups)] + [{"dp": flip(dd, 1)}])

    def back_copy(m, d):
        return rcopy(gc_s.at[m - 1, d], gctx_ref.at[z, d], asem.at[0, m - 1, d], asem.at[1, m - 1, d], {"mp": partner(z, m)})

    spread_out = Spread(groups, out_hbm, osem)

    def core_copy(g, part):
        lo, size = ((OW_ROWS, SLICE - OW_ROWS), (0, OW_ROWS))[part]
        return rcopy(w_s.at[g, :, 1 - kk, pl.ds(lo, size)], rc_s.at[g, :, pl.ds(lo, size)], csem.at[0, g, part], csem.at[1, g, part], {"dp": flip(dd, 1)})

    def take(g, part):
        lo, size = PARTS[part]
        return w_s[g, :, :, lo : lo + size, :].reshape(SLOTS * size, dim)

    def put(g, part, val):
        lo, size = PARTS[part]
        w_s[g, :, :, lo : lo + size, :] = val.astype(BF).reshape(SLOTS // 2, 2, size, dim)

    first = z * rows
    gain1, bias1 = g1_ref[...].reshape(1, dim), b1_ref[...].reshape(1, dim)
    gain2, bias2 = g2_ref[...].reshape(1, dim), b2_ref[...].reshape(1, dim)
    for c in heads_first:
        c.wait()
    small_ref[...] = jnp.zeros_like(small_ref)

    def doc(d, _):
        here = pl.ds(pl.multiple_of(d * rows, rows), rows)
        live = (lax.broadcasted_iota(jnp.int32, (rows, 1), 0) + first < len_ref[d]).astype(F32)
        mixed = x_s[here].astype(F32)
        for g in range(groups):
            mixed = mixed + tn(ctx_ref[g, d], take(g, 0)).astype(BF).astype(F32)
        xh1, r1 = ln_stats(mixed)
        x1_s[...] = xh1
        normed = xh1 * gain1 + bias1
        nb_s[here] = normed.astype(BF)
        br_s[...] = normed

        @pl.when(d == 0)
        def _():
            for c in rest:
                c.wait()

        def fwd_group(g, _):
            h = nn(nb_s[here], take(g, 1))
            phi_big = 0.5 * (1.0 + lax.erf(h * ROOT_HALF))
            act = (h * phi_big).astype(BF)
            act_s[g, here] = act
            fac_s[g] = phi_big + h * (jnp.exp(-0.5 * h * h) * INV_ROOT_2PI)
            br_s[...] += nn(act, take(g, 2)).astype(BF).astype(F32)
            return 0

        lax.fori_loop(0, groups, fwd_group, 0, unroll=True)
        xh2, r2 = ln_stats(br_s[...])
        o_s[d] = (live * (xh2 * gain2 + bias2)).astype(BF)

        @pl.when(d == 0)
        def _():
            spread_out.start(0, 0, o_s.at[0])

        g_out = live * cot_s[here].astype(F32)
        gg2 = jnp.sum(g_out * xh2, axis=0, keepdims=True)
        gb2 = jnp.sum(g_out, axis=0, keepdims=True)
        g_res = ln_back(g_out * gain2, xh2, r2)
        gn_s[...] = g_res
        gbr_s[here] = g_res.astype(BF)

        def back_group(g, _):
            g_pre = (nt(gbr_s[here], take(g, 2)) * fac_s[g]).astype(BF)
            gp_s[g, here] = g_pre
            gn_s[...] += nt(g_pre, take(g, 1))
            return 0

        lax.fori_loop(0, groups, back_group, 0)
        g_n = gn_s[...]
        xh1 = x1_s[...]
        gg1 = jnp.sum(g_n * xh1, axis=0, keepdims=True)
        gb1 = jnp.sum(g_n, axis=0, keepdims=True)
        small_ref[...] += jnp.concatenate([gg1, gb1, gg2, gb2, jnp.zeros((4, dim), F32)], axis=0)
        g_mix = ln_back(g_n * gain1, xh1, r1)
        gmix_ref[d] = g_mix
        g_att = g_mix.astype(BF)
        ga_s[here] = g_att
        for m in reversed(range(groups)):
            t = nt(take(partner(z, m), 0), g_att).astype(BF)
            if m:
                gc_s[m - 1, d] = t
                back_copy(m, d).start()
            else:
                gctx_ref[z, d] = t
        return 0

    gbr_s = cot_s
    lax.fori_loop(0, docs, doc, 0)
    for d in range(docs):
        local.start(o_s.at[d], out_hbm.at[d, z])

    def weight_group(g, _):
        put(g, 2, tn(act_s[g], gbr_s[...]))
        put(g, 1, tn(nb_s[...], gp_s[g]))
        core_copy(g, 0).start()
        return 0

    lax.fori_loop(0, groups, weight_group, 0)
    for g in range(groups):
        acc = None
        for d in range(docs):
            t = nn(ctx_ref[g, d], ga_s[d * rows : (d + 1) * rows])
            acc = t if acc is None else acc + t
        put(g, 0, acc)
        core_copy(g, 1).start()

    def add_group(g, _):
        core_copy(g, 0).wait_recv()
        core_copy(g, 1).wait_recv()

        def add_slot(j, _):
            s1_s[g, j // 2, j % 2] = (w_s[g, j, kk].astype(F32) + rc_s[g, j].astype(F32)).astype(BF)
            return 0

        lax.fori_loop(0, SLOTS // 2, add_slot, 0)
        return 0

    lax.fori_loop(0, groups, add_group, 0)
    local.start(s1_s, s1_hbm)
    for m in range(1, groups):
        for d in range(docs):
            back_copy(m, d).wait()
    spread_out.wait(0, 0)
    spread_out.sent(0, 0, o_s.at[0])
    for g in range(groups):
        for part in range(2):
            core_copy(g, part).wait_send()
    local.finish()


def ffn(lengths, x, cot, ctx, ow, up, dn, wall, g1, b1, g2, b2):
    docs, seq, dim = x.shape
    groups, _, width, rows = ctx.shape
    ff = SLOTS * UP_ROWS
    n = docs * rows
    sds = jax.ShapeDtypeStruct
    out = [
        sds((docs, groups, rows, dim), BF),
        sds((docs, rows, dim), F32),
        sds((groups, docs, width, rows), BF),
        sds((groups, 2, 2, SLICE, dim), BF),
        sds((8, dim), F32),
    ]
    wall = wall.reshape(groups, SLOTS // 2, 2, SLICE, dim)
    ow, up, dn = (t.reshape(SLOTS // 2, 2, -1, dim) for t in (ow, up, dn))
    return pl.pallas_call(
        functools.partial(ffn_kernel, groups, docs, rows),
        out_shape=out,
        in_specs=[SM, ANY, ANY, VM, ANY, ANY, ANY, ANY, VM, VM, VM, VM],
        out_specs=[ANY, VM, VM, ANY, VM],
        scratch_shapes=[
            pltpu.VMEM((n, dim), BF),
            pltpu.VMEM((n, dim), BF),
            pltpu.VMEM((groups, SLOTS // 2, 2, SLICE, dim), BF),
            pltpu.VMEM((groups, SLOTS // 2, SLICE, dim), BF),
            pltpu.VMEM((groups - 1, docs, width, rows), BF),
            pltpu.VMEM((n, dim), BF),
            pltpu.VMEM((groups, rows, ff), F32),
            pltpu.VMEM((groups, n, ff), BF),
            pltpu.VMEM((groups, n, ff), BF),
            pltpu.VMEM((rows, dim), F32),
            pltpu.VMEM((rows, dim), F32),
            pltpu.VMEM((rows, dim), F32),
            pltpu.VMEM((n, dim), BF),
            pltpu.VMEM((docs, rows, dim), BF),
            pltpu.VMEM((groups, 2, 2, SLICE, dim), BF),
            DMA((24,)),
            DMA((2, groups, 2)),
            DMA((2, 2, groups - 1, docs)),
            DMA((2, groups - 1, docs)),
        ],
        compiler_params=pltpu.CompilerParams(vmem_limit_bytes=62 * 2**20, collective_id=1, has_side_effects=True),
        cost_estimate=pl.CostEstimate(flops=int(1.8e10), bytes_accessed=int(4e7), transcendentals=0),
        name="ffn",
    )(lengths, x, cot, ctx, ow, up, dn, wall, g1, b1, g2, b2)


def attn_bwd_kernel(docs, heads, seq, parts, dp, len_ref, x_hbm, wt_ref, taps_ref, qkv_ref, gctx_ref, lq_ref, lk_ref, sum_ref, mix_ref, k2_ref,
                    z_hbm, p_hbm, l1_ref, l3_ref, s1, small_in, gmix_hbm, out_in, gq, ig, taps_out, gw, small, out_hbm,
                    x_s, z_s, p_s, gmix_s, g_s, gs1_s, gs3_s, ginv_s, glq_s, glk_s, gz_s, gk_s, taps_s, gacc_s,
                    ipart, ri, ra1, rb1, rz, fin, rfin, rq0, rq1, rq2, gqb, q, rsm, rtp, lsem, ssem, rsem, isem, osem, pz, acc, gsem):
    width = heads * HD
    nblk = seq // BLK
    dim = x_s.shape[-1]
    zi = lax.axis_index("mp")
    local = Local(lsem)
    loads = [local.start(a, b) for a, b in ((z_hbm, z_s), (p_hbm, p_s), (x_hbm, x_s), (gmix_hbm, gmix_s))]
    local.open = []
    nd = Sums(docs, seq, parts, dp, locals())
    nd.begin()
    out = Spread(parts, out_hbm, osem)
    left = [(s, d) for s in range(parts - 1) for d in range(docs) if (s, d) != (0, 0)]
    waves = [[(0, d) for d in range(1, docs)] + [(1, 0)]]
    waves += [[(s, d) for d in range(1, docs)] + [(s + 1, 0)] for s in range(1, parts - 2)] + [[(parts - 2, d) for d in range(1, docs)]]

    def out_step(i):
        for s, d in waves[i] if i < len(waves) else ():
            if s > 0 and (s - 1, d) != (0, 0):
                out.wait(s - 1, d)
            out.start(s, d)

    out_step(0)
    taps_s[...] = jnp.zeros_like(taps_s)
    taps_s[:, TAP0 : TAP0 + KSIZE] = taps_ref[...]
    mask = block_mask(width)
    eye = identity(width)
    anti = jnp.where(
        lax.broadcasted_iota(jnp.int32, (BLK, BLK), 0) + lax.broadcasted_iota(jnp.int32, (BLK, BLK), 1) == BLK - 1, 1.0, 0.0
    ).astype(BF)
    gacc_s[...] = jnp.zeros_like(gacc_s)

    def doc(d, _):
        length = len_ref[d]
        live = live_lanes(length, seq)
        q_ = qkv_ref[d, 0:width, :]
        k = qkv_ref[d, width : 2 * width, :]
        v = qkv_ref[d, 2 * width : 3 * width, :]
        gc = jnp.concatenate([gctx_ref[i, d] for i in range(parts)], axis=1)
        gc = jnp.where(live, gc, 0).astype(BF)
        lq, lk = lq_ref[d], lk_ref[d]
        s1_ = (nn(lk, q_) * SCALE).reshape(heads, LM, seq)
        k1 = jnp.exp(s1_ - l1_ref[d].reshape(heads, 1, seq))
        gmixing = jnp.where(mask, nt(k1.reshape(width, seq).astype(BF), gc), 0.0)
        gk1 = nn(mix_ref[d], gc).reshape(heads, LM, seq)
        gs1 = (k1 * (gk1 - jnp.sum(gk1 * k1, axis=1, keepdims=True))).reshape(width, seq).astype(BF)
        gz_s[d] = nt(gmixing, sum_ref[d], HI)
        gk_s[d] = jnp.zeros((width, width), F32)
        gsum = jnp.where(mask, tn(ginv_s[d], gmixing, HI), 0.0)
        gsum_b = gsum.astype(BF)
        s3 = jnp.where(live, nn(lq, k) * SCALE, -1e30)
        k3 = jnp.exp(s3 - l3_ref[d][:, 0:1])
        gk3 = nn(gsum_b, v)
        gs3 = (k3 * (gk3 - jnp.sum(gk3 * k3, axis=1, keepdims=True))).astype(BF)
        at(d, {1: lambda: out_step(1)})
        glq_s[d] = jnp.where(mask, nt(gs3, k), 0.0) * SCALE
        glk_s[d] = jnp.where(mask, nt(gs1, q_), 0.0) * SCALE
        gs1_s[d] = gs1
        gs3_s[d] = gs3
        gv = nn(gsum.T.astype(BF), k3.astype(BF))
        gvl = banded(gc, taps_s[...], heads, seq)
        g_s[d, 2 * width : 3 * width, :] = (gv + jnp.where(live, gvl, 0.0)).astype(BF)
        vl = jnp.where(live, v, 0).astype(BF)
        for h in range(heads):
            wins = windows(vl[h * HD : (h + 1) * HD], seq)
            gch = gc[h * HD : (h + 1) * HD]
            stack = jnp.concatenate([gch[:, b * BLK : (b + 1) * BLK] for b in range(nblk)], axis=0)
            gacc_s[h] += nn(nt(anti, stack).astype(BF), wins)
        at(d, {i: functools.partial(nd.small_step, 1 + i) for i in range(docs)})
        return 0

    loads[0].wait()
    for d in range(docs):
        ginv_s[d] = z_s[d, NS_ITERS]
    lax.fori_loop(0, docs, doc, 0)
    for h in range(heads):
        rolled = pltpu.roll(gacc_s[h], 0, 1, stride=1, stride_axis=0)
        taps_out[h : h + 1, :] = jnp.sum(rolled, axis=0, keepdims=True)
    loads[1].wait()

    def newton_back(j, _):
        i = NS_ITERS - 1 - j
        for d in range(docs):
            z, p, b, c = z_s[d, i], p_s[d, i, 0], p_s[d, i, 1], p_s[d, i, 2]
            a = 7.0 * eye - p
            g = 0.25 * gz_s[d]
            gc_ = tn(z, g, HI)
            gp = -nt(gc_, b, HI)
            gb = -tn(p, gc_, HI)
            gp = gp - nt(gb, a, HI)
            ga = -tn(p, gb, HI)
            gp = gp - ga
            gk_s[d] += nt(gp, z, HI)
            gz_s[d] = nt(g, c, HI) + tn(k2_ref[d], gp, HI)
        base = 1 + docs
        at(j, {
            1: lambda: (nd.small_step(base), nd.taps_step(0)),
            3: lambda: (nd.small_step(base + 1), nd.taps_step(1), nd.g_step1()),
            5: lambda: (nd.small_step(base + 2), nd.taps_step(2), out_step(2)),
        })
        return 0

    lax.fori_loop(0, NS_ITERS, newton_back, 0)
    for c in loads[2:]:
        c.wait()

    def finish(d, _):
        length = len_ref[d]
        k2 = k2_ref[d]
        tot = per_head_total(jnp.sum(k2 * k2, axis=1, keepdims=True), heads)
        g = gz_s[d]
        dot = per_head_total(jnp.sum(g * k2.T, axis=1, keepdims=True), heads)
        gk2 = gk_s[d] + (g / tot).T - k2 * (2.0 * dot / (tot * tot))
        gs2 = k2 * (gk2 - jnp.sum(gk2 * k2, axis=1, keepdims=True)) * SCALE
        memb = jnp.where(members(length, seq), 1.0, 0.0).astype(F32)
        counts = jnp.maximum(jnp.sum(memb, axis=1, keepdims=True), 1.0)
        counts = jnp.concatenate([counts] * heads, axis=0)
        memb3 = jnp.concatenate([memb.astype(BF)] * heads, axis=0)
        lq, lk = lq_ref[d].astype(F32), lk_ref[d].astype(F32)
        glq = (glq_s[d] + nn(gs2, lk, HI)) / counts
        glk = (glk_s[d] + tn(gs2, lq, HI)) / counts
        hi, lo = hi_lo(glq.T)
        gq_ = nn(lk.T.astype(BF), gs1_s[d]) * SCALE + nn(hi, memb3) + nn(lo, memb3)
        hi, lo = hi_lo(glk.T)
        gk_ = nn(lq.T.astype(BF), gs3_s[d]) * SCALE + nn(hi, memb3) + nn(lo, memb3)
        g_s[d, 0:width, :] = gq_.astype(BF)
        g_s[d, width : 2 * width, :] = gk_.astype(BF)

        def inputs(c, _):
            rows = pl.ds(pl.multiple_of(c * BLK, BLK), BLK)
            t = tn(g_s[d, :, rows], wt_ref[...])
            t = (t + jnp.where(zi == c, 1.0, 0.0) * gmix_s[d]).astype(BF)
            per = BLK // CHUNK
            ipart[d, pl.ds(c * per, per)] = t.reshape(per, CHUNK, dim)
            return 0

        lax.fori_loop(0, nblk, inputs, 0)
        return 0

    lax.fori_loop(0, docs, finish, 0)
    for i in range(3, len(waves)):
        out_step(i)
    nd.i_time(0)

    def weights(c, _):
        rows = pl.ds(pl.multiple_of(c * width, width), width)
        acc_q = nn(g_s[0, rows], x_s[0])
        for d in range(1, docs):
            acc_q = acc_q + nn(g_s[d, rows], x_s[d])
        gqb[rows] = acc_q.astype(BF)
        return 0

    lax.fori_loop(0, 3, weights, 0)
    nd.tail()
    for s, d in left:
        if s == parts - 2:
            out.wait(s, d)
    for s, d in left:
        out.sent(s, d)


class Sums:
    def __init__(self, docs, seq, parts, dp, refs):
        for name in ("pz", "acc", "gsem", "s1", "small_in", "gq", "ig", "taps_out", "gw", "small", "ipart", "ri", "ra1", "rb1", "rz", "fin", "rfin", "rq0", "rq1", "rq2", "gqb", "q", "rsm", "rtp", "ssem", "rsem", "isem"):
            setattr(self, name, refs[name])
        self.docs, self.parts = docs, parts
        self.z, self.d = lax.axis_index("mp"), lax.axis_index("dp")
        self.r = lax.rem(self.d, SLOTS)
        self.y, self.x, self.k = self.r // 4, lax.rem(self.r // 2, 2), lax.rem(self.r, 2)
        self.net = Net(self.ssem, self.rsem)
        self.extra = [b for b in (8, 16, 32, 64, 128) if b < dp]
        self.bits = [1, 2, 4] + self.extra

    def dev(self, bit):
        return {"dp": flip(self.d, bit)}

    def zdev(self, m):
        return {"mp": partner(self.z, m)}

    def begin(self):
        greet([self.zdev(m) for m in range(1, self.parts)] + [self.dev(b) for b in self.bits])
        self.i_setup()
        self.line = Line(self.parts)
        c = self.net.copy
        low, high = pl.ds(0, GCUT), pl.ds(GCUT, SLICE - GCUT)
        self.a1 = c(self.s1.at[:, 1 - self.y, :, low], self.ra1, self.dev(4))
        self.b1 = c(self.s1.at[:, :, 1 - self.x, high], self.rb1, self.dev(2))
        self.a1.start()
        self.b1.start()
        self.a2 = c(self.ra1.at[:, 1 - self.x], self.pz.at[:, low], self.dev(2))
        self.b2 = c(self.rb1.at[:, 1 - self.y], self.pz.at[:, high], self.dev(4))
        r, gw = self.r, self.gw
        r4, r2, r6 = flip(r, 4), flip(r, 2), partner(r, 6)
        self.gy = c(gw.at[r], gw.at[r], self.dev(4))
        self.gx = c(gw.at[r], gw.at[r], self.dev(2))
        self.gyx = c(gw.at[r4, low], gw.at[r4, low], self.dev(2))
        self.gxy = c(gw.at[r2, high], gw.at[r2, high], self.dev(4))
        self.gc = [c(gw.at[i], gw.at[i], self.dev(1)) for i in (r, r4, r2, r6)]
        h = self.gqb.shape[0] // 2
        self.half = h
        mine, other = (pl.ds(pl.multiple_of(k * h, 8), h) for k in (self.k, 1 - self.k))
        self.mine = mine
        self.q0 = c(self.gqb.at[other], self.rq0, self.dev(1))
        self.qa = self.q_pair(self.rq1, 4, 2)
        self.qb = self.q_pair(self.rq2.at[0], 2, 4)
        self.qc = c(self.gq.at[mine], self.gq.at[mine], self.dev(1))
        self.extras = [(c(self.fin, self.rfin.at[i], self.dev(b), late=False), c(self.q, self.rq2.at[1 + i], self.dev(b), late=False)) for i, b in enumerate(self.extra)]
        self.small[...] = self.small_in[...]
        zs = [self.zdev(1 << j) for j in range(self.parts.bit_length() - 1)]
        self.smalls = [c(self.small, self.rsm.at[i], dev, late=False) for i, dev in enumerate([self.dev(b) for b in self.bits] + zs)]
        self.tapsums = [c(self.taps_out, self.rtp.at[i], self.dev(b), late=False) for i, b in enumerate(self.bits)]
        self.small_step(0)

    def exchange(self, copies, buf, recv, i):
        if 0 < i <= len(copies):
            copies[i - 1].wait()
            buf[...] = buf[...] + recv[i - 1]
        if i < len(copies):
            copies[i].start()

    def small_step(self, i):
        self.exchange(self.smalls, self.small, self.rsm, i)

    def taps_step(self, i):
        self.exchange(self.tapsums, self.taps_out, self.rtp, i)

    def double(self, c, buf, recv):
        c.start()
        c.wait()
        buf[...] = (buf[...].astype(F32) + recv[...].astype(F32)).astype(buf.dtype)

    def g_step1(self):
        self.a1.wait_recv()
        self.b1.wait_recv()

        def add(i, _):
            g, j = i // 2, i % 2
            self.ra1[g, j] = (self.ra1[g, j].astype(F32) + self.s1[g, self.y, j, 0:GCUT].astype(F32)).astype(BF)
            self.rb1[g, j] = (self.rb1[g, j].astype(F32) + self.s1[g, j, self.x, GCUT:SLICE].astype(F32)).astype(BF)
            return 0

        lax.fori_loop(0, 2 * self.parts, add, 0)
        self.a2.start()
        self.b2.start()

    def g_step2(self):
        self.a2.wait_recv()
        self.b2.wait_recv()

        def add(g, _):
            self.pz[g, 0:GCUT] = (self.pz[g, 0:GCUT].astype(F32) + self.ra1[g, self.x].astype(F32)).astype(BF)
            self.pz[g, GCUT:SLICE] = (self.pz[g, GCUT:SLICE].astype(F32) + self.rb1[g, self.y].astype(F32)).astype(BF)
            return 0

        lax.fori_loop(0, self.parts, add, 0)
        self.z_hop(0)

    def z_piece(self, way, s):
        last = self.parts - 1
        g = last - s + self.z if way == 0 else s - last + self.z
        return g, (self.z <= s) & (self.z < last) if way == 0 else (last - self.z <= s) & (self.z > 0)

    def z_copy(self, way, s, g):
        return rcopy(self.pz.at[g], self.rz.at[way, s], self.gsem.at[0, way, s], self.gsem.at[1, way, s], self.line.ahead(way))

    def z_hop(self, s):
        last = self.parts - 1
        for way in range(2):
            g, ok = self.z_piece(way, s)
            inner = self.z > 0 if way == 0 else self.z < last

            if s > 0:

                @pl.when(ok & inner)
                def _():
                    self.z_copy(way, s - 1, 0).wait_recv()
                    self.pz[g] = (self.pz[g].astype(F32) + self.rz[way, s - 1].astype(F32)).astype(BF)

            @pl.when(ok)
            def _():
                self.z_copy(way, s, g).start()

    def z_done(self):
        last = self.parts - 1
        for way in range(2):
            for s in range(last):
                g, ok = self.z_piece(way, s)

                @pl.when(ok)
                def _():
                    self.z_copy(way, s, g).wait_send()

    def g_step3(self):
        last = self.parts - 1
        self.acc[...] = self.pz[self.z].astype(F32)
        for way in range(2):

            @pl.when(self.z > 0 if way == 0 else self.z < last)
            def _():
                self.z_copy(way, last - 1, 0).wait_recv()
                self.acc[...] += self.rz[way, last - 1].astype(F32)

        self.fin[...] = self.acc[...].astype(BF)
        for i, (c, _) in enumerate(self.extras):
            self.double(c, self.fin, self.rfin.at[i])
        self.gw[self.r] = self.fin[...]
        self.gy.start()
        self.gx.start()
        self.gc[0].start()

    def g_step4(self):
        self.gy.wait_recv()
        self.gyx.start()
        self.gc[1].start()
        self.gx.wait_recv()
        self.gxy.start()
        self.gc[2].start()

    def g_step5(self):
        self.gyx.wait_recv()
        self.gxy.wait_recv()
        self.gc[3].start()
        for s in self.gc:
            s.wait_recv()

    def q_pair(self, recv, a, b):
        h = self.half // 2
        return [
            self.net.copy(self.q.at[pl.ds(0, h)], recv.at[pl.ds(0, h)], self.dev(a), late=False),
            self.net.copy(self.q.at[pl.ds(h, h)], recv.at[pl.ds(h, h)], self.dev(b), late=False),
        ]

    def q_step0(self):
        self.q0.start()

    def q_step1(self):
        self.q0.wait_recv()
        self.q[...] = (self.gqb[self.mine].astype(F32) + self.rq0[...].astype(F32)).astype(BF)
        for s in self.qa:
            s.start()

    def q_step2(self):
        for s in self.qa:
            s.wait()
        self.q[...] = (self.q[...].astype(F32) + self.rq1[...].astype(F32)).astype(BF)
        for s in self.qb:
            s.start()

    def q_step3(self):
        for s in self.qb:
            s.wait()
        self.q[...] = (self.q[...].astype(F32) + self.rq2[0].astype(F32)).astype(BF)
        for i, (_, c) in enumerate(self.extras):
            self.double(c, self.q, self.rq2.at[1 + i])
        self.gq[self.mine] = self.q[...]
        self.qc.start()

    def i_setup(self):
        last = self.parts - 1
        self.chunks = self.ipart.shape[1]
        self.pos, self.lower, self.upper = [], [], []
        for d in range(self.docs):
            step = 1 if d % 2 == 0 else -1
            self.pos.append(self.z if d % 2 == 0 else last - self.z)
            self.lower.append({"mp": lax.rem(self.z - step + self.parts, self.parts)})
            self.upper.append({"mp": lax.rem(self.z + step + self.parts, self.parts)})

    def red(self, d, c):
        return rcopy(self.ipart.at[d, c], self.ri.at[d, c], self.isem.at[0, d, c], self.isem.at[1, d, c], self.lower[d])

    def bc(self, d, c):
        return rcopy(self.ig.at[d, c], self.ig.at[d, c], self.isem.at[2, d, c], self.isem.at[3, d, c], self.upper[d])

    def i_time(self, t):
        last = self.parts - 1
        for d in range(self.docs):
            p = self.pos[d]
            c = t - last + p
            ok = (c >= 0) & (c < self.chunks)

            @pl.when(ok & (p < last))
            def _():
                self.red(d, c).wait_recv()
                self.ipart[d, c] = (self.ipart[d, c].astype(F32) + self.ri[d, c].astype(F32)).astype(BF)

            @pl.when(ok & (p > 0))
            def _():
                self.red(d, c).start()

            @pl.when(ok & (p == 0))
            def _():
                self.ig[d, c] = self.ipart[d, c]
                self.bc(d, c).start()

        for d in range(self.docs):
            p = self.pos[d]
            c = t - last - p
            ok = (c >= 0) & (c < self.chunks) & (p > 0)

            @pl.when(ok)
            def _():
                self.bc(d, c).wait_recv()

            @pl.when(ok & (p < last))
            def _():
                self.bc(d, c).start()

    def i_end(self):
        last = self.parts - 1
        for d in range(self.docs):
            p = self.pos[d]

            def sent(c, _, d=d):
                self.red(d, c).wait_send()
                return 0

            def back(c, _, d=d):
                self.bc(d, c).wait_send()
                return 0

            @pl.when(p > 0)
            def _():
                lax.fori_loop(0, self.chunks, sent, 0)

            @pl.when(p < last)
            def _():
                lax.fori_loop(0, self.chunks, back, 0)

    def tail(self):
        done = 3 + self.docs
        rest = [functools.partial(self.small_step, i) for i in range(done + 1, len(self.smalls) + 1)]
        rest += [functools.partial(self.taps_step, i) for i in range(3, len(self.tapsums) + 1)]

        def run(*fs):
            def go():
                for f in fs:
                    f()

            return go

        todo = {
            1: run(self.g_step2),
            2: run(self.q_step1),
            3: run(lambda: self.z_hop(1)),
            4: run(self.q_step2),
            5: run(lambda: self.z_hop(2)),
            6: run(self.q_step3, *rest),
            8: run(self.g_step3),
            10: run(self.g_step4),
            12: run(self.g_step5),
        }
        self.q_step0()

        def step(t, _):
            self.i_time(t)
            at(t, todo)
            return 0

        lax.fori_loop(1, self.chunks + 2 * (self.parts - 1), step, 0)
        self.qc.wait_recv()
        self.i_end()
        self.z_done()
        self.net.drain()


def attn_bwd(dp, lengths, x, wt, taps, qkv, gctx, lq, lk, sm, mix, k2, z, p, l1, l3, s1, small, gmix, out_rows):
    docs, seq, dim = x.shape
    width = wt.shape[0] // 3
    heads = width // HD
    parts = gctx.shape[0]
    nchunk = seq // CHUNK
    more = max(1, dp.bit_length() - 4)
    steps = dp.bit_length() + parts.bit_length()
    sds = jax.ShapeDtypeStruct
    vmem = pltpu.VMEM
    out = [
        sds((3 * width, dim), BF),
        sds((docs, nchunk, CHUNK, dim), BF),
        sds((heads, WIN), F32),
        sds((SLOTS, SLICE, dim), BF),
        sds((8, dim), F32),
        sds(out_rows.shape, BF),
    ]
    h = 3 * width // 2
    sq = (docs, width, width)
    return pl.pallas_call(
        functools.partial(attn_bwd_kernel, docs, heads, seq, parts, dp),
        out_shape=out,
        in_specs=[SM, ANY, VM, VM, VM, VM, VM, VM, VM, VM, VM, ANY, ANY, VM, VM, VM, VM, ANY, ANY],
        out_specs=[VM] * 5 + [ANY],
        input_output_aliases={18: 5},
        scratch_shapes=[
            vmem(x.shape, BF),
            vmem(z.shape, F32),
            vmem(p.shape, F32),
            vmem(gmix.shape, F32),
            vmem((docs, 3 * width, seq), BF),
            vmem((docs, width, seq), BF),
            vmem((docs, width, seq), BF),
            vmem(sq, F32),
            vmem(sq, F32),
            vmem(sq, F32),
            vmem(sq, F32),
            vmem(sq, F32),
            vmem((heads, WIN), F32),
            vmem((heads, BLK, WIN), F32),
            vmem((docs, nchunk, CHUNK, dim), BF),
            vmem((docs, nchunk, CHUNK, dim), BF),
            vmem((parts, 2, GCUT, dim), BF),
            vmem((parts, 2, SLICE - GCUT, dim), BF),
            vmem((2, parts - 1, SLICE, dim), BF),
            vmem((SLICE, dim), BF),
            vmem((more, SLICE, dim), BF),
            vmem((h, dim), BF),
            vmem((h, dim), BF),
            vmem((1 + more, h, dim), BF),
            vmem((3 * width, dim), BF),
            vmem((h, dim), BF),
            vmem((steps, 8, dim), F32),
            vmem((steps, heads, WIN), F32),
            DMA((4,)),
            DMA((64,)),
            DMA((64,)),
            DMA((4, docs, nchunk)),
            DMA((2, 2, parts - 1, docs)),
            vmem((parts, SLICE, dim), BF),
            vmem((SLICE, dim), F32),
            DMA((2, 2, parts - 1)),
        ],
        compiler_params=pltpu.CompilerParams(vmem_limit_bytes=62 * 2**20, collective_id=2, has_side_effects=True),
        cost_estimate=pl.CostEstimate(flops=int(1.2e10), bytes_accessed=int(3e7), transcendentals=0),
        name="attn_bwd",
    )(lengths, x, wt, taps, qkv, gctx, lq, lk, sm, mix, k2, z, p, l1, l3, s1, small, gmix, out_rows)


def finish_kernel(gw_ref, gq_ref, ig_ref, out_ref, small_ref, taps_ref, ow_o, up_o, dn_o, q_o, ig_o, out_o, g1_o, b1_o, g2_o, b2_o, taps_o):
    for i, o in enumerate((ow_o, up_o, dn_o)):
        lo, size = PARTS[i]
        o[...] = gw_ref[0, lo : lo + size].astype(F32)
    q_o[...] = gq_ref[...].astype(F32)
    ig_o[...] = ig_ref[:, 0]
    out_o[...] = out_ref[...]

    @pl.when(pl.program_id(0) == 0)
    def _():
        for i, o in enumerate((g1_o, b1_o, g2_o, b2_o)):
            o[...] = small_ref[i]
        taps_o[...] = taps_ref[:, TAP_END : TAP_END + KSIZE]


def finish_up(gw, gq, ig, out_rows, small, taps):
    docs, nchunk, chunk, dim = ig.shape
    groups, rows = out_rows.shape[1:3]
    seq = nchunk * chunk
    heads = taps.shape[0]
    qrows = gq.shape[0] // SLOTS
    per = seq // SLOTS
    ratio = rows // per
    sds = jax.ShapeDtypeStruct
    whole = lambda shape: pl.BlockSpec(shape, lambda i: (0,) * len(shape))
    return pl.pallas_call(
        finish_kernel,
        grid=(SLOTS,),
        out_shape=[sds((SLOTS * t, dim), F32) for t in (OW_ROWS, UP_ROWS, DN_ROWS)]
        + [sds(gq.shape, F32), sds((docs, seq, dim), BF), sds((docs, seq, dim), BF)]
        + [sds((dim,), F32)] * 4
        + [sds((heads, KSIZE), F32)],
        in_specs=[
            pl.BlockSpec((1, SLICE, dim), lambda i: (i, 0, 0)),
            pl.BlockSpec((qrows, dim), lambda i: (i, 0)),
            pl.BlockSpec((docs, 1, chunk, dim), lambda i: (0, i, 0, 0)),
            pl.BlockSpec((docs, pl.Squeezed(), per, dim), lambda i: (0, i // ratio, i % ratio, 0)),
            whole(small.shape),
            whole(taps.shape),
        ],
        out_specs=[pl.BlockSpec((t, dim), lambda i: (i, 0)) for t in (OW_ROWS, UP_ROWS, DN_ROWS, qrows)]
        + [pl.BlockSpec((docs, per, dim), lambda i: (0, i, 0))] * 2
        + [whole((dim,))] * 4
        + [whole((heads, KSIZE))],
        compiler_params=pltpu.CompilerParams(vmem_limit_bytes=62 * 2**20),
        name="finish",
    )(gw, gq, ig, out_rows, small, taps)


def body_of(dp, mp):
    def body(tokens, lengths, qkv_weight, out_weight, conv_taps, norm1_gain, norm1_bias, norm2_gain, norm2_bias, up_weight, down_weight, cotangent):
        dim = tokens.shape[2]
        width = qkv_weight.shape[2]
        wt = jnp.transpose(qkv_weight, (0, 2, 1)).reshape(3 * width, dim)
        ow, up, dn = (t.reshape(SLOTS, -1, dim) for t in (out_weight, up_weight, down_weight))
        qkv, ctx, lq, lk, sm, mix, k2, z, p, l1, l3, wall = attn_fwd(lengths, tokens, wt, conv_taps, ow, up, dn, mp)
        out_rows, gmix, gctx, s1, small = ffn(lengths, tokens, cotangent, ctx, ow, up, dn, wall, norm1_gain, norm1_bias, norm2_gain, norm2_bias)
        gq, ig, gtaps, gw, small, out_rows = attn_bwd(
            dp, lengths, tokens, wt, conv_taps[:, ::-1], qkv, gctx, lq, lk, sm, mix, k2, z, p, l1, l3, s1, small, gmix, out_rows
        )
        g_ow, g_up, g_dn, gq, input_grad, output, g1, b1, g2, b2, g_taps = finish_up(gw, gq, ig, out_rows, small, gtaps)
        gqkv = jnp.transpose(gq.reshape(3, width, dim), (0, 2, 1))
        return output, input_grad, gqkv, g_ow, g_taps, g1, b1, g2, b2, g_up, g_dn

    return body


def solution(mesh):
    rep, rows = P(), P("mp", None)
    docs, cols, qkv = P("dp", None, None), P(None, "mp"), P(None, None, "mp")
    return jax.shard_map(
        body_of(mesh.shape["dp"], mesh.shape["mp"]),
        mesh=mesh,
        in_specs=(docs, P("dp"), qkv, rows, rows, rep, rep, rep, rep, cols, rows, docs),
        out_specs=(docs, docs, qkv, rows, rows, rep, rep, rep, rep, cols, rows),
        check_vma=False,
    )
```

```python
import functools

import jax
import jax.numpy as jnp
from jax import lax
from jax.experimental import pallas as pl
from jax.experimental.pallas import tpu as pltpu
from jax.sharding import PartitionSpec as P

HD = 64
LM = 64
KSIZE = 33
NS_ITERS = 6
EPS = 1e-5
HI = lax.Precision.HIGHEST
BF = jnp.bfloat16
F32 = jnp.float32
SCALE = HD**-0.5
WIN = 512
BLK = 256
CHUNK = 128
TAP0 = 112
TAP_END = TAP0 + BLK - 1
ROOT_HALF = 0.7071067811865476
INV_ROOT_2PI = 0.3989422804014327
MESH = pl.DeviceIdType.MESH
SLOTS = 8
OW_ROWS, UP_ROWS, DN_ROWS = 24, 96, 96
SLICE = OW_ROWS + UP_ROWS + DN_ROWS
CUT = OW_ROWS + UP_ROWS
GCUT = 112
PARTS = ((0, OW_ROWS), (OW_ROWS, UP_ROWS), (CUT, DN_ROWS))
VM = pl.BlockSpec(memory_space=pltpu.VMEM)
SM = pl.BlockSpec(memory_space=pltpu.SMEM)
ANY = pl.BlockSpec(memory_space=pl.ANY)
DMA = pltpu.SemaphoreType.DMA


def nn(a, b, precision=None):
    return lax.dot_general(a, b, (((1,), (0,)), ((), ())), precision=precision, preferred_element_type=F32)


def nt(a, b, precision=None):
    return lax.dot_general(a, b, (((1,), (1,)), ((), ())), precision=precision, preferred_element_type=F32)


def tn(a, b, precision=None):
    return lax.dot_general(a, b, (((0,), (0,)), ((), ())), precision=precision, preferred_element_type=F32)


def block_mask(width):
    r = lax.broadcasted_iota(jnp.int32, (width, width), 0) // HD
    c = lax.broadcasted_iota(jnp.int32, (width, width), 1) // HD
    return r == c


def identity(width):
    r = lax.broadcasted_iota(jnp.int32, (width, width), 0)
    c = lax.broadcasted_iota(jnp.int32, (width, width), 1)
    return jnp.where(r == c, 1.0, 0.0).astype(F32)


def spread(x, heads, mask):
    return jnp.where(mask, jnp.concatenate([x] * heads, axis=0), 0.0)


def per_head_total(col, heads):
    tot = jnp.sum(col.reshape(heads, HD, 1), axis=1, keepdims=True)
    return jnp.broadcast_to(tot, (heads, HD, 1)).reshape(heads * HD, 1)


def members(length, count):
    s = lax.broadcasted_iota(jnp.int32, (LM, count), 1)
    j = lax.broadcasted_iota(jnp.int32, (LM, count), 0)
    s64 = s * LM
    return (j * length <= s64) & (s64 < (j + 1) * length) & (s < length)


def live_lanes(length, count):
    return lax.broadcasted_iota(jnp.int32, (1, count), 1) < length


def toeplitz(row):
    return pltpu.roll(jnp.broadcast_to(row, (BLK, WIN)), 0, 1, stride=1, stride_axis=0)


def windows(x, seq):
    pad = jnp.zeros((x.shape[0], 128), x.dtype)
    padded = jnp.concatenate([pad, x, pad], axis=1)
    return jnp.concatenate([padded[:, b * BLK : b * BLK + WIN] for b in range(seq // BLK)], axis=0)


def hi_lo(x):
    hi = x.astype(BF)
    return hi, (x - hi.astype(F32)).astype(BF)


def banded(x, row, heads, seq):
    outs = []
    for h in range(heads):
        wins = windows(x[h * HD : (h + 1) * HD], seq)
        hi, lo = hi_lo(toeplitz(row[h : h + 1]))
        y = nt(wins, hi) + nt(wins, lo)
        outs.append(jnp.concatenate([y[b * HD : (b + 1) * HD] for b in range(seq // BLK)], axis=1))
    return jnp.concatenate(outs, axis=0)


def flip(i, bit):
    return i + bit * (1 - 2 * ((i // bit) % 2))


def partner(i, m):
    for bit in (1, 2, 4):
        if m & bit:
            i = flip(i, bit)
    return i


def greet(peers):
    bar = pltpu.get_barrier_semaphore()
    for p in peers:
        pl.semaphore_signal(bar, inc=1, device_id=p, device_id_type=MESH)
    pl.semaphore_wait(bar, len(peers))


def rcopy(src, dst, ss, rs, dev):
    return pltpu.make_async_remote_copy(src_ref=src, dst_ref=dst, send_sem=ss, recv_sem=rs, device_id=dev, device_id_type=MESH)


class Net:
    def __init__(self, ssem, rsem):
        self.ssem, self.rsem, self.n = ssem, rsem, 0
        self.sent = []

    def copy(self, src, dst, dev, late=True):
        i = self.n
        self.n += 1
        c = rcopy(src, dst, self.ssem.at[i], self.rsem.at[i], dev)
        if late:
            self.sent.append(c)
        return c

    def drain(self):
        for c in self.sent:
            c.wait_send()
        self.sent = []


def at(i, steps):
    for k, f in steps.items():

        @pl.when(i == k)
        def _():
            f()


class Local:
    def __init__(self, sem):
        self.sem, self.n, self.open = sem, 0, []

    def start(self, src, dst):
        c = pltpu.make_async_copy(src, dst, self.sem.at[self.n])
        self.n += 1
        c.start()
        self.open.append(c)
        return c

    def finish(self):
        for c in self.open:
            c.wait()
        self.open = []


class Line:
    def __init__(self, parts):
        self.last, self.z = parts - 1, lax.axis_index("mp")

    def sends(self, way, s):
        z = self.z
        return (z < self.last) & (z >= s) if way == 0 else (z > 0) & (z + s <= self.last)

    def gets(self, way, s):
        z = self.z
        return z - 1 >= s if way == 0 else z + 1 + s <= self.last

    def sent_from(self, way, s):
        return self.z - (1 - 2 * way) * s

    def got_from(self, way, s):
        return self.z - (1 - 2 * way) * (s + 1)

    def ahead(self, way):
        size = self.last + 1
        return {"mp": lax.rem(self.z + (1 - 2 * way) + size, size)}


class Gather:
    def __init__(self, mp, srcs, wall, zsem, psem):
        self.line = Line(mp)
        self.srcs, self.wall, self.zsem, self.psem = srcs, wall, zsem, psem
        self.d = lax.axis_index("dp")
        r = lax.rem(self.d, SLOTS)
        self.rs = (r, flip(r, 4), flip(r, 2), partner(r, 6))
        self.steps = mp - 1

    def z(self, way, s, origin):
        dev = self.line.ahead(way)
        r = self.rs[0]
        out = []
        for i, (lo, size) in enumerate(PARTS):
            dst = self.wall.at[origin, r, pl.ds(lo, size)]
            src = self.srcs[i].at[r] if s == 0 else dst
            out.append(rcopy(src, dst, self.zsem.at[0, way, s, i], self.zsem.at[1, way, s, i], dev))
        return out

    def plane(self, way, s, k):
        w = self.wall.at[self.line.got_from(way, s)]
        q, rows, bit = (
            (0, (0, SLICE), 4),
            (0, (0, SLICE), 2),
            (1, (0, CUT), 2),
            (2, (CUT, DN_ROWS), 4),
            (0, (0, SLICE), 1),
            (1, (0, SLICE), 1),
            (2, (0, SLICE), 1),
            (3, (0, SLICE), 1),
        )[k]
        ref = w.at[self.rs[q], pl.ds(*rows)]
        return rcopy(ref, ref, self.psem.at[0, way, s, k], self.psem.at[1, way, s, k], {"dp": flip(self.d, bit)})

    def send(self, s):
        for way in range(2):

            @pl.when(self.line.sends(way, s))
            def _():
                for c in self.z(way, s, self.line.sent_from(way, s)):
                    c.start()

    def got(self, s, f):
        for way in range(2):
            pl.when(self.line.gets(way, s))(functools.partial(f, way, s))

    def step1(self, s):
        def arrive(way, s):
            for c in self.z(way, s, self.line.got_from(way, s)):
                c.wait_recv()

        self.got(s, arrive)
        if s + 1 < self.steps:
            self.send(s + 1)

        def pass_on(way, s):
            for k in (0, 1, 4):
                self.plane(way, s, k).start()

        self.got(s, pass_on)

    def step2(self, s):
        def f(way, s):
            self.plane(way, s, 0).wait_recv()
            self.plane(way, s, 2).start()
            self.plane(way, s, 5).start()
            self.plane(way, s, 1).wait_recv()
            self.plane(way, s, 3).start()
            self.plane(way, s, 6).start()

        self.got(s, f)

    def step3(self, s):
        def f(way, s):
            self.plane(way, s, 2).wait_recv()
            self.plane(way, s, 3).wait_recv()
            self.plane(way, s, 7).start()

        self.got(s, f)

    def finish(self):
        def f(way, s):
            for k in range(8):
                if k >= 4:
                    self.plane(way, s, k).wait_recv()
                self.plane(way, s, k).wait_send()

        for s in range(self.steps):
            self.got(s, f)
            for way in range(2):

                @pl.when(self.line.sends(way, s))
                def _():
                    for c in self.z(way, s, self.line.sent_from(way, s)):
                        c.wait_send()


def attn_fwd_kernel(docs, heads, seq, dest, len_ref, x_hbm, wt_ref, taps_ref, ow_ref, up_ref, dn_ref,
                    qkv_hbm, ctx_ref, lq_hbm, lk_hbm, sum_hbm, mix_hbm, k2_hbm, z_hbm, p_hbm, l1_ref, l3_ref, wall_ref,
                    x_s, qkv_s, lq_s, lk_s, sum_s, mix_s, k2_s, z_s, p_s, ctx_s, taps_s, lsem, asem, zsem, psem):
    width = heads * HD
    me, dd = lax.axis_index("mp"), lax.axis_index("dp")
    local = Local(lsem)
    loads = [local.start(x_hbm.at[d], x_s.at[d]) for d in range(docs)]
    local.open = []
    greet([{"mp": partner(me, m)} for m in range(1, dest)] + [{"dp": flip(dd, b)} for b in (1, 2, 4)])
    gather = Gather(dest, (ow_ref, up_ref, dn_ref), wall_ref, zsem, psem)
    gather.send(0)

    def a_copy(m, d):
        return rcopy(ctx_s.at[partner(me, m), d], ctx_ref.at[me, d], asem.at[0, m - 1, d], asem.at[1, m - 1, d], {"mp": partner(me, m)})

    taps_s[...] = jnp.zeros_like(taps_s)
    taps_s[:, TAP0 : TAP0 + KSIZE] = taps_ref[...]
    mask = block_mask(width)
    eye = identity(width)
    for c in loads:
        c.wait()

    def project(i, _):
        d, c = i // (seq // BLK), lax.rem(i, seq // BLK)
        rows = pl.ds(pl.multiple_of(c * BLK, BLK), BLK)
        qkv_s[d, :, rows] = nt(wt_ref[...], x_s[d, rows, :]).astype(BF)
        return 0

    lax.fori_loop(0, docs * (seq // BLK), project, 0)
    local.start(qkv_s, qkv_hbm)

    def landmarks(d, _):
        length = len_ref[d]
        memb = jnp.where(members(length, seq), 1.0, 0.0).astype(F32)
        counts = jnp.maximum(jnp.sum(memb, axis=1, keepdims=True), 1.0)
        memb_b = memb.astype(BF)
        q = qkv_s[d, 0:width, :]
        k = qkv_s[d, width : 2 * width, :]
        v = qkv_s[d, 2 * width : 3 * width, :]
        lq = spread(nt(memb_b, q) / counts, heads, mask).astype(BF)
        lk = spread(nt(memb_b, k) / counts, heads, mask).astype(BF)
        lq_s[d] = lq
        lk_s[d] = lk
        s2 = jnp.where(mask, nt(lq, lk) * SCALE, -1e30)
        e2 = jnp.where(mask, jnp.exp(s2 - jnp.max(s2, axis=1, keepdims=True)), 0.0)
        k2_s[d] = e2 / jnp.sum(e2, axis=1, keepdims=True)
        s3 = jnp.where(live_lanes(length, seq), nn(lq, k) * SCALE, -1e30)
        m3 = jnp.max(s3, axis=1, keepdims=True)
        e3 = jnp.exp(s3 - m3)
        t3 = jnp.sum(e3, axis=1, keepdims=True)
        l3_ref[d] = jnp.broadcast_to(m3 + jnp.log(t3), (width, 128))
        k3 = (e3 / t3).astype(BF)
        sum_s[d] = jnp.where(mask, nt(k3, v), 0.0)
        at(d, {0: lambda: (gather.step1(0),), 1: lambda: (gather.step1(1),)})
        return 0

    lax.fori_loop(0, docs, landmarks, 0)
    for src, dst in ((lq_s, lq_hbm), (lk_s, lk_hbm), (k2_s, k2_hbm), (sum_s, sum_hbm)):
        local.start(src, dst)
    for d in range(docs):
        k2 = k2_s[d]
        z_s[d, 0] = k2.T / per_head_total(jnp.sum(k2 * k2, axis=1, keepdims=True), heads)

    def newton(i, _):
        k2s = [k2_s[d] for d in range(docs)]
        zs = [z_s[d, i] for d in range(docs)]
        ps = [nn(k2s[d], zs[d], HI) for d in range(docs)]
        bs = [15.0 * eye - nn(ps[d], 7.0 * eye - ps[d], HI) for d in range(docs)]
        cs = [13.0 * eye - nn(ps[d], bs[d], HI) for d in range(docs)]
        zs = [0.25 * nn(zs[d], cs[d], HI) for d in range(docs)]
        for d in range(docs):
            p_s[d, i, 0] = ps[d]
            p_s[d, i, 1] = bs[d]
            p_s[d, i, 2] = cs[d]
            z_s[d, i + 1] = zs[d]
        at(i, {3: lambda: (gather.step1(2), gather.step2(0),)})
        return 0

    lax.fori_loop(0, NS_ITERS, newton, 0)
    local.start(z_s, z_hbm)
    local.start(p_s, p_hbm)
    part = seq // dest

    def contexts(d, _):
        length = len_ref[d]
        q = qkv_s[d, 0:width, :]
        v = qkv_s[d, 2 * width : 3 * width, :]
        live = live_lanes(length, seq)
        mix = jnp.where(mask, nn(z_s[d, NS_ITERS], sum_s[d], HI), 0.0)
        mix_s[d] = mix.astype(BF)
        s1 = (nn(lk_s[d], q) * SCALE).reshape(heads, LM, seq)
        m1 = jnp.max(s1, axis=1, keepdims=True)
        e1 = jnp.exp(s1 - m1)
        t1 = jnp.sum(e1, axis=1, keepdims=True)
        l1_ref[d] = (m1 + jnp.log(t1)).reshape(heads, seq)
        k1 = (e1 / t1).reshape(width, seq).astype(BF)
        vl = jnp.where(live, v, 0).astype(BF)
        ctx = nn(mix.T.astype(BF), k1) + banded(vl, taps_s[...], heads, seq)
        ctx = jnp.where(live, ctx, 0.0).astype(BF)
        for i in range(dest):
            ctx_s[i, d] = ctx[:, i * part : (i + 1) * part]
        for m in range(1, dest):
            a_copy(m, d).start()
        ctx_ref[me, d] = ctx_s[me, d]
        at(d, {0: lambda: (gather.step3(0), gather.step2(1), gather.step2(2),)})
        return 0

    lax.fori_loop(0, docs, contexts, 0)
    local.start(mix_s, mix_hbm)
    gather.step3(1)
    gather.step3(2)
    gather.finish()
    for d in range(docs):
        for m in range(1, dest):
            a_copy(m, d).wait()
    local.finish()


def attn_fwd(lengths, x, wt, taps, ow, up, dn, dest):
    docs, seq, dim = x.shape
    width = wt.shape[0] // 3
    heads = width // HD
    sds = jax.ShapeDtypeStruct
    kept = [
        sds((docs, 3 * width, seq), BF),
        sds((docs, width, width), BF),
        sds((docs, width, width), BF),
        sds((docs, width, width), F32),
        sds((docs, width, width), BF),
        sds((docs, width, width), F32),
        sds((docs, NS_ITERS + 1, width, width), F32),
        sds((docs, NS_ITERS, 3, width, width), F32),
    ]
    out = [kept[0], sds((dest, docs, width, seq // dest), BF)] + kept[1:] + [
        sds((docs, heads, seq), F32),
        sds((docs, width, 128), F32),
        sds((dest, SLOTS, SLICE, dim), BF),
    ]
    return pl.pallas_call(
        functools.partial(attn_fwd_kernel, docs, heads, seq, dest),
        out_shape=out,
        in_specs=[SM, ANY, VM, VM, ANY, ANY, ANY],
        out_specs=[ANY, VM] + [ANY] * 7 + [VM, VM, ANY],
        scratch_shapes=[pltpu.VMEM((docs, seq, dim), BF)]
        + [pltpu.VMEM(t.shape, t.dtype) for t in kept]
        + [
            pltpu.VMEM((dest, docs, width, seq // dest), BF),
            pltpu.VMEM((heads, WIN), F32),
            DMA((16,)),
            DMA((2, dest - 1, docs)),
            DMA((2, 2, dest - 1, 3)),
            DMA((2, 2, dest - 1, 8)),
        ],
        compiler_params=pltpu.CompilerParams(vmem_limit_bytes=60 * 2**20, collective_id=0, has_side_effects=True),
        cost_estimate=pl.CostEstimate(flops=int(8e9), bytes_accessed=int(3e7), transcendentals=0),
        name="attn_fwd",
    )(lengths, x, wt, taps, ow, up, dn)


def ln_stats(v):
    mu = jnp.mean(v, axis=-1, keepdims=True)
    cen = v - mu
    var = jnp.mean(cen * cen, axis=-1, keepdims=True)
    r = lax.rsqrt(var + EPS)
    return cen * r, r


def ln_back(g, xhat, r):
    m1 = jnp.mean(g, axis=-1, keepdims=True)
    m2 = jnp.mean(g * xhat, axis=-1, keepdims=True)
    return r * (g - m1 - xhat * m2)


class Spread:
    def __init__(self, parts, buf, sem):
        self.line, self.buf, self.sem = Line(parts), buf, sem

    def one(self, way, s, d, origin, src=None):
        dst = self.buf.at[d, origin]
        return rcopy(dst if src is None else src, dst, self.sem.at[way, 0, s, d], self.sem.at[way, 1, s, d], self.line.ahead(way))

    def start(self, s, d, src=None):
        for way in range(2):

            @pl.when(self.line.sends(way, s))
            def _():
                self.one(way, s, d, self.line.sent_from(way, s), src).start()

    def wait(self, s, d):
        for way in range(2):

            @pl.when(self.line.gets(way, s))
            def _():
                self.one(way, s, d, self.line.got_from(way, s)).wait_recv()

    def sent(self, s, d, src=None):
        for way in range(2):

            @pl.when(self.line.sends(way, s))
            def _():
                self.one(way, s, d, self.line.sent_from(way, s), src).wait_send()


def ffn_kernel(groups, docs, rows, len_ref, x_hbm, cot_hbm, ctx_ref, ow_hbm, up_hbm, dn_hbm, wall_hbm, g1_ref, b1_ref, g2_ref, b2_ref,
               out_hbm, gmix_ref, gctx_ref, s1_hbm, small_ref,
               x_s, cot_s, w_s, rc_s, gc_s, nb_s, fac_s, act_s, gp_s, br_s, x1_s, gn_s, ga_s, o_s, s1_s, lsem, csem, osem, asem):
    n = docs * rows
    dim = x_s.shape[-1]
    z, dd = lax.axis_index("mp"), lax.axis_index("dp")
    kk = lax.rem(dd, 2)
    local = Local(lsem)
    mine = pl.ds(pl.multiple_of(z * rows, rows), rows)
    others = [partner(z, m) for m in range(1, groups)]
    heads_first = [local.start(ow_hbm, w_s.at[z, :, :, pl.ds(*PARTS[0])])]
    heads_first += [local.start(wall_hbm.at[g, :, :, pl.ds(*PARTS[0])], w_s.at[g, :, :, pl.ds(*PARTS[0])]) for g in others]
    heads_first += [local.start(x_hbm.at[d, mine], x_s.at[pl.ds(d * rows, rows)]) for d in range(docs)]
    rest = [local.start(up_hbm, w_s.at[z, :, :, pl.ds(*PARTS[1])]), local.start(dn_hbm, w_s.at[z, :, :, pl.ds(*PARTS[2])])]
    body = pl.ds(OW_ROWS, SLICE - OW_ROWS)
    rest += [local.start(wall_hbm.at[g, :, :, body], w_s.at[g, :, :, body]) for g in others]
    rest += [local.start(cot_hbm.at[d, mine], cot_s.at[pl.ds(d * rows, rows)]) for d in range(docs)]
    local.open = []
    greet([{"mp": partner(z, m)} for m in range(1, groups)] + [{"dp": flip(dd, 1)}])

    def back_copy(m, d):
        return rcopy(gc_s.at[m - 1, d], gctx_ref.at[z, d], asem.at[0, m - 1, d], asem.at[1, m - 1, d], {"mp": partner(z, m)})

    spread_out = Spread(groups, out_hbm, osem)

    def core_copy(g, part):
        lo, size = ((OW_ROWS, SLICE - OW_ROWS), (0, OW_ROWS))[part]
        return rcopy(w_s.at[g, :, 1 - kk, pl.ds(lo, size)], rc_s.at[g, :, pl.ds(lo, size)], csem.at[0, g, part], csem.at[1, g, part], {"dp": flip(dd, 1)})

    def take(g, part):
        lo, size = PARTS[part]
        return w_s[g, :, :, lo : lo + size, :].reshape(SLOTS * size, dim)

    def put(g, part, val):
        lo, size = PARTS[part]
        w_s[g, :, :, lo : lo + size, :] = val.astype(BF).reshape(SLOTS // 2, 2, size, dim)

    first = z * rows
    gain1, bias1 = g1_ref[...].reshape(1, dim), b1_ref[...].reshape(1, dim)
    gain2, bias2 = g2_ref[...].reshape(1, dim), b2_ref[...].reshape(1, dim)
    for c in heads_first:
        c.wait()
    small_ref[...] = jnp.zeros_like(small_ref)

    def doc(d, _):
        here = pl.ds(pl.multiple_of(d * rows, rows), rows)
        live = (lax.broadcasted_iota(jnp.int32, (rows, 1), 0) + first < len_ref[d]).astype(F32)
        mixed = x_s[here].astype(F32)
        for g in range(groups):
            mixed = mixed + tn(ctx_ref[g, d], take(g, 0)).astype(BF).astype(F32)
        xh1, r1 = ln_stats(mixed)
        x1_s[...] = xh1
        normed = xh1 * gain1 + bias1
        nb_s[here] = normed.astype(BF)
        br_s[...] = normed

        @pl.when(d == 0)
        def _():
            for c in rest:
                c.wait()

        def fwd_group(g, _):
            h = nn(nb_s[here], take(g, 1))
            phi_big = 0.5 * (1.0 + lax.erf(h * ROOT_HALF))
            act = (h * phi_big).astype(BF)
            act_s[g, here] = act
            fac_s[g] = phi_big + h * (jnp.exp(-0.5 * h * h) * INV_ROOT_2PI)
            br_s[...] += nn(act, take(g, 2)).astype(BF).astype(F32)
            return 0

        lax.fori_loop(0, groups, fwd_group, 0, unroll=True)
        xh2, r2 = ln_stats(br_s[...])
        o_s[d] = (live * (xh2 * gain2 + bias2)).astype(BF)

        @pl.when(d == 0)
        def _():
            spread_out.start(0, 0, o_s.at[0])

        g_out = live * cot_s[here].astype(F32)
        gg2 = jnp.sum(g_out * xh2, axis=0, keepdims=True)
        gb2 = jnp.sum(g_out, axis=0, keepdims=True)
        g_res = ln_back(g_out * gain2, xh2, r2)
        gn_s[...] = g_res
        gbr_s[here] = g_res.astype(BF)

        def back_group(g, _):
            g_pre = (nt(gbr_s[here], take(g, 2)) * fac_s[g]).astype(BF)
            gp_s[g, here] = g_pre
            gn_s[...] += nt(g_pre, take(g, 1))
            return 0

        lax.fori_loop(0, groups, back_group, 0)
        g_n = gn_s[...]
        xh1 = x1_s[...]
        gg1 = jnp.sum(g_n * xh1, axis=0, keepdims=True)
        gb1 = jnp.sum(g_n, axis=0, keepdims=True)
        small_ref[...] += jnp.concatenate([gg1, gb1, gg2, gb2, jnp.zeros((4, dim), F32)], axis=0)
        g_mix = ln_back(g_n * gain1, xh1, r1)
        gmix_ref[d] = g_mix
        g_att = g_mix.astype(BF)
        ga_s[here] = g_att
        for m in reversed(range(groups)):
            t = nt(take(partner(z, m), 0), g_att).astype(BF)
            if m:
                gc_s[m - 1, d] = t
                back_copy(m, d).start()
            else:
                gctx_ref[z, d] = t
        return 0

    gbr_s = cot_s
    lax.fori_loop(0, docs, doc, 0)
    for d in range(docs):
        local.start(o_s.at[d], out_hbm.at[d, z])

    def weight_group(g, _):
        put(g, 2, tn(act_s[g], gbr_s[...]))
        put(g, 1, tn(nb_s[...], gp_s[g]))
        core_copy(g, 0).start()
        return 0

    lax.fori_loop(0, groups, weight_group, 0)
    for g in range(groups):
        acc = None
        for d in range(docs):
            t = nn(ctx_ref[g, d], ga_s[d * rows : (d + 1) * rows])
            acc = t if acc is None else acc + t
        put(g, 0, acc)
        core_copy(g, 1).start()

    def add_group(g, _):
        core_copy(g, 0).wait_recv()
        core_copy(g, 1).wait_recv()

        def add_slot(j, _):
            s1_s[g, j // 2, j % 2] = (w_s[g, j, kk].astype(F32) + rc_s[g, j].astype(F32)).astype(BF)
            return 0

        lax.fori_loop(0, SLOTS // 2, add_slot, 0)
        return 0

    lax.fori_loop(0, groups, add_group, 0)
    local.start(s1_s, s1_hbm)
    for m in range(1, groups):
        for d in range(docs):
            back_copy(m, d).wait()
    spread_out.wait(0, 0)
    spread_out.sent(0, 0, o_s.at[0])
    for g in range(groups):
        for part in range(2):
            core_copy(g, part).wait_send()
    local.finish()


def ffn(lengths, x, cot, ctx, ow, up, dn, wall, g1, b1, g2, b2):
    docs, seq, dim = x.shape
    groups, _, width, rows = ctx.shape
    ff = SLOTS * UP_ROWS
    n = docs * rows
    sds = jax.ShapeDtypeStruct
    out = [
        sds((docs, groups, rows, dim), BF),
        sds((docs, rows, dim), F32),
        sds((groups, docs, width, rows), BF),
        sds((groups, 2, 2, SLICE, dim), BF),
        sds((8, dim), F32),
    ]
    wall = wall.reshape(groups, SLOTS // 2, 2, SLICE, dim)
    ow, up, dn = (t.reshape(SLOTS // 2, 2, -1, dim) for t in (ow, up, dn))
    return pl.pallas_call(
        functools.partial(ffn_kernel, groups, docs, rows),
        out_shape=out,
        in_specs=[SM, ANY, ANY, VM, ANY, ANY, ANY, ANY, VM, VM, VM, VM],
        out_specs=[ANY, VM, VM, ANY, VM],
        scratch_shapes=[
            pltpu.VMEM((n, dim), BF),
            pltpu.VMEM((n, dim), BF),
            pltpu.VMEM((groups, SLOTS // 2, 2, SLICE, dim), BF),
            pltpu.VMEM((groups, SLOTS // 2, SLICE, dim), BF),
            pltpu.VMEM((groups - 1, docs, width, rows), BF),
            pltpu.VMEM((n, dim), BF),
            pltpu.VMEM((groups, rows, ff), F32),
            pltpu.VMEM((groups, n, ff), BF),
            pltpu.VMEM((groups, n, ff), BF),
            pltpu.VMEM((rows, dim), F32),
            pltpu.VMEM((rows, dim), F32),
            pltpu.VMEM((rows, dim), F32),
            pltpu.VMEM((n, dim), BF),
            pltpu.VMEM((docs, rows, dim), BF),
            pltpu.VMEM((groups, 2, 2, SLICE, dim), BF),
            DMA((24,)),
            DMA((2, groups, 2)),
            DMA((2, 2, groups - 1, docs)),
            DMA((2, groups - 1, docs)),
        ],
        compiler_params=pltpu.CompilerParams(vmem_limit_bytes=62 * 2**20, collective_id=1, has_side_effects=True),
        cost_estimate=pl.CostEstimate(flops=int(1.8e10), bytes_accessed=int(4e7), transcendentals=0),
        name="ffn",
    )(lengths, x, cot, ctx, ow, up, dn, wall, g1, b1, g2, b2)


def attn_bwd_kernel(docs, heads, seq, parts, dp, len_ref, x_hbm, wt_ref, taps_ref, qkv_ref, gctx_ref, lq_ref, lk_ref, sum_ref, mix_ref, k2_ref,
                    z_hbm, p_hbm, l1_ref, l3_ref, s1, small_in, gmix_hbm, out_in, gq, ig, taps_out, gw, small, out_hbm,
                    x_s, z_s, p_s, gmix_s, g_s, gs1_s, gs3_s, ginv_s, glq_s, glk_s, gz_s, gk_s, taps_s, gacc_s,
                    ipart, ri, ra1, rb1, rz, fin, rfin, rq0, rq1, rq2, gqb, q, rsm, rtp, lsem, ssem, rsem, isem, osem, pz, acc, gsem):
    width = heads * HD
    nblk = seq // BLK
    dim = x_s.shape[-1]
    zi = lax.axis_index("mp")
    local = Local(lsem)
    loads = [local.start(a, b) for a, b in ((z_hbm, z_s), (p_hbm, p_s), (x_hbm, x_s), (gmix_hbm, gmix_s))]
    local.open = []
    nd = Sums(docs, seq, parts, dp, locals())
    nd.begin()
    out = Spread(parts, out_hbm, osem)
    left = [(s, d) for s in range(parts - 1) for d in range(docs) if (s, d) != (0, 0)]
    waves = [[(0, d) for d in range(1, docs)] + [(1, 0)]]
    waves += [[(s, d) for d in range(1, docs)] + [(s + 1, 0)] for s in range(1, parts - 2)] + [[(parts - 2, d) for d in range(1, docs)]]

    def out_step(i):
        for s, d in waves[i] if i < len(waves) else ():
            if s > 0 and (s - 1, d) != (0, 0):
                out.wait(s - 1, d)
            out.start(s, d)

    out_step(0)
    taps_s[...] = jnp.zeros_like(taps_s)
    taps_s[:, TAP0 : TAP0 + KSIZE] = taps_ref[...]
    mask = block_mask(width)
    eye = identity(width)
    anti = jnp.where(
        lax.broadcasted_iota(jnp.int32, (BLK, BLK), 0) + lax.broadcasted_iota(jnp.int32, (BLK, BLK), 1) == BLK - 1, 1.0, 0.0
    ).astype(BF)
    gacc_s[...] = jnp.zeros_like(gacc_s)

    def doc(d, _):
        length = len_ref[d]
        live = live_lanes(length, seq)
        q_ = qkv_ref[d, 0:width, :]
        k = qkv_ref[d, width : 2 * width, :]
        v = qkv_ref[d, 2 * width : 3 * width, :]
        gc = jnp.concatenate([gctx_ref[i, d] for i in range(parts)], axis=1)
        gc = jnp.where(live, gc, 0).astype(BF)
        lq, lk = lq_ref[d], lk_ref[d]
        s1_ = (nn(lk, q_) * SCALE).reshape(heads, LM, seq)
        k1 = jnp.exp(s1_ - l1_ref[d].reshape(heads, 1, seq))
        gmixing = jnp.where(mask, nt(k1.reshape(width, seq).astype(BF), gc), 0.0)
        gk1 = nn(mix_ref[d], gc).reshape(heads, LM, seq)
        gs1 = (k1 * (gk1 - jnp.sum(gk1 * k1, axis=1, keepdims=True))).reshape(width, seq).astype(BF)
        gz_s[d] = nt(gmixing, sum_ref[d], HI)
        gk_s[d] = jnp.zeros((width, width), F32)
        gsum = jnp.where(mask, tn(ginv_s[d], gmixing, HI), 0.0)
        gsum_b = gsum.astype(BF)
        s3 = jnp.where(live, nn(lq, k) * SCALE, -1e30)
        k3 = jnp.exp(s3 - l3_ref[d][:, 0:1])
        gk3 = nn(gsum_b, v)
        gs3 = (k3 * (gk3 - jnp.sum(gk3 * k3, axis=1, keepdims=True))).astype(BF)
        at(d, {1: lambda: out_step(1)})
        glq_s[d] = jnp.where(mask, nt(gs3, k), 0.0) * SCALE
        glk_s[d] = jnp.where(mask, nt(gs1, q_), 0.0) * SCALE
        gs1_s[d] = gs1
        gs3_s[d] = gs3
        gv = nn(gsum.T.astype(BF), k3.astype(BF))
        gvl = banded(gc, taps_s[...], heads, seq)
        g_s[d, 2 * width : 3 * width, :] = (gv + jnp.where(live, gvl, 0.0)).astype(BF)
        vl = jnp.where(live, v, 0).astype(BF)
        for h in range(heads):
            wins = windows(vl[h * HD : (h + 1) * HD], seq)
            gch = gc[h * HD : (h + 1) * HD]
            stack = jnp.concatenate([gch[:, b * BLK : (b + 1) * BLK] for b in range(nblk)], axis=0)
            gacc_s[h] += nn(nt(anti, stack).astype(BF), wins)
        at(d, {i: functools.partial(nd.small_step, 1 + i) for i in range(docs)})
        return 0

    loads[0].wait()
    for d in range(docs):
        ginv_s[d] = z_s[d, NS_ITERS]
    lax.fori_loop(0, docs, doc, 0)
    for h in range(heads):
        rolled = pltpu.roll(gacc_s[h], 0, 1, stride=1, stride_axis=0)
        taps_out[h : h + 1, :] = jnp.sum(rolled, axis=0, keepdims=True)
    loads[1].wait()

    def newton_back(j, _):
        i = NS_ITERS - 1 - j
        for d in range(docs):
            z, p, b, c = z_s[d, i], p_s[d, i, 0], p_s[d, i, 1], p_s[d, i, 2]
            a = 7.0 * eye - p
            g = 0.25 * gz_s[d]
            gc_ = tn(z, g, HI)
            gp = -nt(gc_, b, HI)
            gb = -tn(p, gc_, HI)
            gp = gp - nt(gb, a, HI)
            ga = -tn(p, gb, HI)
            gp = gp - ga
            gk_s[d] += nt(gp, z, HI)
            gz_s[d] = nt(g, c, HI) + tn(k2_ref[d], gp, HI)
        base = 1 + docs
        at(j, {
            1: lambda: (nd.small_step(base), nd.taps_step(0)),
            3: lambda: (nd.small_step(base + 1), nd.taps_step(1), nd.g_step1()),
            5: lambda: (nd.small_step(base + 2), nd.taps_step(2), out_step(2)),
        })
        return 0

    lax.fori_loop(0, NS_ITERS, newton_back, 0)
    for c in loads[2:]:
        c.wait()

    def finish(d, _):
        length = len_ref[d]
        k2 = k2_ref[d]
        tot = per_head_total(jnp.sum(k2 * k2, axis=1, keepdims=True), heads)
        g = gz_s[d]
        dot = per_head_total(jnp.sum(g * k2.T, axis=1, keepdims=True), heads)
        gk2 = gk_s[d] + (g / tot).T - k2 * (2.0 * dot / (tot * tot))
        gs2 = k2 * (gk2 - jnp.sum(gk2 * k2, axis=1, keepdims=True)) * SCALE
        memb = jnp.where(members(length, seq), 1.0, 0.0).astype(F32)
        counts = jnp.maximum(jnp.sum(memb, axis=1, keepdims=True), 1.0)
        counts = jnp.concatenate([counts] * heads, axis=0)
        memb3 = jnp.concatenate([memb.astype(BF)] * heads, axis=0)
        lq, lk = lq_ref[d].astype(F32), lk_ref[d].astype(F32)
        glq = (glq_s[d] + nn(gs2, lk, HI)) / counts
        glk = (glk_s[d] + tn(gs2, lq, HI)) / counts
        hi, lo = hi_lo(glq.T)
        gq_ = nn(lk.T.astype(BF), gs1_s[d]) * SCALE + nn(hi, memb3) + nn(lo, memb3)
        hi, lo = hi_lo(glk.T)
        gk_ = nn(lq.T.astype(BF), gs3_s[d]) * SCALE + nn(hi, memb3) + nn(lo, memb3)
        g_s[d, 0:width, :] = gq_.astype(BF)
        g_s[d, width : 2 * width, :] = gk_.astype(BF)

        def inputs(c, _):
            rows = pl.ds(pl.multiple_of(c * BLK, BLK), BLK)
            t = tn(g_s[d, :, rows], wt_ref[...])
            t = (t + jnp.where(zi == c, 1.0, 0.0) * gmix_s[d]).astype(BF)
            per = BLK // CHUNK
            ipart[d, pl.ds(c * per, per)] = t.reshape(per, CHUNK, dim)
            return 0

        lax.fori_loop(0, nblk, inputs, 0)
        return 0

    lax.fori_loop(0, docs, finish, 0)
    for i in range(3, len(waves)):
        out_step(i)
    nd.i_time(0)

    def weights(c, _):
        rows = pl.ds(pl.multiple_of(c * width, width), width)
        acc_q = nn(g_s[0, rows], x_s[0])
        for d in range(1, docs):
            acc_q = acc_q + nn(g_s[d, rows], x_s[d])
        gqb[rows] = acc_q.astype(BF)
        return 0

    lax.fori_loop(0, 3, weights, 0)
    nd.tail()
    for s, d in left:
        if s == parts - 2:
            out.wait(s, d)
    for s, d in left:
        out.sent(s, d)


class Sums:
    def __init__(self, docs, seq, parts, dp, refs):
        for name in ("pz", "acc", "gsem", "s1", "small_in", "gq", "ig", "taps_out", "gw", "small", "ipart", "ri", "ra1", "rb1", "rz", "fin", "rfin", "rq0", "rq1", "rq2", "gqb", "q", "rsm", "rtp", "ssem", "rsem", "isem"):
            setattr(self, name, refs[name])
        self.docs, self.parts = docs, parts
        self.z, self.d = lax.axis_index("mp"), lax.axis_index("dp")
        self.r = lax.rem(self.d, SLOTS)
        self.y, self.x, self.k = self.r // 4, lax.rem(self.r // 2, 2), lax.rem(self.r, 2)
        self.net = Net(self.ssem, self.rsem)
        self.extra = [b for b in (8, 16, 32, 64, 128) if b < dp]
        self.bits = [1, 2, 4] + self.extra

    def dev(self, bit):
        return {"dp": flip(self.d, bit)}

    def zdev(self, m):
        return {"mp": partner(self.z, m)}

    def begin(self):
        greet([self.zdev(m) for m in range(1, self.parts)] + [self.dev(b) for b in self.bits])
        self.i_setup()
        self.line = Line(self.parts)
        c = self.net.copy
        low, high = pl.ds(0, GCUT), pl.ds(GCUT, SLICE - GCUT)
        self.a1 = c(self.s1.at[:, 1 - self.y, :, low], self.ra1, self.dev(4))
        self.b1 = c(self.s1.at[:, :, 1 - self.x, high], self.rb1, self.dev(2))
        self.a1.start()
        self.b1.start()
        self.a2 = c(self.ra1.at[:, 1 - self.x], self.pz.at[:, low], self.dev(2))
        self.b2 = c(self.rb1.at[:, 1 - self.y], self.pz.at[:, high], self.dev(4))
        r, gw = self.r, self.gw
        r4, r2, r6 = flip(r, 4), flip(r, 2), partner(r, 6)
        self.gy = c(gw.at[r], gw.at[r], self.dev(4))
        self.gx = c(gw.at[r], gw.at[r], self.dev(2))
        self.gyx = c(gw.at[r4, low], gw.at[r4, low], self.dev(2))
        self.gxy = c(gw.at[r2, high], gw.at[r2, high], self.dev(4))
        self.gc = [c(gw.at[i], gw.at[i], self.dev(1)) for i in (r, r4, r2, r6)]
        h = self.gqb.shape[0] // 2
        self.half = h
        mine, other = (pl.ds(pl.multiple_of(k * h, 8), h) for k in (self.k, 1 - self.k))
        self.mine = mine
        self.q0 = c(self.gqb.at[other], self.rq0, self.dev(1))
        self.qa = self.q_pair(self.rq1, 4, 2)
        self.qb = self.q_pair(self.rq2.at[0], 2, 4)
        self.qc = c(self.gq.at[mine], self.gq.at[mine], self.dev(1))
        self.extras = [(c(self.fin, self.rfin.at[i], self.dev(b), late=False), c(self.q, self.rq2.at[1 + i], self.dev(b), late=False)) for i, b in enumerate(self.extra)]
        self.small[...] = self.small_in[...]
        zs = [self.zdev(1 << j) for j in range(self.parts.bit_length() - 1)]
        self.smalls = [c(self.small, self.rsm.at[i], dev, late=False) for i, dev in enumerate([self.dev(b) for b in self.bits] + zs)]
        self.tapsums = [c(self.taps_out, self.rtp.at[i], self.dev(b), late=False) for i, b in enumerate(self.bits)]
        self.small_step(0)

    def exchange(self, copies, buf, recv, i):
        if 0 < i <= len(copies):
            copies[i - 1].wait()
            buf[...] = buf[...] + recv[i - 1]
        if i < len(copies):
            copies[i].start()

    def small_step(self, i):
        self.exchange(self.smalls, self.small, self.rsm, i)

    def taps_step(self, i):
        self.exchange(self.tapsums, self.taps_out, self.rtp, i)

    def double(self, c, buf, recv):
        c.start()
        c.wait()
        buf[...] = (buf[...].astype(F32) + recv[...].astype(F32)).astype(buf.dtype)

    def g_step1(self):
        self.a1.wait_recv()
        self.b1.wait_recv()

        def add(i, _):
            g, j = i // 2, i % 2
            self.ra1[g, j] = (self.ra1[g, j].astype(F32) + self.s1[g, self.y, j, 0:GCUT].astype(F32)).astype(BF)
            self.rb1[g, j] = (self.rb1[g, j].astype(F32) + self.s1[g, j, self.x, GCUT:SLICE].astype(F32)).astype(BF)
            return 0

        lax.fori_loop(0, 2 * self.parts, add, 0)
        self.a2.start()
        self.b2.start()

    def g_step2(self):
        self.a2.wait_recv()
        self.b2.wait_recv()

        def add(g, _):
            self.pz[g, 0:GCUT] = (self.pz[g, 0:GCUT].astype(F32) + self.ra1[g, self.x].astype(F32)).astype(BF)
            self.pz[g, GCUT:SLICE] = (self.pz[g, GCUT:SLICE].astype(F32) + self.rb1[g, self.y].astype(F32)).astype(BF)
            return 0

        lax.fori_loop(0, self.parts, add, 0)
        self.z_hop(0)

    def z_piece(self, way, s):
        last = self.parts - 1
        g = last - s + self.z if way == 0 else s - last + self.z
        return g, (self.z <= s) & (self.z < last) if way == 0 else (last - self.z <= s) & (self.z > 0)

    def z_copy(self, way, s, g):
        return rcopy(self.pz.at[g], self.rz.at[way, s], self.gsem.at[0, way, s], self.gsem.at[1, way, s], self.line.ahead(way))

    def z_hop(self, s):
        last = self.parts - 1
        for way in range(2):
            g, ok = self.z_piece(way, s)
            inner = self.z > 0 if way == 0 else self.z < last

            if s > 0:

                @pl.when(ok & inner)
                def _():
                    self.z_copy(way, s - 1, 0).wait_recv()
                    self.pz[g] = (self.pz[g].astype(F32) + self.rz[way, s - 1].astype(F32)).astype(BF)

            @pl.when(ok)
            def _():
                self.z_copy(way, s, g).start()

    def z_done(self):
        last = self.parts - 1
        for way in range(2):
            for s in range(last):
                g, ok = self.z_piece(way, s)

                @pl.when(ok)
                def _():
                    self.z_copy(way, s, g).wait_send()

    def g_step3(self):
        last = self.parts - 1
        self.acc[...] = self.pz[self.z].astype(F32)
        for way in range(2):

            @pl.when(self.z > 0 if way == 0 else self.z < last)
            def _():
                self.z_copy(way, last - 1, 0).wait_recv()
                self.acc[...] += self.rz[way, last - 1].astype(F32)

        self.fin[...] = self.acc[...].astype(BF)
        for i, (c, _) in enumerate(self.extras):
            self.double(c, self.fin, self.rfin.at[i])
        self.gw[self.r] = self.fin[...]
        self.gy.start()
        self.gx.start()
        self.gc[0].start()

    def g_step4(self):
        self.gy.wait_recv()
        self.gyx.start()
        self.gc[1].start()
        self.gx.wait_recv()
        self.gxy.start()
        self.gc[2].start()

    def g_step5(self):
        self.gyx.wait_recv()
        self.gxy.wait_recv()
        self.gc[3].start()
        for s in self.gc:
            s.wait_recv()

    def q_pair(self, recv, a, b):
        h = self.half // 2
        return [
            self.net.copy(self.q.at[pl.ds(0, h)], recv.at[pl.ds(0, h)], self.dev(a), late=False),
            self.net.copy(self.q.at[pl.ds(h, h)], recv.at[pl.ds(h, h)], self.dev(b), late=False),
        ]

    def q_step0(self):
        self.q0.start()

    def q_step1(self):
        self.q0.wait_recv()
        self.q[...] = (self.gqb[self.mine].astype(F32) + self.rq0[...].astype(F32)).astype(BF)
        for s in self.qa:
            s.start()

    def q_step2(self):
        for s in self.qa:
            s.wait()
        self.q[...] = (self.q[...].astype(F32) + self.rq1[...].astype(F32)).astype(BF)
        for s in self.qb:
            s.start()

    def q_step3(self):
        for s in self.qb:
            s.wait()
        self.q[...] = (self.q[...].astype(F32) + self.rq2[0].astype(F32)).astype(BF)
        for i, (_, c) in enumerate(self.extras):
            self.double(c, self.q, self.rq2.at[1 + i])
        self.gq[self.mine] = self.q[...]
        self.qc.start()

    def i_setup(self):
        last = self.parts - 1
        self.chunks = self.ipart.shape[1]
        self.pos, self.lower, self.upper = [], [], []
        for d in range(self.docs):
            step = 1 if d % 2 == 0 else -1
            self.pos.append(self.z if d % 2 == 0 else last - self.z)
            self.lower.append({"mp": lax.rem(self.z - step + self.parts, self.parts)})
            self.upper.append({"mp": lax.rem(self.z + step + self.parts, self.parts)})

    def red(self, d, c):
        return rcopy(self.ipart.at[d, c], self.ri.at[d, c], self.isem.at[0, d, c], self.isem.at[1, d, c], self.lower[d])

    def bc(self, d, c):
        return rcopy(self.ig.at[d, c], self.ig.at[d, c], self.isem.at[2, d, c], self.isem.at[3, d, c], self.upper[d])

    def i_time(self, t):
        last = self.parts - 1
        for d in range(self.docs):
            p = self.pos[d]
            c = t - last + p
            ok = (c >= 0) & (c < self.chunks)

            @pl.when(ok & (p < last))
            def _():
                self.red(d, c).wait_recv()
                self.ipart[d, c] = (self.ipart[d, c].astype(F32) + self.ri[d, c].astype(F32)).astype(BF)

            @pl.when(ok & (p > 0))
            def _():
                self.red(d, c).start()

            @pl.when(ok & (p == 0))
            def _():
                self.ig[d, c] = self.ipart[d, c]
                self.bc(d, c).start()

        for d in range(self.docs):
            p = self.pos[d]
            c = t - last - p
            ok = (c >= 0) & (c < self.chunks) & (p > 0)

            @pl.when(ok)
            def _():
                self.bc(d, c).wait_recv()

            @pl.when(ok & (p < last))
            def _():
                self.bc(d, c).start()

    def i_end(self):
        last = self.parts - 1
        for d in range(self.docs):
            p = self.pos[d]

            def sent(c, _, d=d):
                self.red(d, c).wait_send()
                return 0

            def back(c, _, d=d):
                self.bc(d, c).wait_send()
                return 0

            @pl.when(p > 0)
            def _():
                lax.fori_loop(0, self.chunks, sent, 0)

            @pl.when(p < last)
            def _():
                lax.fori_loop(0, self.chunks, back, 0)

    def tail(self):
        done = 3 + self.docs
        rest = [functools.partial(self.small_step, i) for i in range(done + 1, len(self.smalls) + 1)]
        rest += [functools.partial(self.taps_step, i) for i in range(3, len(self.tapsums) + 1)]

        def run(*fs):
            def go():
                for f in fs:
                    f()

            return go

        todo = {
            1: run(self.g_step2),
            2: run(self.q_step1),
            3: run(lambda: self.z_hop(1)),
            4: run(self.q_step2),
            5: run(lambda: self.z_hop(2)),
            6: run(self.q_step3, *rest),
            8: run(self.g_step3),
            10: run(self.g_step4),
            12: run(self.g_step5),
        }
        self.q_step0()

        def step(t, _):
            self.i_time(t)
            at(t, todo)
            return 0

        lax.fori_loop(1, self.chunks + 2 * (self.parts - 1), step, 0)
        self.qc.wait_recv()
        self.i_end()
        self.z_done()
        self.net.drain()


def attn_bwd(dp, lengths, x, wt, taps, qkv, gctx, lq, lk, sm, mix, k2, z, p, l1, l3, s1, small, gmix, out_rows):
    docs, seq, dim = x.shape
    width = wt.shape[0] // 3
    heads = width // HD
    parts = gctx.shape[0]
    nchunk = seq // CHUNK
    more = max(1, dp.bit_length() - 4)
    steps = dp.bit_length() + parts.bit_length()
    sds = jax.ShapeDtypeStruct
    vmem = pltpu.VMEM
    out = [
        sds((3 * width, dim), BF),
        sds((docs, nchunk, CHUNK, dim), BF),
        sds((heads, WIN), F32),
        sds((SLOTS, SLICE, dim), BF),
        sds((8, dim), F32),
        sds(out_rows.shape, BF),
    ]
    h = 3 * width // 2
    sq = (docs, width, width)
    return pl.pallas_call(
        functools.partial(attn_bwd_kernel, docs, heads, seq, parts, dp),
        out_shape=out,
        in_specs=[SM, ANY, VM, VM, VM, VM, VM, VM, VM, VM, VM, ANY, ANY, VM, VM, VM, VM, ANY, ANY],
        out_specs=[VM] * 5 + [ANY],
        input_output_aliases={18: 5},
        scratch_shapes=[
            vmem(x.shape, BF),
            vmem(z.shape, F32),
            vmem(p.shape, F32),
            vmem(gmix.shape, F32),
            vmem((docs, 3 * width, seq), BF),
            vmem((docs, width, seq), BF),
            vmem((docs, width, seq), BF),
            vmem(sq, F32),
            vmem(sq, F32),
            vmem(sq, F32),
            vmem(sq, F32),
            vmem(sq, F32),
            vmem((heads, WIN), F32),
            vmem((heads, BLK, WIN), F32),
            vmem((docs, nchunk, CHUNK, dim), BF),
            vmem((docs, nchunk, CHUNK, dim), BF),
            vmem((parts, 2, GCUT, dim), BF),
            vmem((parts, 2, SLICE - GCUT, dim), BF),
            vmem((2, parts - 1, SLICE, dim), BF),
            vmem((SLICE, dim), BF),
            vmem((more, SLICE, dim), BF),
            vmem((h, dim), BF),
            vmem((h, dim), BF),
            vmem((1 + more, h, dim), BF),
            vmem((3 * width, dim), BF),
            vmem((h, dim), BF),
            vmem((steps, 8, dim), F32),
            vmem((steps, heads, WIN), F32),
            DMA((4,)),
            DMA((64,)),
            DMA((64,)),
            DMA((4, docs, nchunk)),
            DMA((2, 2, parts - 1, docs)),
            vmem((parts, SLICE, dim), BF),
            vmem((SLICE, dim), F32),
            DMA((2, 2, parts - 1)),
        ],
        compiler_params=pltpu.CompilerParams(vmem_limit_bytes=62 * 2**20, collective_id=2, has_side_effects=True),
        cost_estimate=pl.CostEstimate(flops=int(1.2e10), bytes_accessed=int(3e7), transcendentals=0),
        name="attn_bwd",
    )(lengths, x, wt, taps, qkv, gctx, lq, lk, sm, mix, k2, z, p, l1, l3, s1, small, gmix, out_rows)


def finish_kernel(gw_ref, gq_ref, ig_ref, out_ref, small_ref, taps_ref, ow_o, up_o, dn_o, q_o, ig_o, out_o, g1_o, b1_o, g2_o, b2_o, taps_o):
    each = gw_ref.shape[0]
    for i, o in enumerate((ow_o, up_o, dn_o)):
        lo, size = PARTS[i]
        for j in range(each):
            o[j * size : (j + 1) * size] = gw_ref[j, lo : lo + size].astype(F32)
    q_o[...] = gq_ref[...].astype(F32)
    ig_o[...] = ig_ref[...].reshape(ig_o.shape)
    out_o[...] = out_ref[...]

    @pl.when(pl.program_id(0) == 0)
    def _():
        for i, o in enumerate((g1_o, b1_o, g2_o, b2_o)):
            o[...] = small_ref[i]
        taps_o[...] = taps_ref[:, TAP_END : TAP_END + KSIZE]


def finish_up(gw, gq, ig, out_rows, small, taps):
    docs, nchunk, chunk, dim = ig.shape
    groups, rows = out_rows.shape[1:3]
    seq = nchunk * chunk
    heads = taps.shape[0]
    steps = 4
    each = SLOTS // steps
    qrows = gq.shape[0] // steps
    per = seq // steps
    ratio = rows // per
    sds = jax.ShapeDtypeStruct
    whole = lambda shape: pl.BlockSpec(shape, lambda i: (0,) * len(shape))
    return pl.pallas_call(
        finish_kernel,
        grid=(steps,),
        out_shape=[sds((SLOTS * t, dim), F32) for t in (OW_ROWS, UP_ROWS, DN_ROWS)]
        + [sds(gq.shape, F32), sds((docs, seq, dim), BF), sds((docs, seq, dim), BF)]
        + [sds((dim,), F32)] * 4
        + [sds((heads, KSIZE), F32)],
        in_specs=[
            pl.BlockSpec((each, SLICE, dim), lambda i: (i, 0, 0)),
            pl.BlockSpec((qrows, dim), lambda i: (i, 0)),
            pl.BlockSpec((docs, nchunk // steps, chunk, dim), lambda i: (0, i, 0, 0)),
            pl.BlockSpec((docs, pl.Squeezed(), per, dim), lambda i: (0, i // ratio, i % ratio, 0)),
            whole(small.shape),
            whole(taps.shape),
        ],
        out_specs=[pl.BlockSpec((t, dim), lambda i: (i, 0)) for t in (each * OW_ROWS, each * UP_ROWS, each * DN_ROWS, qrows)]
        + [pl.BlockSpec((docs, per, dim), lambda i: (0, i, 0))] * 2
        + [whole((dim,))] * 4
        + [whole((heads, KSIZE))],
        compiler_params=pltpu.CompilerParams(vmem_limit_bytes=62 * 2**20),
        name="finish",
    )(gw, gq, ig, out_rows, small, taps)


def body_of(dp, mp):
    def body(tokens, lengths, qkv_weight, out_weight, conv_taps, norm1_gain, norm1_bias, norm2_gain, norm2_bias, up_weight, down_weight, cotangent):
        dim = tokens.shape[2]
        width = qkv_weight.shape[2]
        wt = jnp.transpose(qkv_weight, (0, 2, 1)).reshape(3 * width, dim)
        ow, up, dn = (t.reshape(SLOTS, -1, dim) for t in (out_weight, up_weight, down_weight))
        qkv, ctx, lq, lk, sm, mix, k2, z, p, l1, l3, wall = attn_fwd(lengths, tokens, wt, conv_taps, ow, up, dn, mp)
        out_rows, gmix, gctx, s1, small = ffn(lengths, tokens, cotangent, ctx, ow, up, dn, wall, norm1_gain, norm1_bias, norm2_gain, norm2_bias)
        gq, ig, gtaps, gw, small, out_rows = attn_bwd(
            dp, lengths, tokens, wt, conv_taps[:, ::-1], qkv, gctx, lq, lk, sm, mix, k2, z, p, l1, l3, s1, small, gmix, out_rows
        )
        g_ow, g_up, g_dn, gq, input_grad, output, g1, b1, g2, b2, g_taps = finish_up(gw, gq, ig, out_rows, small, gtaps)
        gqkv = jnp.transpose(gq.reshape(3, width, dim), (0, 2, 1))
        return output, input_grad, gqkv, g_ow, g_taps, g1, b1, g2, b2, g_up, g_dn

    return body


def solution(mesh):
    rep, rows = P(), P("mp", None)
    docs, cols, qkv = P("dp", None, None), P(None, "mp"), P(None, None, "mp")
    return jax.shard_map(
        body_of(mesh.shape["dp"], mesh.shape["mp"]),
        mesh=mesh,
        in_specs=(docs, P("dp"), qkv, rows, rows, rep, rep, rep, rep, cols, rows, docs),
        out_specs=(docs, docs, qkv, rows, rows, rep, rep, rep, rep, cols, rows),
        check_vma=False,
    )
```

```python
import functools

import jax
import jax.numpy as jnp
from jax import lax
from jax.experimental import pallas as pl
from jax.experimental.pallas import tpu as pltpu
from jax.sharding import PartitionSpec as P

HD = 64
LM = 64
KSIZE = 33
NS_ITERS = 6
EPS = 1e-5
HI = lax.Precision.HIGHEST
BF = jnp.bfloat16
F32 = jnp.float32
SCALE = HD**-0.5
WIN = 512
BLK = 256
CHUNK = 128
TAP0 = 112
TAP_END = TAP0 + BLK - 1
ROOT_HALF = 0.7071067811865476
INV_ROOT_2PI = 0.3989422804014327
MESH = pl.DeviceIdType.MESH
SLOTS = 8
OW_ROWS, UP_ROWS, DN_ROWS = 24, 96, 96
SLICE = OW_ROWS + UP_ROWS + DN_ROWS
CUT = OW_ROWS + UP_ROWS
GCUT = 112
PARTS = ((0, OW_ROWS), (OW_ROWS, UP_ROWS), (CUT, DN_ROWS))
VM = pl.BlockSpec(memory_space=pltpu.VMEM)
SM = pl.BlockSpec(memory_space=pltpu.SMEM)
ANY = pl.BlockSpec(memory_space=pl.ANY)
DMA = pltpu.SemaphoreType.DMA


def nn(a, b, precision=None):
    return lax.dot_general(a, b, (((1,), (0,)), ((), ())), precision=precision, preferred_element_type=F32)


def nt(a, b, precision=None):
    return lax.dot_general(a, b, (((1,), (1,)), ((), ())), precision=precision, preferred_element_type=F32)


def tn(a, b, precision=None):
    return lax.dot_general(a, b, (((0,), (0,)), ((), ())), precision=precision, preferred_element_type=F32)


def block_mask(width):
    r = lax.broadcasted_iota(jnp.int32, (width, width), 0) // HD
    c = lax.broadcasted_iota(jnp.int32, (width, width), 1) // HD
    return r == c


def identity(width):
    r = lax.broadcasted_iota(jnp.int32, (width, width), 0)
    c = lax.broadcasted_iota(jnp.int32, (width, width), 1)
    return jnp.where(r == c, 1.0, 0.0).astype(F32)


def spread(x, heads, mask):
    return jnp.where(mask, jnp.concatenate([x] * heads, axis=0), 0.0)


def per_head_total(col, heads):
    tot = jnp.sum(col.reshape(heads, HD, 1), axis=1, keepdims=True)
    return jnp.broadcast_to(tot, (heads, HD, 1)).reshape(heads * HD, 1)


def members(length, count):
    s = lax.broadcasted_iota(jnp.int32, (LM, count), 1)
    j = lax.broadcasted_iota(jnp.int32, (LM, count), 0)
    s64 = s * LM
    return (j * length <= s64) & (s64 < (j + 1) * length) & (s < length)


def live_lanes(length, count):
    return lax.broadcasted_iota(jnp.int32, (1, count), 1) < length


def toeplitz(row):
    return pltpu.roll(jnp.broadcast_to(row, (BLK, WIN)), 0, 1, stride=1, stride_axis=0)


def windows(x, seq):
    pad = jnp.zeros((x.shape[0], 128), x.dtype)
    padded = jnp.concatenate([pad, x, pad], axis=1)
    return jnp.concatenate([padded[:, b * BLK : b * BLK + WIN] for b in range(seq // BLK)], axis=0)


def hi_lo(x):
    hi = x.astype(BF)
    return hi, (x - hi.astype(F32)).astype(BF)


def banded(x, row, heads, seq):
    outs = []
    for h in range(heads):
        wins = windows(x[h * HD : (h + 1) * HD], seq)
        hi, lo = hi_lo(toeplitz(row[h : h + 1]))
        y = nt(wins, hi) + nt(wins, lo)
        outs.append(jnp.concatenate([y[b * HD : (b + 1) * HD] for b in range(seq // BLK)], axis=1))
    return jnp.concatenate(outs, axis=0)


def flip(i, bit):
    return i + bit * (1 - 2 * ((i // bit) % 2))


def partner(i, m):
    for bit in (1, 2, 4):
        if m & bit:
            i = flip(i, bit)
    return i


def greet(peers):
    bar = pltpu.get_barrier_semaphore()
    for p in peers:
        pl.semaphore_signal(bar, inc=1, device_id=p, device_id_type=MESH)
    pl.semaphore_wait(bar, len(peers))


def rcopy(src, dst, ss, rs, dev):
    return pltpu.make_async_remote_copy(src_ref=src, dst_ref=dst, send_sem=ss, recv_sem=rs, device_id=dev, device_id_type=MESH)


class Net:
    def __init__(self, ssem, rsem):
        self.ssem, self.rsem, self.n = ssem, rsem, 0
        self.sent = []

    def copy(self, src, dst, dev, late=True):
        i = self.n
        self.n += 1
        c = rcopy(src, dst, self.ssem.at[i], self.rsem.at[i], dev)
        if late:
            self.sent.append(c)
        return c

    def drain(self):
        for c in self.sent:
            c.wait_send()
        self.sent = []


def at(i, steps):
    for k, f in steps.items():

        @pl.when(i == k)
        def _():
            f()


class Local:
    def __init__(self, sem):
        self.sem, self.n, self.open = sem, 0, []

    def start(self, src, dst):
        c = pltpu.make_async_copy(src, dst, self.sem.at[self.n])
        self.n += 1
        c.start()
        self.open.append(c)
        return c

    def finish(self):
        for c in self.open:
            c.wait()
        self.open = []


class Line:
    def __init__(self, parts):
        self.last, self.z = parts - 1, lax.axis_index("mp")

    def sends(self, way, s):
        z = self.z
        return (z < self.last) & (z >= s) if way == 0 else (z > 0) & (z + s <= self.last)

    def gets(self, way, s):
        z = self.z
        return z - 1 >= s if way == 0 else z + 1 + s <= self.last

    def sent_from(self, way, s):
        return self.z - (1 - 2 * way) * s

    def got_from(self, way, s):
        return self.z - (1 - 2 * way) * (s + 1)

    def ahead(self, way):
        size = self.last + 1
        return {"mp": lax.rem(self.z + (1 - 2 * way) + size, size)}


class Gather:
    def __init__(self, mp, srcs, wall, zsem, psem):
        self.line = Line(mp)
        self.srcs, self.wall, self.zsem, self.psem = srcs, wall, zsem, psem
        self.d = lax.axis_index("dp")
        r = lax.rem(self.d, SLOTS)
        self.rs = (r, flip(r, 4), flip(r, 2), partner(r, 6))
        self.steps = mp - 1

    def z(self, way, s, origin):
        dev = self.line.ahead(way)
        r = self.rs[0]
        out = []
        for i, (lo, size) in enumerate(PARTS):
            dst = self.wall.at[origin, r, pl.ds(lo, size)]
            src = self.srcs[i].at[r] if s == 0 else dst
            out.append(rcopy(src, dst, self.zsem.at[0, way, s, i], self.zsem.at[1, way, s, i], dev))
        return out

    def plane(self, way, s, k):
        w = self.wall.at[self.line.got_from(way, s)]
        q, rows, bit = (
            (0, (0, SLICE), 4),
            (0, (0, SLICE), 2),
            (1, (0, CUT), 2),
            (2, (CUT, DN_ROWS), 4),
            (0, (0, SLICE), 1),
            (1, (0, SLICE), 1),
            (2, (0, SLICE), 1),
            (3, (0, SLICE), 1),
        )[k]
        ref = w.at[self.rs[q], pl.ds(*rows)]
        return rcopy(ref, ref, self.psem.at[0, way, s, k], self.psem.at[1, way, s, k], {"dp": flip(self.d, bit)})

    def send(self, s):
        for way in range(2):

            @pl.when(self.line.sends(way, s))
            def _():
                for c in self.z(way, s, self.line.sent_from(way, s)):
                    c.start()

    def got(self, s, f):
        for way in range(2):
            pl.when(self.line.gets(way, s))(functools.partial(f, way, s))

    def step1(self, s):
        def arrive(way, s):
            for c in self.z(way, s, self.line.got_from(way, s)):
                c.wait_recv()

        self.got(s, arrive)
        if s + 1 < self.steps:
            self.send(s + 1)

        def pass_on(way, s):
            for k in (0, 1, 4):
                self.plane(way, s, k).start()

        self.got(s, pass_on)

    def step2(self, s):
        def f(way, s):
            self.plane(way, s, 0).wait_recv()
            self.plane(way, s, 2).start()
            self.plane(way, s, 5).start()
            self.plane(way, s, 1).wait_recv()
            self.plane(way, s, 3).start()
            self.plane(way, s, 6).start()

        self.got(s, f)

    def step3(self, s):
        def f(way, s):
            self.plane(way, s, 2).wait_recv()
            self.plane(way, s, 3).wait_recv()
            self.plane(way, s, 7).start()

        self.got(s, f)

    def finish(self):
        def f(way, s):
            for k in range(8):
                if k >= 4:
                    self.plane(way, s, k).wait_recv()
                self.plane(way, s, k).wait_send()

        for s in range(self.steps):
            self.got(s, f)
            for way in range(2):

                @pl.when(self.line.sends(way, s))
                def _():
                    for c in self.z(way, s, self.line.sent_from(way, s)):
                        c.wait_send()


def attn_fwd_kernel(docs, heads, seq, dest, len_ref, x_hbm, wt_ref, taps_ref, ow_ref, up_ref, dn_ref,
                    qkv_hbm, ctx_ref, lq_hbm, lk_hbm, sum_hbm, mix_hbm, k2_hbm, z_hbm, p_hbm, l1_ref, l3_ref, wall_ref,
                    x_s, qkv_s, lq_s, lk_s, sum_s, mix_s, k2_s, z_s, p_s, ctx_s, taps_s, lsem, asem, zsem, psem):
    width = heads * HD
    me, dd = lax.axis_index("mp"), lax.axis_index("dp")
    local = Local(lsem)
    loads = [local.start(x_hbm.at[d], x_s.at[d]) for d in range(docs)]
    local.open = []
    greet([{"mp": partner(me, m)} for m in range(1, dest)] + [{"dp": flip(dd, b)} for b in (1, 2, 4)])
    gather = Gather(dest, (ow_ref, up_ref, dn_ref), wall_ref, zsem, psem)
    gather.send(0)

    def a_copy(m, d):
        return rcopy(ctx_s.at[partner(me, m), d], ctx_ref.at[me, d], asem.at[0, m - 1, d], asem.at[1, m - 1, d], {"mp": partner(me, m)})

    taps_s[...] = jnp.zeros_like(taps_s)
    taps_s[:, TAP0 : TAP0 + KSIZE] = taps_ref[...]
    mask = block_mask(width)
    eye = identity(width)
    for c in loads:
        c.wait()

    def project(i, _):
        d, c = i // (seq // BLK), lax.rem(i, seq // BLK)
        rows = pl.ds(pl.multiple_of(c * BLK, BLK), BLK)
        qkv_s[d, :, rows] = nt(wt_ref[...], x_s[d, rows, :]).astype(BF)
        return 0

    lax.fori_loop(0, docs * (seq // BLK), project, 0)
    local.start(qkv_s, qkv_hbm)

    def landmarks(d, _):
        length = len_ref[d]
        memb = jnp.where(members(length, seq), 1.0, 0.0).astype(F32)
        counts = jnp.maximum(jnp.sum(memb, axis=1, keepdims=True), 1.0)
        memb_b = memb.astype(BF)
        q = qkv_s[d, 0:width, :]
        k = qkv_s[d, width : 2 * width, :]
        v = qkv_s[d, 2 * width : 3 * width, :]
        lq = spread(nt(memb_b, q) / counts, heads, mask).astype(BF)
        lk = spread(nt(memb_b, k) / counts, heads, mask).astype(BF)
        lq_s[d] = lq
        lk_s[d] = lk
        s2 = jnp.where(mask, nt(lq, lk) * SCALE, -1e30)
        e2 = jnp.where(mask, jnp.exp(s2 - jnp.max(s2, axis=1, keepdims=True)), 0.0)
        k2_s[d] = e2 / jnp.sum(e2, axis=1, keepdims=True)
        s3 = jnp.where(live_lanes(length, seq), nn(lq, k) * SCALE, -1e30)
        m3 = jnp.max(s3, axis=1, keepdims=True)
        e3 = jnp.exp(s3 - m3)
        t3 = jnp.sum(e3, axis=1, keepdims=True)
        l3_ref[d] = jnp.broadcast_to(m3 + jnp.log(t3), (width, 128))
        k3 = (e3 / t3).astype(BF)
        sum_s[d] = jnp.where(mask, nt(k3, v), 0.0)
        at(d, {0: lambda: (gather.step1(0),), 1: lambda: (gather.step1(1),)})
        return 0

    lax.fori_loop(0, docs, landmarks, 0)
    for src, dst in ((lq_s, lq_hbm), (lk_s, lk_hbm), (k2_s, k2_hbm), (sum_s, sum_hbm)):
        local.start(src, dst)
    for d in range(docs):
        k2 = k2_s[d]
        z_s[d, 0] = k2.T / per_head_total(jnp.sum(k2 * k2, axis=1, keepdims=True), heads)

    def newton(i, _):
        k2s = [k2_s[d] for d in range(docs)]
        zs = [z_s[d, i] for d in range(docs)]
        ps = [nn(k2s[d], zs[d], HI) for d in range(docs)]
        bs = [15.0 * eye - nn(ps[d], 7.0 * eye - ps[d], HI) for d in range(docs)]
        cs = [13.0 * eye - nn(ps[d], bs[d], HI) for d in range(docs)]
        zs = [0.25 * nn(zs[d], cs[d], HI) for d in range(docs)]
        for d in range(docs):
            p_s[d, i, 0] = ps[d]
            p_s[d, i, 1] = bs[d]
            p_s[d, i, 2] = cs[d]
            z_s[d, i + 1] = zs[d]
        at(i, {3: lambda: (gather.step1(2), gather.step2(0),)})
        return 0

    lax.fori_loop(0, NS_ITERS, newton, 0)
    local.start(z_s, z_hbm)
    local.start(p_s, p_hbm)
    part = seq // dest

    def contexts(d, _):
        length = len_ref[d]
        q = qkv_s[d, 0:width, :]
        v = qkv_s[d, 2 * width : 3 * width, :]
        live = live_lanes(length, seq)
        mix = jnp.where(mask, nn(z_s[d, NS_ITERS], sum_s[d], HI), 0.0)
        mix_s[d] = mix.astype(BF)
        s1 = (nn(lk_s[d], q) * SCALE).reshape(heads, LM, seq)
        m1 = jnp.max(s1, axis=1, keepdims=True)
        e1 = jnp.exp(s1 - m1)
        t1 = jnp.sum(e1, axis=1, keepdims=True)
        l1_ref[d] = (m1 + jnp.log(t1)).reshape(heads, seq)
        k1 = (e1 / t1).reshape(width, seq).astype(BF)
        vl = jnp.where(live, v, 0).astype(BF)
        ctx = nn(mix.T.astype(BF), k1) + banded(vl, taps_s[...], heads, seq)
        ctx = jnp.where(live, ctx, 0.0).astype(BF)
        for i in range(dest):
            ctx_s[i, d] = ctx[:, i * part : (i + 1) * part]
        for m in range(1, dest):
            a_copy(m, d).start()
        ctx_ref[me, d] = ctx_s[me, d]
        at(d, {0: lambda: (gather.step3(0), gather.step2(1), gather.step2(2),)})
        return 0

    lax.fori_loop(0, docs, contexts, 0)
    local.start(mix_s, mix_hbm)
    gather.step3(1)
    gather.step3(2)
    gather.finish()
    for d in range(docs):
        for m in range(1, dest):
            a_copy(m, d).wait()
    local.finish()


def attn_fwd(lengths, x, wt, taps, ow, up, dn, dest):
    docs, seq, dim = x.shape
    width = wt.shape[0] // 3
    heads = width // HD
    sds = jax.ShapeDtypeStruct
    kept = [
        sds((docs, 3 * width, seq), BF),
        sds((docs, width, width), BF),
        sds((docs, width, width), BF),
        sds((docs, width, width), F32),
        sds((docs, width, width), BF),
        sds((docs, width, width), F32),
        sds((docs, NS_ITERS + 1, width, width), F32),
        sds((docs, NS_ITERS, 3, width, width), F32),
    ]
    out = [kept[0], sds((dest, docs, width, seq // dest), BF)] + kept[1:] + [
        sds((docs, heads, seq), F32),
        sds((docs, width, 128), F32),
        sds((dest, SLOTS, SLICE, dim), BF),
    ]
    return pl.pallas_call(
        functools.partial(attn_fwd_kernel, docs, heads, seq, dest),
        out_shape=out,
        in_specs=[SM, ANY, VM, VM, ANY, ANY, ANY],
        out_specs=[ANY, VM] + [ANY] * 7 + [VM, VM, ANY],
        scratch_shapes=[pltpu.VMEM((docs, seq, dim), BF)]
        + [pltpu.VMEM(t.shape, t.dtype) for t in kept]
        + [
            pltpu.VMEM((dest, docs, width, seq // dest), BF),
            pltpu.VMEM((heads, WIN), F32),
            DMA((16,)),
            DMA((2, dest - 1, docs)),
            DMA((2, 2, dest - 1, 3)),
            DMA((2, 2, dest - 1, 8)),
        ],
        compiler_params=pltpu.CompilerParams(vmem_limit_bytes=60 * 2**20, collective_id=0, has_side_effects=True),
        cost_estimate=pl.CostEstimate(flops=int(8e9), bytes_accessed=int(3e7), transcendentals=0),
        name="attn_fwd",
    )(lengths, x, wt, taps, ow, up, dn)


def ln_stats(v):
    mu = jnp.mean(v, axis=-1, keepdims=True)
    cen = v - mu
    var = jnp.mean(cen * cen, axis=-1, keepdims=True)
    r = lax.rsqrt(var + EPS)
    return cen * r, r


def ln_back(g, xhat, r):
    m1 = jnp.mean(g, axis=-1, keepdims=True)
    m2 = jnp.mean(g * xhat, axis=-1, keepdims=True)
    return r * (g - m1 - xhat * m2)


class Spread:
    def __init__(self, parts, buf, sem):
        self.line, self.buf, self.sem = Line(parts), buf, sem

    def one(self, way, s, d, origin, src=None):
        dst = self.buf.at[d, origin]
        return rcopy(dst if src is None else src, dst, self.sem.at[way, 0, s, d], self.sem.at[way, 1, s, d], self.line.ahead(way))

    def start(self, s, d, src=None):
        for way in range(2):

            @pl.when(self.line.sends(way, s))
            def _():
                self.one(way, s, d, self.line.sent_from(way, s), src).start()

    def wait(self, s, d):
        for way in range(2):

            @pl.when(self.line.gets(way, s))
            def _():
                self.one(way, s, d, self.line.got_from(way, s)).wait_recv()

    def sent(self, s, d, src=None):
        for way in range(2):

            @pl.when(self.line.sends(way, s))
            def _():
                self.one(way, s, d, self.line.sent_from(way, s), src).wait_send()


def ffn_kernel(groups, docs, rows, len_ref, x_hbm, cot_hbm, ctx_ref, ow_hbm, up_hbm, dn_hbm, wall_hbm, g1_ref, b1_ref, g2_ref, b2_ref,
               out_hbm, gmix_ref, gctx_ref, s1_hbm, small_ref,
               x_s, cot_s, w_s, rc_s, gc_s, nb_s, fac_s, act_s, gp_s, br_s, x1_s, gn_s, ga_s, o_s, s1_s, lsem, csem, osem, asem):
    n = docs * rows
    dim = x_s.shape[-1]
    z, dd = lax.axis_index("mp"), lax.axis_index("dp")
    kk = lax.rem(dd, 2)
    local = Local(lsem)
    mine = pl.ds(pl.multiple_of(z * rows, rows), rows)
    others = [partner(z, m) for m in range(1, groups)]
    heads_first = [local.start(ow_hbm, w_s.at[z, :, :, pl.ds(*PARTS[0])])]
    heads_first += [local.start(wall_hbm.at[g, :, :, pl.ds(*PARTS[0])], w_s.at[g, :, :, pl.ds(*PARTS[0])]) for g in others]
    heads_first += [local.start(x_hbm.at[d, mine], x_s.at[pl.ds(d * rows, rows)]) for d in range(docs)]
    rest = [local.start(up_hbm, w_s.at[z, :, :, pl.ds(*PARTS[1])]), local.start(dn_hbm, w_s.at[z, :, :, pl.ds(*PARTS[2])])]
    body = pl.ds(OW_ROWS, SLICE - OW_ROWS)
    rest += [local.start(wall_hbm.at[g, :, :, body], w_s.at[g, :, :, body]) for g in others]
    rest += [local.start(cot_hbm.at[d, mine], cot_s.at[pl.ds(d * rows, rows)]) for d in range(docs)]
    local.open = []
    greet([{"mp": partner(z, m)} for m in range(1, groups)] + [{"dp": flip(dd, 1)}])

    def back_copy(m, d):
        return rcopy(gc_s.at[m - 1, d], gctx_ref.at[z, d], asem.at[0, m - 1, d], asem.at[1, m - 1, d], {"mp": partner(z, m)})

    spread_out = Spread(groups, out_hbm, osem)

    def core_copy(g, part):
        lo, size = ((OW_ROWS, SLICE - OW_ROWS), (0, OW_ROWS))[part]
        return rcopy(w_s.at[g, :, 1 - kk, pl.ds(lo, size)], rc_s.at[g, :, pl.ds(lo, size)], csem.at[0, g, part], csem.at[1, g, part], {"dp": flip(dd, 1)})

    def take(g, part):
        lo, size = PARTS[part]
        return w_s[g, :, :, lo : lo + size, :].reshape(SLOTS * size, dim)

    def put(g, part, val):
        lo, size = PARTS[part]
        w_s[g, :, :, lo : lo + size, :] = val.astype(BF).reshape(SLOTS // 2, 2, size, dim)

    first = z * rows
    gain1, bias1 = g1_ref[...].reshape(1, dim), b1_ref[...].reshape(1, dim)
    gain2, bias2 = g2_ref[...].reshape(1, dim), b2_ref[...].reshape(1, dim)
    for c in heads_first:
        c.wait()
    small_ref[...] = jnp.zeros_like(small_ref)

    def doc(d, _):
        here = pl.ds(pl.multiple_of(d * rows, rows), rows)
        live = (lax.broadcasted_iota(jnp.int32, (rows, 1), 0) + first < len_ref[d]).astype(F32)
        mixed = x_s[here].astype(F32)
        for g in range(groups):
            mixed = mixed + tn(ctx_ref[g, d], take(g, 0)).astype(BF).astype(F32)
        xh1, r1 = ln_stats(mixed)
        x1_s[...] = xh1
        normed = xh1 * gain1 + bias1
        nb_s[here] = normed.astype(BF)
        br_s[...] = normed

        @pl.when(d == 0)
        def _():
            for c in rest:
                c.wait()

        def fwd_group(g, _):
            h = nn(nb_s[here], take(g, 1))
            phi_big = 0.5 * (1.0 + lax.erf(h * ROOT_HALF))
            act = (h * phi_big).astype(BF)
            act_s[g, here] = act
            fac_s[g] = phi_big + h * (jnp.exp(-0.5 * h * h) * INV_ROOT_2PI)
            br_s[...] += nn(act, take(g, 2)).astype(BF).astype(F32)
            return 0

        lax.fori_loop(0, groups, fwd_group, 0, unroll=True)
        xh2, r2 = ln_stats(br_s[...])
        o_s[d] = (live * (xh2 * gain2 + bias2)).astype(BF)

        @pl.when(d == 0)
        def _():
            spread_out.start(0, 0, o_s.at[0])

        g_out = live * cot_s[here].astype(F32)
        gg2 = jnp.sum(g_out * xh2, axis=0, keepdims=True)
        gb2 = jnp.sum(g_out, axis=0, keepdims=True)
        g_res = ln_back(g_out * gain2, xh2, r2)
        gn_s[...] = g_res
        gbr_s[here] = g_res.astype(BF)

        def back_group(g, _):
            g_pre = (nt(gbr_s[here], take(g, 2)) * fac_s[g]).astype(BF)
            gp_s[g, here] = g_pre
            gn_s[...] += nt(g_pre, take(g, 1))
            return 0

        lax.fori_loop(0, groups, back_group, 0)
        g_n = gn_s[...]
        xh1 = x1_s[...]
        gg1 = jnp.sum(g_n * xh1, axis=0, keepdims=True)
        gb1 = jnp.sum(g_n, axis=0, keepdims=True)
        small_ref[...] += jnp.concatenate([gg1, gb1, gg2, gb2, jnp.zeros((4, dim), F32)], axis=0)
        g_mix = ln_back(g_n * gain1, xh1, r1)
        gmix_ref[d] = g_mix
        g_att = g_mix.astype(BF)
        ga_s[here] = g_att
        for m in reversed(range(groups)):
            t = nt(take(partner(z, m), 0), g_att).astype(BF)
            if m:
                gc_s[m - 1, d] = t
                back_copy(m, d).start()
            else:
                gctx_ref[z, d] = t
        return 0

    gbr_s = cot_s
    lax.fori_loop(0, docs, doc, 0)
    for d in range(docs):
        local.start(o_s.at[d], out_hbm.at[d, z])

    def weight_group(g, _):
        put(g, 2, tn(act_s[g], gbr_s[...]))
        put(g, 1, tn(nb_s[...], gp_s[g]))
        core_copy(g, 0).start()
        return 0

    lax.fori_loop(0, groups, weight_group, 0)
    for g in range(groups):
        acc = None
        for d in range(docs):
            t = nn(ctx_ref[g, d], ga_s[d * rows : (d + 1) * rows])
            acc = t if acc is None else acc + t
        put(g, 0, acc)
        core_copy(g, 1).start()

    def add_group(g, _):
        core_copy(g, 0).wait_recv()
        core_copy(g, 1).wait_recv()

        def add_slot(j, _):
            s1_s[g, j // 2, j % 2] = (w_s[g, j, kk].astype(F32) + rc_s[g, j].astype(F32)).astype(BF)
            return 0

        lax.fori_loop(0, SLOTS // 2, add_slot, 0)
        return 0

    lax.fori_loop(0, groups, add_group, 0)
    local.start(s1_s, s1_hbm)
    for m in range(1, groups):
        for d in range(docs):
            back_copy(m, d).wait()
    spread_out.wait(0, 0)
    spread_out.sent(0, 0, o_s.at[0])
    for g in range(groups):
        for part in range(2):
            core_copy(g, part).wait_send()
    local.finish()


def ffn(lengths, x, cot, ctx, ow, up, dn, wall, g1, b1, g2, b2):
    docs, seq, dim = x.shape
    groups, _, width, rows = ctx.shape
    ff = SLOTS * UP_ROWS
    n = docs * rows
    sds = jax.ShapeDtypeStruct
    out = [
        sds((docs, groups, rows, dim), BF),
        sds((docs, rows, dim), F32),
        sds((groups, docs, width, rows), BF),
        sds((groups, 2, 2, SLICE, dim), BF),
        sds((8, dim), F32),
    ]
    wall = wall.reshape(groups, SLOTS // 2, 2, SLICE, dim)
    ow, up, dn = (t.reshape(SLOTS // 2, 2, -1, dim) for t in (ow, up, dn))
    return pl.pallas_call(
        functools.partial(ffn_kernel, groups, docs, rows),
        out_shape=out,
        in_specs=[SM, ANY, ANY, VM, ANY, ANY, ANY, ANY, VM, VM, VM, VM],
        out_specs=[ANY, VM, VM, ANY, VM],
        scratch_shapes=[
            pltpu.VMEM((n, dim), BF),
            pltpu.VMEM((n, dim), BF),
            pltpu.VMEM((groups, SLOTS // 2, 2, SLICE, dim), BF),
            pltpu.VMEM((groups, SLOTS // 2, SLICE, dim), BF),
            pltpu.VMEM((groups - 1, docs, width, rows), BF),
            pltpu.VMEM((n, dim), BF),
            pltpu.VMEM((groups, rows, ff), F32),
            pltpu.VMEM((groups, n, ff), BF),
            pltpu.VMEM((groups, n, ff), BF),
            pltpu.VMEM((rows, dim), F32),
            pltpu.VMEM((rows, dim), F32),
            pltpu.VMEM((rows, dim), F32),
            pltpu.VMEM((n, dim), BF),
            pltpu.VMEM((docs, rows, dim), BF),
            pltpu.VMEM((groups, 2, 2, SLICE, dim), BF),
            DMA((24,)),
            DMA((2, groups, 2)),
            DMA((2, 2, groups - 1, docs)),
            DMA((2, groups - 1, docs)),
        ],
        compiler_params=pltpu.CompilerParams(vmem_limit_bytes=62 * 2**20, collective_id=1, has_side_effects=True),
        cost_estimate=pl.CostEstimate(flops=int(1.8e10), bytes_accessed=int(4e7), transcendentals=0),
        name="ffn",
    )(lengths, x, cot, ctx, ow, up, dn, wall, g1, b1, g2, b2)


def attn_bwd_kernel(docs, heads, seq, parts, dp, len_ref, x_hbm, wt_ref, taps_ref, qkv_ref, gctx_ref, lq_ref, lk_ref, sum_ref, mix_ref, k2_ref,
                    z_hbm, p_hbm, l1_ref, l3_ref, s1, small_in, gmix_hbm, out_in, gq, ig, taps_out, gw, small, out_hbm,
                    x_s, z_s, p_s, gmix_s, g_s, gs1_s, gs3_s, ginv_s, glq_s, glk_s, gz_s, gk_s, taps_s, gacc_s,
                    ipart, ri, ra1, rb1, rz, fin, rfin, rq0, rq1, rq2, gqb, q, rsm, rtp, lsem, ssem, rsem, isem, osem, pz, acc, gsem):
    width = heads * HD
    nblk = seq // BLK
    dim = x_s.shape[-1]
    zi = lax.axis_index("mp")
    local = Local(lsem)
    loads = [local.start(a, b) for a, b in ((z_hbm, z_s), (p_hbm, p_s), (x_hbm, x_s), (gmix_hbm, gmix_s))]
    local.open = []
    nd = Sums(docs, seq, parts, dp, locals())
    nd.begin()
    out = Spread(parts, out_hbm, osem)
    left = [(s, d) for s in range(parts - 1) for d in range(docs) if (s, d) != (0, 0)]
    waves = [[(0, d) for d in range(1, docs)] + [(1, 0)]]
    waves += [[(s, d) for d in range(1, docs)] + [(s + 1, 0)] for s in range(1, parts - 2)] + [[(parts - 2, d) for d in range(1, docs)]]

    def out_step(i):
        for s, d in waves[i] if i < len(waves) else ():
            if s > 0 and (s - 1, d) != (0, 0):
                out.wait(s - 1, d)
            out.start(s, d)

    out_step(0)
    taps_s[...] = jnp.zeros_like(taps_s)
    for i in range(KSIZE):
        taps_s[:, TAP0 + KSIZE - 1 - i : TAP0 + KSIZE - i] = taps_ref[:, i : i + 1]
    mask = block_mask(width)
    eye = identity(width)
    anti = jnp.where(
        lax.broadcasted_iota(jnp.int32, (BLK, BLK), 0) + lax.broadcasted_iota(jnp.int32, (BLK, BLK), 1) == BLK - 1, 1.0, 0.0
    ).astype(BF)
    gacc_s[...] = jnp.zeros_like(gacc_s)

    def doc(d, _):
        length = len_ref[d]
        live = live_lanes(length, seq)
        q_ = qkv_ref[d, 0:width, :]
        k = qkv_ref[d, width : 2 * width, :]
        v = qkv_ref[d, 2 * width : 3 * width, :]
        gc = jnp.concatenate([gctx_ref[i, d] for i in range(parts)], axis=1)
        gc = jnp.where(live, gc, 0).astype(BF)
        lq, lk = lq_ref[d], lk_ref[d]
        s1_ = (nn(lk, q_) * SCALE).reshape(heads, LM, seq)
        k1 = jnp.exp(s1_ - l1_ref[d].reshape(heads, 1, seq))
        gmixing = jnp.where(mask, nt(k1.reshape(width, seq).astype(BF), gc), 0.0)
        gk1 = nn(mix_ref[d], gc).reshape(heads, LM, seq)
        gs1 = (k1 * (gk1 - jnp.sum(gk1 * k1, axis=1, keepdims=True))).reshape(width, seq).astype(BF)
        gz_s[d] = nt(gmixing, sum_ref[d], HI)
        gk_s[d] = jnp.zeros((width, width), F32)
        gsum = jnp.where(mask, tn(ginv_s[d], gmixing, HI), 0.0)
        gsum_b = gsum.astype(BF)
        s3 = jnp.where(live, nn(lq, k) * SCALE, -1e30)
        k3 = jnp.exp(s3 - l3_ref[d][:, 0:1])
        gk3 = nn(gsum_b, v)
        gs3 = (k3 * (gk3 - jnp.sum(gk3 * k3, axis=1, keepdims=True))).astype(BF)
        at(d, {1: lambda: out_step(1)})
        glq_s[d] = jnp.where(mask, nt(gs3, k), 0.0) * SCALE
        glk_s[d] = jnp.where(mask, nt(gs1, q_), 0.0) * SCALE
        gs1_s[d] = gs1
        gs3_s[d] = gs3
        gv = nn(gsum.T.astype(BF), k3.astype(BF))
        gvl = banded(gc, taps_s[...], heads, seq)
        g_s[d, 2 * width : 3 * width, :] = (gv + jnp.where(live, gvl, 0.0)).astype(BF)
        vl = jnp.where(live, v, 0).astype(BF)
        for h in range(heads):
            wins = windows(vl[h * HD : (h + 1) * HD], seq)
            gch = gc[h * HD : (h + 1) * HD]
            stack = jnp.concatenate([gch[:, b * BLK : (b + 1) * BLK] for b in range(nblk)], axis=0)
            gacc_s[h] += nn(nt(anti, stack).astype(BF), wins)
        at(d, {i: functools.partial(nd.small_step, 1 + i) for i in range(docs)})
        return 0

    loads[0].wait()
    for d in range(docs):
        ginv_s[d] = z_s[d, NS_ITERS]
    lax.fori_loop(0, docs, doc, 0)
    for h in range(heads):
        rolled = pltpu.roll(gacc_s[h], 0, 1, stride=1, stride_axis=0)
        taps_out[h : h + 1, :] = jnp.sum(rolled, axis=0, keepdims=True)
    loads[1].wait()

    def newton_back(j, _):
        i = NS_ITERS - 1 - j
        for d in range(docs):
            z, p, b, c = z_s[d, i], p_s[d, i, 0], p_s[d, i, 1], p_s[d, i, 2]
            a = 7.0 * eye - p
            g = 0.25 * gz_s[d]
            gc_ = tn(z, g, HI)
            gp = -nt(gc_, b, HI)
            gb = -tn(p, gc_, HI)
            gp = gp - nt(gb, a, HI)
            ga = -tn(p, gb, HI)
            gp = gp - ga
            gk_s[d] += nt(gp, z, HI)
            gz_s[d] = nt(g, c, HI) + tn(k2_ref[d], gp, HI)
        base = 1 + docs
        at(j, {
            1: lambda: (nd.small_step(base), nd.taps_step(0)),
            3: lambda: (nd.small_step(base + 1), nd.taps_step(1), nd.g_step1()),
            5: lambda: (nd.small_step(base + 2), nd.taps_step(2), out_step(2)),
        })
        return 0

    lax.fori_loop(0, NS_ITERS, newton_back, 0)
    for c in loads[2:]:
        c.wait()

    def finish(d, _):
        length = len_ref[d]
        k2 = k2_ref[d]
        tot = per_head_total(jnp.sum(k2 * k2, axis=1, keepdims=True), heads)
        g = gz_s[d]
        dot = per_head_total(jnp.sum(g * k2.T, axis=1, keepdims=True), heads)
        gk2 = gk_s[d] + (g / tot).T - k2 * (2.0 * dot / (tot * tot))
        gs2 = k2 * (gk2 - jnp.sum(gk2 * k2, axis=1, keepdims=True)) * SCALE
        memb = jnp.where(members(length, seq), 1.0, 0.0).astype(F32)
        counts = jnp.maximum(jnp.sum(memb, axis=1, keepdims=True), 1.0)
        counts = jnp.concatenate([counts] * heads, axis=0)
        memb3 = jnp.concatenate([memb.astype(BF)] * heads, axis=0)
        lq, lk = lq_ref[d].astype(F32), lk_ref[d].astype(F32)
        glq = (glq_s[d] + nn(gs2, lk, HI)) / counts
        glk = (glk_s[d] + tn(gs2, lq, HI)) / counts
        hi, lo = hi_lo(glq.T)
        gq_ = nn(lk.T.astype(BF), gs1_s[d]) * SCALE + nn(hi, memb3) + nn(lo, memb3)
        hi, lo = hi_lo(glk.T)
        gk_ = nn(lq.T.astype(BF), gs3_s[d]) * SCALE + nn(hi, memb3) + nn(lo, memb3)
        g_s[d, 0:width, :] = gq_.astype(BF)
        g_s[d, width : 2 * width, :] = gk_.astype(BF)

        def inputs(c, _):
            rows = pl.ds(pl.multiple_of(c * BLK, BLK), BLK)
            t = tn(g_s[d, :, rows], wt_ref[...])
            t = (t + jnp.where(zi == c, 1.0, 0.0) * gmix_s[d]).astype(BF)
            per = BLK // CHUNK
            ipart[d, pl.ds(c * per, per)] = t.reshape(per, CHUNK, dim)
            return 0

        lax.fori_loop(0, nblk, inputs, 0)
        return 0

    lax.fori_loop(0, docs, finish, 0)
    for i in range(3, len(waves)):
        out_step(i)
    nd.i_time(0)

    def weights(c, _):
        rows = pl.ds(pl.multiple_of(c * width, width), width)
        acc_q = nn(g_s[0, rows], x_s[0])
        for d in range(1, docs):
            acc_q = acc_q + nn(g_s[d, rows], x_s[d])
        gqb[rows] = acc_q.astype(BF)
        return 0

    lax.fori_loop(0, 3, weights, 0)
    nd.tail()
    for s, d in left:
        if s == parts - 2:
            out.wait(s, d)
    for s, d in left:
        out.sent(s, d)


class Sums:
    def __init__(self, docs, seq, parts, dp, refs):
        for name in ("pz", "acc", "gsem", "s1", "small_in", "gq", "ig", "taps_out", "gw", "small", "ipart", "ri", "ra1", "rb1", "rz", "fin", "rfin", "rq0", "rq1", "rq2", "gqb", "q", "rsm", "rtp", "ssem", "rsem", "isem"):
            setattr(self, name, refs[name])
        self.docs, self.parts = docs, parts
        self.z, self.d = lax.axis_index("mp"), lax.axis_index("dp")
        self.r = lax.rem(self.d, SLOTS)
        self.y, self.x, self.k = self.r // 4, lax.rem(self.r // 2, 2), lax.rem(self.r, 2)
        self.net = Net(self.ssem, self.rsem)
        self.extra = [b for b in (8, 16, 32, 64, 128) if b < dp]
        self.bits = [1, 2, 4] + self.extra

    def dev(self, bit):
        return {"dp": flip(self.d, bit)}

    def zdev(self, m):
        return {"mp": partner(self.z, m)}

    def begin(self):
        greet([self.zdev(m) for m in range(1, self.parts)] + [self.dev(b) for b in self.bits])
        self.i_setup()
        self.line = Line(self.parts)
        c = self.net.copy
        low, high = pl.ds(0, GCUT), pl.ds(GCUT, SLICE - GCUT)
        self.a1 = c(self.s1.at[:, 1 - self.y, :, low], self.ra1, self.dev(4))
        self.b1 = c(self.s1.at[:, :, 1 - self.x, high], self.rb1, self.dev(2))
        self.a1.start()
        self.b1.start()
        self.a2 = c(self.ra1.at[:, 1 - self.x], self.pz.at[:, low], self.dev(2))
        self.b2 = c(self.rb1.at[:, 1 - self.y], self.pz.at[:, high], self.dev(4))
        r, gw = self.r, self.gw
        r4, r2, r6 = flip(r, 4), flip(r, 2), partner(r, 6)
        self.gy = c(gw.at[r], gw.at[r], self.dev(4))
        self.gx = c(gw.at[r], gw.at[r], self.dev(2))
        self.gyx = c(gw.at[r4, low], gw.at[r4, low], self.dev(2))
        self.gxy = c(gw.at[r2, high], gw.at[r2, high], self.dev(4))
        self.gc = [c(gw.at[i], gw.at[i], self.dev(1)) for i in (r, r4, r2, r6)]
        h = self.gqb.shape[0] // 2
        self.half = h
        mine, other = (pl.ds(pl.multiple_of(k * h, 8), h) for k in (self.k, 1 - self.k))
        self.mine = mine
        self.q0 = c(self.gqb.at[other], self.rq0, self.dev(1))
        self.qa = self.q_pair(self.rq1, 4, 2)
        self.qb = self.q_pair(self.rq2.at[0], 2, 4)
        self.qc = c(self.gq.at[mine], self.gq.at[mine], self.dev(1))
        self.extras = [(c(self.fin, self.rfin.at[i], self.dev(b), late=False), c(self.q, self.rq2.at[1 + i], self.dev(b), late=False)) for i, b in enumerate(self.extra)]
        self.small[...] = self.small_in[...]
        zs = [self.zdev(1 << j) for j in range(self.parts.bit_length() - 1)]
        self.smalls = [c(self.small, self.rsm.at[i], dev, late=False) for i, dev in enumerate([self.dev(b) for b in self.bits] + zs)]
        self.tapsums = [c(self.taps_out, self.rtp.at[i], self.dev(b), late=False) for i, b in enumerate(self.bits)]
        self.small_step(0)

    def exchange(self, copies, buf, recv, i):
        if 0 < i <= len(copies):
            copies[i - 1].wait()
            buf[...] = buf[...] + recv[i - 1]
        if i < len(copies):
            copies[i].start()

    def small_step(self, i):
        self.exchange(self.smalls, self.small, self.rsm, i)

    def taps_step(self, i):
        self.exchange(self.tapsums, self.taps_out, self.rtp, i)

    def double(self, c, buf, recv):
        c.start()
        c.wait()
        buf[...] = (buf[...].astype(F32) + recv[...].astype(F32)).astype(buf.dtype)

    def g_step1(self):
        self.a1.wait_recv()
        self.b1.wait_recv()

        def add(i, _):
            g, j = i // 2, i % 2
            self.ra1[g, j] = (self.ra1[g, j].astype(F32) + self.s1[g, self.y, j, 0:GCUT].astype(F32)).astype(BF)
            self.rb1[g, j] = (self.rb1[g, j].astype(F32) + self.s1[g, j, self.x, GCUT:SLICE].astype(F32)).astype(BF)
            return 0

        lax.fori_loop(0, 2 * self.parts, add, 0)
        self.a2.start()
        self.b2.start()

    def g_step2(self):
        self.a2.wait_recv()
        self.b2.wait_recv()

        def add(g, _):
            self.pz[g, 0:GCUT] = (self.pz[g, 0:GCUT].astype(F32) + self.ra1[g, self.x].astype(F32)).astype(BF)
            self.pz[g, GCUT:SLICE] = (self.pz[g, GCUT:SLICE].astype(F32) + self.rb1[g, self.y].astype(F32)).astype(BF)
            return 0

        lax.fori_loop(0, self.parts, add, 0)
        self.z_hop(0)

    def z_piece(self, way, s):
        last = self.parts - 1
        g = last - s + self.z if way == 0 else s - last + self.z
        return g, (self.z <= s) & (self.z < last) if way == 0 else (last - self.z <= s) & (self.z > 0)

    def z_copy(self, way, s, g):
        return rcopy(self.pz.at[g], self.rz.at[way, s], self.gsem.at[0, way, s], self.gsem.at[1, way, s], self.line.ahead(way))

    def z_hop(self, s):
        last = self.parts - 1
        for way in range(2):
            g, ok = self.z_piece(way, s)
            inner = self.z > 0 if way == 0 else self.z < last

            if s > 0:

                @pl.when(ok & inner)
                def _():
                    self.z_copy(way, s - 1, 0).wait_recv()
                    self.pz[g] = (self.pz[g].astype(F32) + self.rz[way, s - 1].astype(F32)).astype(BF)

            @pl.when(ok)
            def _():
                self.z_copy(way, s, g).start()

    def z_done(self):
        last = self.parts - 1
        for way in range(2):
            for s in range(last):
                g, ok = self.z_piece(way, s)

                @pl.when(ok)
                def _():
                    self.z_copy(way, s, g).wait_send()

    def g_step3(self):
        last = self.parts - 1
        self.acc[...] = self.pz[self.z].astype(F32)
        for way in range(2):

            @pl.when(self.z > 0 if way == 0 else self.z < last)
            def _():
                self.z_copy(way, last - 1, 0).wait_recv()
                self.acc[...] += self.rz[way, last - 1].astype(F32)

        self.fin[...] = self.acc[...].astype(BF)
        for i, (c, _) in enumerate(self.extras):
            self.double(c, self.fin, self.rfin.at[i])
        self.gw[self.r] = self.fin[...]
        self.gy.start()
        self.gx.start()
        self.gc[0].start()

    def g_step4(self):
        self.gy.wait_recv()
        self.gyx.start()
        self.gc[1].start()
        self.gx.wait_recv()
        self.gxy.start()
        self.gc[2].start()

    def g_step5(self):
        self.gyx.wait_recv()
        self.gxy.wait_recv()
        self.gc[3].start()
        for s in self.gc:
            s.wait_recv()

    def q_pair(self, recv, a, b):
        h = self.half // 2
        return [
            self.net.copy(self.q.at[pl.ds(0, h)], recv.at[pl.ds(0, h)], self.dev(a), late=False),
            self.net.copy(self.q.at[pl.ds(h, h)], recv.at[pl.ds(h, h)], self.dev(b), late=False),
        ]

    def q_step0(self):
        self.q0.start()

    def q_step1(self):
        self.q0.wait_recv()
        self.q[...] = (self.gqb[self.mine].astype(F32) + self.rq0[...].astype(F32)).astype(BF)
        for s in self.qa:
            s.start()

    def q_step2(self):
        for s in self.qa:
            s.wait()
        self.q[...] = (self.q[...].astype(F32) + self.rq1[...].astype(F32)).astype(BF)
        for s in self.qb:
            s.start()

    def q_step3(self):
        for s in self.qb:
            s.wait()
        self.q[...] = (self.q[...].astype(F32) + self.rq2[0].astype(F32)).astype(BF)
        for i, (_, c) in enumerate(self.extras):
            self.double(c, self.q, self.rq2.at[1 + i])
        self.gq[self.mine] = self.q[...]
        self.qc.start()

    def i_setup(self):
        last = self.parts - 1
        self.chunks = self.ipart.shape[1]
        self.pos, self.lower, self.upper = [], [], []
        for d in range(self.docs):
            step = 1 if d % 2 == 0 else -1
            self.pos.append(self.z if d % 2 == 0 else last - self.z)
            self.lower.append({"mp": lax.rem(self.z - step + self.parts, self.parts)})
            self.upper.append({"mp": lax.rem(self.z + step + self.parts, self.parts)})

    def red(self, d, c):
        return rcopy(self.ipart.at[d, c], self.ri.at[d, c], self.isem.at[0, d, c], self.isem.at[1, d, c], self.lower[d])

    def bc(self, d, c):
        return rcopy(self.ig.at[d, c], self.ig.at[d, c], self.isem.at[2, d, c], self.isem.at[3, d, c], self.upper[d])

    def i_time(self, t):
        last = self.parts - 1
        for d in range(self.docs):
            p = self.pos[d]
            c = t - last + p
            ok = (c >= 0) & (c < self.chunks)

            @pl.when(ok & (p < last))
            def _():
                self.red(d, c).wait_recv()
                self.ipart[d, c] = (self.ipart[d, c].astype(F32) + self.ri[d, c].astype(F32)).astype(BF)

            @pl.when(ok & (p > 0))
            def _():
                self.red(d, c).start()

            @pl.when(ok & (p == 0))
            def _():
                self.ig[d, c] = self.ipart[d, c]
                self.bc(d, c).start()

        for d in range(self.docs):
            p = self.pos[d]
            c = t - last - p
            ok = (c >= 0) & (c < self.chunks) & (p > 0)

            @pl.when(ok)
            def _():
                self.bc(d, c).wait_recv()

            @pl.when(ok & (p < last))
            def _():
                self.bc(d, c).start()

    def i_end(self):
        last = self.parts - 1
        for d in range(self.docs):
            p = self.pos[d]

            def sent(c, _, d=d):
                self.red(d, c).wait_send()
                return 0

            def back(c, _, d=d):
                self.bc(d, c).wait_send()
                return 0

            @pl.when(p > 0)
            def _():
                lax.fori_loop(0, self.chunks, sent, 0)

            @pl.when(p < last)
            def _():
                lax.fori_loop(0, self.chunks, back, 0)

    def tail(self):
        done = 3 + self.docs
        rest = [functools.partial(self.small_step, i) for i in range(done + 1, len(self.smalls) + 1)]
        rest += [functools.partial(self.taps_step, i) for i in range(3, len(self.tapsums) + 1)]

        def run(*fs):
            def go():
                for f in fs:
                    f()

            return go

        todo = {
            1: run(self.g_step2),
            2: run(self.q_step1),
            3: run(lambda: self.z_hop(1)),
            4: run(self.q_step2),
            5: run(lambda: self.z_hop(2)),
            6: run(self.q_step3, *rest),
            8: run(self.g_step3),
            10: run(self.g_step4),
            12: run(self.g_step5),
        }
        self.q_step0()

        def step(t, _):
            self.i_time(t)
            at(t, todo)
            return 0

        lax.fori_loop(1, self.chunks + 2 * (self.parts - 1), step, 0)
        self.qc.wait_recv()
        self.i_end()
        self.z_done()
        self.net.drain()


def attn_bwd(dp, lengths, x, wt, taps, qkv, gctx, lq, lk, sm, mix, k2, z, p, l1, l3, s1, small, gmix, out_rows):
    docs, seq, dim = x.shape
    width = wt.shape[0] // 3
    heads = width // HD
    parts = gctx.shape[0]
    nchunk = seq // CHUNK
    more = max(1, dp.bit_length() - 4)
    steps = dp.bit_length() + parts.bit_length()
    sds = jax.ShapeDtypeStruct
    vmem = pltpu.VMEM
    out = [
        sds((3 * width, dim), BF),
        sds((docs, nchunk, CHUNK, dim), BF),
        sds((heads, WIN), F32),
        sds((SLOTS, SLICE, dim), BF),
        sds((8, dim), F32),
        sds(out_rows.shape, BF),
    ]
    h = 3 * width // 2
    sq = (docs, width, width)
    return pl.pallas_call(
        functools.partial(attn_bwd_kernel, docs, heads, seq, parts, dp),
        out_shape=out,
        in_specs=[SM, ANY, VM, VM, VM, VM, VM, VM, VM, VM, VM, ANY, ANY, VM, VM, VM, VM, ANY, ANY],
        out_specs=[VM] * 5 + [ANY],
        input_output_aliases={18: 5},
        scratch_shapes=[
            vmem(x.shape, BF),
            vmem(z.shape, F32),
            vmem(p.shape, F32),
            vmem(gmix.shape, F32),
            vmem((docs, 3 * width, seq), BF),
            vmem((docs, width, seq), BF),
            vmem((docs, width, seq), BF),
            vmem(sq, F32),
            vmem(sq, F32),
            vmem(sq, F32),
            vmem(sq, F32),
            vmem(sq, F32),
            vmem((heads, WIN), F32),
            vmem((heads, BLK, WIN), F32),
            vmem((docs, nchunk, CHUNK, dim), BF),
            vmem((docs, nchunk, CHUNK, dim), BF),
            vmem((parts, 2, GCUT, dim), BF),
            vmem((parts, 2, SLICE - GCUT, dim), BF),
            vmem((2, parts - 1, SLICE, dim), BF),
            vmem((SLICE, dim), BF),
            vmem((more, SLICE, dim), BF),
            vmem((h, dim), BF),
            vmem((h, dim), BF),
            vmem((1 + more, h, dim), BF),
            vmem((3 * width, dim), BF),
            vmem((h, dim), BF),
            vmem((steps, 8, dim), F32),
            vmem((steps, heads, WIN), F32),
            DMA((4,)),
            DMA((64,)),
            DMA((64,)),
            DMA((4, docs, nchunk)),
            DMA((2, 2, parts - 1, docs)),
            vmem((parts, SLICE, dim), BF),
            vmem((SLICE, dim), F32),
            DMA((2, 2, parts - 1)),
        ],
        compiler_params=pltpu.CompilerParams(vmem_limit_bytes=62 * 2**20, collective_id=2, has_side_effects=True),
        cost_estimate=pl.CostEstimate(flops=int(1.2e10), bytes_accessed=int(3e7), transcendentals=0),
        name="attn_bwd",
    )(lengths, x, wt, taps, qkv, gctx, lq, lk, sm, mix, k2, z, p, l1, l3, s1, small, gmix, out_rows)


def finish_kernel(gw_ref, gq_ref, ig_ref, out_ref, small_ref, taps_ref, ow_o, up_o, dn_o, q_o, ig_o, out_o, g1_o, b1_o, g2_o, b2_o, taps_o):
    each = gw_ref.shape[0]
    for i, o in enumerate((ow_o, up_o, dn_o)):
        lo, size = PARTS[i]
        for j in range(each):
            o[j * size : (j + 1) * size] = gw_ref[j, lo : lo + size].astype(F32)
    q_o[...] = gq_ref[...].astype(F32)
    ig_o[...] = ig_ref[...].reshape(ig_o.shape)
    out_o[...] = out_ref[...]

    @pl.when(pl.program_id(0) == 0)
    def _():
        for i, o in enumerate((g1_o, b1_o, g2_o, b2_o)):
            o[...] = small_ref[i]
        taps_o[...] = taps_ref[:, TAP_END : TAP_END + KSIZE]


def finish_up(gw, gq, ig, out_rows, small, taps):
    docs, nchunk, chunk, dim = ig.shape
    groups, rows = out_rows.shape[1:3]
    seq = nchunk * chunk
    heads = taps.shape[0]
    steps = 4
    each = SLOTS // steps
    qrows = gq.shape[0] // steps
    per = seq // steps
    ratio = rows // per
    sds = jax.ShapeDtypeStruct
    whole = lambda shape: pl.BlockSpec(shape, lambda i: (0,) * len(shape))
    return pl.pallas_call(
        finish_kernel,
        grid=(steps,),
        out_shape=[sds((SLOTS * t, dim), F32) for t in (OW_ROWS, UP_ROWS, DN_ROWS)]
        + [sds(gq.shape, F32), sds((docs, seq, dim), BF), sds((docs, seq, dim), BF)]
        + [sds((dim,), F32)] * 4
        + [sds((heads, KSIZE), F32)],
        in_specs=[
            pl.BlockSpec((each, SLICE, dim), lambda i: (i, 0, 0)),
            pl.BlockSpec((qrows, dim), lambda i: (i, 0)),
            pl.BlockSpec((docs, nchunk // steps, chunk, dim), lambda i: (0, i, 0, 0)),
            pl.BlockSpec((docs, pl.Squeezed(), per, dim), lambda i: (0, i // ratio, i % ratio, 0)),
            whole(small.shape),
            whole(taps.shape),
        ],
        out_specs=[pl.BlockSpec((t, dim), lambda i: (i, 0)) for t in (each * OW_ROWS, each * UP_ROWS, each * DN_ROWS, qrows)]
        + [pl.BlockSpec((docs, per, dim), lambda i: (0, i, 0))] * 2
        + [whole((dim,))] * 4
        + [whole((heads, KSIZE))],
        compiler_params=pltpu.CompilerParams(vmem_limit_bytes=62 * 2**20),
        name="finish",
    )(gw, gq, ig, out_rows, small, taps)


def body_of(dp, mp):
    def body(tokens, lengths, qkv_weight, out_weight, conv_taps, norm1_gain, norm1_bias, norm2_gain, norm2_bias, up_weight, down_weight, cotangent):
        dim = tokens.shape[2]
        width = qkv_weight.shape[2]
        wt = jnp.transpose(qkv_weight, (0, 2, 1)).reshape(3 * width, dim)
        ow, up, dn = (t.reshape(SLOTS, -1, dim) for t in (out_weight, up_weight, down_weight))
        qkv, ctx, lq, lk, sm, mix, k2, z, p, l1, l3, wall = attn_fwd(lengths, tokens, wt, conv_taps, ow, up, dn, mp)
        out_rows, gmix, gctx, s1, small = ffn(lengths, tokens, cotangent, ctx, ow, up, dn, wall, norm1_gain, norm1_bias, norm2_gain, norm2_bias)
        gq, ig, gtaps, gw, small, out_rows = attn_bwd(
            dp, lengths, tokens, wt, conv_taps, qkv, gctx, lq, lk, sm, mix, k2, z, p, l1, l3, s1, small, gmix, out_rows
        )
        g_ow, g_up, g_dn, gq, input_grad, output, g1, b1, g2, b2, g_taps = finish_up(gw, gq, ig, out_rows, small, gtaps)
        gqkv = jnp.transpose(gq.reshape(3, width, dim), (0, 2, 1))
        return output, input_grad, gqkv, g_ow, g_taps, g1, b1, g2, b2, g_up, g_dn

    return body


def solution(mesh):
    rep, rows = P(), P("mp", None)
    docs, cols, qkv = P("dp", None, None), P(None, "mp"), P(None, None, "mp")
    return jax.shard_map(
        body_of(mesh.shape["dp"], mesh.shape["mp"]),
        mesh=mesh,
        in_specs=(docs, P("dp"), qkv, rows, rows, rep, rep, rep, rep, cols, rows, docs),
        out_specs=(docs, docs, qkv, rows, rows, rep, rep, rep, rep, cols, rows),
        check_vma=False,
    )
```
